32 devices in a mesh: wide: 16 (over z, y, x), narrow: 2 (over core).
Axes of the slice: x: 2, y: 2, z: 4, core: 2. Of those that a mesh axis runs over, the one named last changes fastest.
Arguments:
- tokens: bfloat16 [64, 1024, 576], P('wide', 'narrow'), may hold values from -6 to 6
- cotangent: bfloat16 [64, 1024, 576], P('wide', 'narrow'), may hold values from -6 to 6
- documents: int32 [64, 1024], P('wide'), may hold values from 0 to 2, as said below
- attention_master: float32 [1536, 576], P(('wide', 'narrow'))
- attention_first: float32 [1536, 576], P(('wide', 'narrow')), may hold values from -0.00036621094 to 0.00036621094
- attention_second: float32 [1536, 576], P(('wide', 'narrow')), may hold values from 2.2605614e-11 to 3.673412e-10
- feedforward_master: float32 [3, 1536, 576], P(None, ('narrow', 'wide'))
- feedforward_first: float32 [3, 1536, 576], P(None, ('narrow', 'wide')), may hold values from -0.0008544922 to 0.0008544922
- feedforward_second: float32 [3, 1536, 576], P(None, ('narrow', 'wide')), may hold values from 1.4128508e-10 to 2.2605613e-09
- gain_master: float32 [2, 576], replicated, may hold values from 0.5 to 1.5
- gain_first: float32 [2, 576], replicated, may hold values from -0.0034179688 to 0.0034179688
- gain_second: float32 [2, 576], replicated, may hold values from 2.2605613e-09 to 3.616898e-08
Outputs:
- outputs: bfloat16 [64, 1024, 576], P('wide', 'narrow')
- grad_tokens: float32 [64, 1024, 576], P('wide', 'narrow')
- grad_norm: float32 [], replicated
- attention_new: float32 [1536, 576], P(('wide', 'narrow'))
- attention_first_new: float32 [1536, 576], P(('wide', 'narrow'))
- attention_second_new: float32 [1536, 576], P(('wide', 'narrow'))
- feedforward_new: float32 [3, 1536, 576], P(None, ('narrow', 'wide'))
- feedforward_first_new: float32 [3, 1536, 576], P(None, ('narrow', 'wide'))
- feedforward_second_new: float32 [3, 1536, 576], P(None, ('narrow', 'wide'))
- gain_new: float32 [2, 576], replicated
- gain_first_new: float32 [2, 576], replicated
- gain_second_new: float32 [2, 576], replicated
The draws below stay inside these ranges and needn't reach their ends.
Inputs may be any that keep to these rules, and one draw needn't show every extreme that they name: Each row holds three documents in order (numbers 0, 1, 2, never falling); document 1 starts at position 256 or earlier and runs through position 767 at least.
All inputs are finite; a program needn't handle non-finite values.
Results may differ from the reference program's by a relative error of at most 0.015.
Values may be sent and summed in bfloat16 or wider, within the bound.
No kernel may reach another device: no remote copies, remote signals or barrier semaphores. Data moves between devices by JAX's collectives and lax.ppermute only.
A program may use at most 192 MiB of HBM per device.

```python
import math
import jax
import jax.numpy as jnp
from jax import lax

D = 576
HEADS = 9
KV_HEADS = 3
HEAD_DIM = 64
FF = 1536
LEN = 1024
STEP = 10
KV_WIDTH = 192
ATT_ROWS = 1536
SEQS = 64
N_NARROW = 2


def draw_documents(key, part):
    first_key = jax.random.fold_in(key, 11)
    second_key = jax.random.fold_in(key, 23)
    first_cut = jax.random.randint(first_key, (SEQS, 1), 1, LEN // 4 + 1)
    second_cut = jax.random.randint(second_key, (SEQS, 1), 3 * LEN // 4, LEN)
    positions = jnp.arange(LEN, dtype=jnp.int32)[None, :]
    return (positions >= first_cut).astype(jnp.int32) + (positions >= second_cut).astype(jnp.int32)


def draw_attention_master(key, part):
    rows = jnp.arange(ATT_ROWS, dtype=jnp.int32)[:, None]
    scales = jnp.where(rows < D + 2 * KV_WIDTH, 1.0, 4.0) * float(D) ** (-0.5)
    entries = jax.random.normal(key, (ATT_ROWS, D), jnp.float32)
    return entries * scales


def draw_feedforward_master(key, part):
    growth = 3.0
    units = jnp.arange(FF, dtype=jnp.int32)
    share = FF // N_NARROW
    level = (units // share).astype(jnp.float32) + (units % share).astype(jnp.float32) / share
    down_scale = growth ** (0.5 * level) * float(FF) ** (-0.5)
    drawn_scale = jnp.full((FF,), float(D) ** (-0.5), jnp.float32)
    scales = jnp.stack([drawn_scale, drawn_scale, down_scale])[:, :, None]
    entries = jax.random.normal(key, (3, FF, D), jnp.float32)
    return entries * scales


def levels(own_key, extent, shards, smallest, top_value):
    loudness = 1.0
    for dim, parts in shards:
        draws = jax.random.uniform(jax.random.fold_in(jax.random.fold_in(own_key, 6), dim), (parts,), jnp.float32, smallest / len(shards), top_value / len(shards))
        loudness = loudness * jnp.repeat(jnp.exp(draws), extent[dim] // parts).reshape((-1,) + (1,) * (len(extent) - 1 - dim))
    return loudness


def centred(stream_key, dims, scale, reach, shards=(), kind=jnp.bfloat16):
    values = jax.random.normal(stream_key, dims, jnp.float32) * scale
    if len(shards) > 0:
        values = levels(stream_key, dims, shards, -0.22, 0.18) * values
    return jnp.clip(values, min=-reach, max=reach).astype(kind)


def setup_inputs(seed: int = 0) -> dict:
    splits = jax.random.split(jax.random.key(seed), 13)
    tokens = centred(splits[0], (SEQS, LEN, D), 1.0, 6.0, ((0, 16), (1, 2)))
    cotangent = centred(splits[1], (SEQS, LEN, D), 1.0, 6.0, ((0, 16), (1, 2)))
    documents = draw_documents(jax.random.fold_in(splits[12], 71), 0)
    attention_master = draw_attention_master(jax.random.fold_in(splits[12], 71), 0)
    attention_first = centred(splits[4], (ATT_ROWS, D), (0.045 * (ATT_ROWS * D + 3 * FF * D) ** -0.5), 0.00036621094, ((0, 32),), jnp.float32)
    attention_second = jnp.clip(jnp.exp(math.log(3.673412130034137e-10) - 2.7880929 * jax.random.uniform(splits[5], (ATT_ROWS, D), jnp.float32) ** levels(splits[5], (ATT_ROWS, D), ((0, 32),), -0.2, 0.2)), 2.260561356159929e-11, 3.673412130034137e-10)
    feedforward_master = draw_feedforward_master(jax.random.fold_in(splits[12], 71), 0)
    feedforward_first = centred(splits[7], (3, FF, D), (0.11 * (ATT_ROWS * D + 3 * FF * D) ** -0.5), 0.0008544922, ((1, 32),), jnp.float32)
    feedforward_second = jnp.clip(jnp.exp(math.log(2.260561293709884e-09) - 2.7725887 * jax.random.uniform(splits[8], (3, FF, D), jnp.float32) ** levels(splits[8], (3, FF, D), ((1, 32),), -0.2, 0.2)), 1.4128508085686775e-10, 2.260561293709884e-09)
    gain_master = jnp.clip(1.0 + 0.1 * jax.random.normal(splits[9], (2, D), jnp.float32), 0.5, 1.5)
    gain_first = centred(splits[10], (2, D), (0.44 * (ATT_ROWS * D + 3 * FF * D) ** -0.5), 0.0034179688, (), jnp.float32)
    gain_second = jnp.clip(jnp.exp(jax.random.uniform(splits[11], (2, D), jnp.float32, math.log(2.260561293709884e-09), math.log(3.6168980699358144e-08))), 2.260561293709884e-09, 3.6168980699358144e-08)
    return {"tokens": tokens, "cotangent": cotangent, "documents": documents, "attention_master": attention_master, "attention_first": attention_first, "attention_second": attention_second, "feedforward_master": feedforward_master, "feedforward_first": feedforward_first, "feedforward_second": feedforward_second, "gain_master": gain_master, "gain_first": gain_first, "gain_second": gain_second}


norm_epsilon = 1e-05
adam_epsilon = 1e-08
beta_first = 0.9
beta_second = 0.999
weight_decay = 0.1
rate_matrix = 0.05
rate_gain = 0.5
clip_limit = 1.0
rotary_base = 10000.0
masked_value = -1e+30

@jax.custom_vjp
def low(v):
    return lax.optimization_barrier(v.astype(jnp.bfloat16)).astype(jnp.float32)

@jax.custom_vjp
def low_back(v):
    return v

def low_keep(v):
    return (low(v), None)

def low_pass(kept, grad):
    return (grad,)

def back_keep(v):
    return (v, None)

def back_low(kept, grad):
    return (low(grad),)
low.defvjp(low_keep, low_pass)
low_back.defvjp(back_keep, back_low)

def product(pattern, left_side, right_side):
    return jnp.einsum(pattern, left_side, right_side, precision=lax.Precision.HIGHEST)

def rotary_tables(positions, head_width):
    halves = head_width // 2
    frequency = rotary_base ** (-2.0 * jnp.arange(halves, dtype=jnp.float32) / head_width)
    angles = positions.astype(jnp.float32)[:, None] * frequency[None, :]
    return (jnp.cos(angles)[:, None, :], jnp.sin(angles)[:, None, :])

def rotate(values, cosine_table, sine_table):
    halves = values.shape[-1] // 2
    front_part = values[..., :halves]
    behind = values[..., halves:]
    return jnp.concatenate([front_part * cosine_table - behind * sine_table, behind * cosine_table + front_part * sine_table], axis=-1)

def adamw_update(master, first_state, second_state, gradient, factor, step_rate, decay_rate):
    clipped = gradient * factor
    first_new = beta_first * first_state + (1.0 - beta_first) * clipped
    second_new = beta_second * second_state + (1.0 - beta_second) * clipped * clipped
    first_hat = first_new / (1.0 - beta_first ** STEP)
    second_hat = second_new / (1.0 - beta_second ** STEP)
    master_new = master * (1.0 - step_rate * decay_rate) - step_rate * first_hat / (jnp.sqrt(second_hat) + adam_epsilon)
    return (master_new, first_new, second_new)

def forward_block(token_in, doc_part, attention_in, feedforward_in, gain_in):
    attention_low = low(attention_in)
    feedforward_low = low(feedforward_in)
    qkv_width = D + 2 * KV_WIDTH
    qkv_rows = attention_low[:qkv_width]
    out_rows = attention_low[qkv_width:]
    seq_count = token_in.shape[0]
    inv_first = lax.rsqrt(lax.optimization_barrier(jnp.mean(token_in * token_in, axis=-1, keepdims=True)) + norm_epsilon)
    normed_first = low(token_in * inv_first * gain_in[0])
    projected = product('spd,jd->spj', normed_first, qkv_rows)
    positions = jnp.arange(LEN, dtype=jnp.int32)
    cosine_table, sine_table = rotary_tables(positions, HEAD_DIM)
    raw_queries = low_back(projected[..., :D]).reshape(seq_count, LEN, HEADS, HEAD_DIM)
    queries = low(rotate(raw_queries, cosine_table, sine_table) * HEAD_DIM ** (-0.5))
    raw_keys = low_back(projected[..., D:D + KV_WIDTH]).reshape(seq_count, LEN, KV_HEADS, HEAD_DIM)
    key_all = low(rotate(raw_keys, cosine_table, sine_table))
    value_all = low(low_back(projected[..., D + KV_WIDTH:])).reshape(seq_count, LEN, KV_HEADS, HEAD_DIM)
    grouped = queries.reshape(seq_count, LEN, KV_HEADS, HEADS // KV_HEADS, HEAD_DIM)
    scores = low_back(product('spkrd,slkd->skrpl', grouped, key_all))
    allowed = (positions[None, :] <= positions[:, None])[None] & (doc_part[:, :, None] == doc_part[:, None, :])
    masked = jnp.where(allowed[:, None, None], scores, masked_value)
    row_top = lax.optimization_barrier(jnp.max(masked, axis=-1, keepdims=True))
    exponent = jnp.exp(masked - row_top)
    weights = low(exponent / lax.optimization_barrier(jnp.sum(exponent, axis=-1, keepdims=True)))
    mixed_heads = product('skrpl,slkd->spkrd', weights, value_all).reshape(seq_count, LEN, D)
    mixed_heads = low(low_back(mixed_heads))
    branch = low_back(product('spj,jd->spd', mixed_heads, out_rows))
    residual_second = token_in + branch
    inv_second = lax.rsqrt(lax.optimization_barrier(jnp.mean(residual_second * residual_second, axis=-1, keepdims=True)) + norm_epsilon)
    normed_second = low(residual_second * inv_second * gain_in[1])
    gate_values = low_back(product('spd,ud->spu', normed_second, feedforward_low[0]))
    upward = low_back(product('spd,ud->spu', normed_second, feedforward_low[1]))
    hidden = low(jax.nn.silu(gate_values) * upward)
    return residual_second + product('spu,ud->spd', hidden, feedforward_low[2])

def reference(tokens, cotangent, documents, attention_master, attention_first, attention_second, feedforward_master, feedforward_first, feedforward_second, gain_master, gain_first, gain_second):
    group_size = math.gcd(SEQS, 4)
    block_count = SEQS // group_size
    token_blocks = tokens.astype(jnp.float32).reshape(block_count, group_size, LEN, D)
    cotangent_blocks = cotangent.astype(jnp.float32).reshape(block_count, group_size, LEN, D)
    document_blocks = documents.reshape(block_count, group_size, LEN)

    def one_block(running, members):
        token_part, cotangent_part, doc_part = members

        def forward(token_in, attention_in, feedforward_in, gain_in):
            return forward_block(token_in, doc_part, attention_in, feedforward_in, gain_in)
        result, pullback = jax.vjp(forward, token_part, attention_master, feedforward_master, gain_master)
        grad_token, grad_attention, grad_feedforward, grad_gain = pullback(cotangent_part)
        running_new = (running[0] + grad_attention, running[1] + grad_feedforward, running[2] + grad_gain)
        return (running_new, (result.astype(jnp.bfloat16), grad_token))
    initial = (jnp.zeros_like(attention_master), jnp.zeros_like(feedforward_master), jnp.zeros_like(gain_master))
    totals, (out_blocks, grad_blocks) = lax.scan(one_block, initial, (token_blocks, cotangent_blocks, document_blocks))
    outputs = out_blocks.reshape(SEQS, LEN, D)
    grad_tokens = grad_blocks.reshape(SEQS, LEN, D)
    attention_grad, feedforward_grad, gain_grad = totals
    squares = jnp.sum(attention_grad * attention_grad) + jnp.sum(feedforward_grad * feedforward_grad) + jnp.sum(gain_grad * gain_grad)
    grad_norm = jnp.sqrt(squares)
    factor = jnp.minimum(1.0, clip_limit / (grad_norm + 1e-06))
    attention_new, attention_first_new, attention_second_new = adamw_update(attention_master, attention_first, attention_second, attention_grad, factor, rate_matrix, weight_decay)
    feedforward_new, feedforward_first_new, feedforward_second_new = adamw_update(feedforward_master, feedforward_first, feedforward_second, feedforward_grad, factor, rate_matrix, weight_decay)
    gain_new, gain_first_new, gain_second_new = adamw_update(gain_master, gain_first, gain_second, gain_grad, factor, rate_gain, 0.0)
    return (outputs, grad_tokens, grad_norm, attention_new, attention_first_new, attention_second_new, feedforward_new, feedforward_first_new, feedforward_second_new, gain_new, gain_first_new, gain_second_new)
```

```python
import functools

import jax
import jax.numpy as jnp
import numpy as np
from jax import lax
from jax.experimental import pallas as pl
from jax.experimental.pallas import tpu as pltpu
from jax.sharding import PartitionSpec as P

D = 576
HEADS = 9
KV_HEADS = 3
RATIO = 3
HEAD_DIM = 64
HALF = 32
STEP = 10
KV_WIDTH = 192
QKV = 960
BLOCK = 256

norm_epsilon = 1e-05
adam_epsilon = 1e-08
beta_first = 0.9
beta_second = 0.999
weight_decay = 0.1
rate_matrix = 0.05
rate_gain = 0.5
clip_limit = 1.0
rotary_base = 10000.0
masked_value = -1e30

F32 = jnp.float32
BF16 = jnp.bfloat16
VMEM_LIMIT = 60 * 2**20


def rotary_tables(length):
    frequency = np.float32(rotary_base) ** (
        np.float32(-2.0) * np.arange(HALF, dtype=np.float32) / np.float32(HEAD_DIM)
    )
    angles = np.arange(length, dtype=np.float32)[None, :] * frequency.astype(np.float32)[:, None]
    return jnp.asarray(np.cos(angles), F32), jnp.asarray(np.sin(angles), F32)


def dot(left, right, left_dim=1, right_dim=0):
    return lax.dot_general(
        left, right, (((left_dim,), (right_dim,)), ((), ())), preferred_element_type=F32
    )


def inverse_root(values):
    return lax.rsqrt(jnp.mean(values * values, axis=-1, keepdims=True) + norm_epsilon)


def visible_scores(scores, start_row, place_row, query_block):
    parts = []
    for key_block in range(query_block + 1):
        part = scores[key_block * BLOCK : (key_block + 1) * BLOCK]
        place = lax.broadcasted_iota(jnp.int32, part.shape, 0) + key_block * BLOCK
        seen = place >= start_row
        if key_block == query_block:
            seen = seen & (place <= place_row)
        parts.append(jnp.where(seen, part, masked_value))
    return jnp.concatenate(parts, axis=0) if len(parts) > 1 else parts[0]


def triple(row):
    return jnp.concatenate([row] * RATIO, axis=1)


def attention_forward_body(
    x_ref,
    start_ref,
    weight_ref,
    gain_ref,
    cosine_ref,
    sine_ref,
    residual_ref,
    query_ref,
    key_ref,
    value_ref,
    mixed_ref,
    total_ref,
    key_rows,
):
    length = x_ref.shape[1]
    x = x_ref[0].astype(F32)
    normed = (x * inverse_root(x) * gain_ref[0:1]).astype(BF16)
    cosine = cosine_ref[...]
    sine = sine_ref[...]
    projected = dot(weight_ref[0:QKV], normed, 1, 1)
    for head in range(HEADS):
        front = projected[head * 64 : head * 64 + 32]
        behind = projected[head * 64 + 32 : head * 64 + 64]
        query_ref[0, head * 64 : head * 64 + 32] = (
            (front * cosine - behind * sine) * HEAD_DIM ** (-0.5)
        ).astype(BF16)
        query_ref[0, head * 64 + 32 : head * 64 + 64] = (
            (behind * cosine + front * sine) * HEAD_DIM ** (-0.5)
        ).astype(BF16)
    for head in range(KV_HEADS):
        base = D + head * 64
        front = projected[base : base + 32]
        behind = projected[base + 32 : base + 64]
        rotated = jnp.concatenate(
            [front * cosine - behind * sine, behind * cosine + front * sine], axis=0
        )
        key_ref[0, head * 64 : head * 64 + 64] = rotated.astype(BF16)
        key_rows[head] = rotated.T.astype(BF16)
    value_ref[0] = projected[D + KV_WIDTH :].astype(BF16)

    def group(member, carry):
        for block in range(length // BLOCK):
            low, high = block * BLOCK, (block + 1) * BLOCK
            queries = jnp.concatenate(
                [
                    query_ref[0, pl.ds(member * 192 + r * 64, 64), low:high]
                    for r in range(RATIO)
                ],
                axis=1,
            )
            scores = dot(key_rows[member, 0:high], queries)
            start_row = triple(start_ref[0, 0:1, low:high])
            place_row = triple(lax.broadcasted_iota(jnp.int32, (1, BLOCK), 1) + low)
            scores = visible_scores(scores, start_row, place_row, block)
            top = jnp.max(scores, axis=0, keepdims=True)
            exponent = jnp.exp(scores - top)
            total = jnp.sum(exponent, axis=0, keepdims=True)
            values = value_ref[0, pl.ds(member * 64, 64), 0:high]
            mixed = dot(values, exponent.astype(BF16)) * (1.0 / total)
            log_total = top + jnp.log(total)
            for r in range(RATIO):
                lanes = slice(r * BLOCK, (r + 1) * BLOCK)
                mixed_ref[0, pl.ds(member * 192 + r * 64, 64), low:high] = mixed[:, lanes].astype(
                    BF16
                )
                total_ref[0, member, r : r + 1, low:high] = log_total[:, lanes]
        return carry

    lax.fori_loop(0, KV_HEADS, group, 0)
    branch = dot(mixed_ref[0].T, weight_ref[QKV:])
    residual_ref[0] = x_ref[0].astype(F32) + branch


def whole(shape):
    return pl.BlockSpec(shape, lambda *_: (0,) * len(shape))


def row_block(shape):
    return pl.BlockSpec((1,) + shape, lambda s: (s,) + (0,) * len(shape))


def params():
    return pltpu.CompilerParams(
        dimension_semantics=("arbitrary",), vmem_limit_bytes=VMEM_LIMIT
    )


def attention_forward(x, start, weights, gain, tables):
    count, length, _ = x.shape
    outs = [
        ((length, D), F32),
        ((D, length), BF16),
        ((KV_WIDTH, length), BF16),
        ((KV_WIDTH, length), BF16),
        ((D, length), BF16),
        ((KV_HEADS, 8, length), F32),
    ]
    return pl.pallas_call(
        attention_forward_body,
        grid=(count,),
        in_specs=[
            row_block((length, D)),
            row_block((1, length)),
            whole(weights.shape),
            whole(gain.shape),
            whole((HALF, length)),
            whole((HALF, length)),
        ],
        out_specs=[row_block(shape) for shape, _ in outs],
        out_shape=[jax.ShapeDtypeStruct((count,) + shape, kind) for shape, kind in outs],
        scratch_shapes=[pltpu.VMEM((KV_HEADS, length, HEAD_DIM), BF16)],
        compiler_params=params(),
        cost_estimate=pl.CostEstimate(
            flops=8_000_000_000, transcendentals=12_000_000, bytes_accessed=20_000_000
        ),
        name="attention_forward",
    )(x, start, weights, gain, *tables)


def feed_body(
    residual_ref,
    cotangent_ref,
    own_ref,
    other_ref,
    gain_ref,
    out_ref,
    back_ref,
    own_grad_ref,
    other_grad_ref,
    gain_grad_ref,
    sums,
):
    step = pl.program_id(0)
    units = own_ref.shape[1]
    residual = residual_ref[...]
    cotangent = cotangent_ref[...]
    gain = gain_ref[1:2]
    inverse = inverse_root(residual)
    normal = residual * inverse
    normed = (normal * gain).astype(BF16)
    normed_across = normed.T
    cotangent_across = cotangent.T

    @pl.when(step == 0)
    def _():
        sums[...] = jnp.zeros_like(sums)
        gain_grad_ref[...] = jnp.zeros_like(gain_grad_ref)

    out = residual
    grad_normed = jnp.zeros_like(residual)
    for part, weight_ref in enumerate((own_ref, other_ref)):
        lanes = slice(part * units, (part + 1) * units)
        gate = dot(normed, weight_ref[0], 1, 1)
        upward = dot(normed, weight_ref[1], 1, 1)
        sigmoid_gate = jax.nn.sigmoid(gate)
        swish = gate * sigmoid_gate
        hidden = (swish * upward).astype(BF16)
        out = out + dot(hidden, weight_ref[2])
        grad_hidden = dot(cotangent, weight_ref[2], 1, 1)
        grad_gate = (
            grad_hidden * upward * sigmoid_gate * (1.0 + gate * (1.0 - sigmoid_gate))
        ).astype(BF16)
        grad_upward = (grad_hidden * swish).astype(BF16)
        grad_normed = (
            grad_normed + dot(grad_gate, weight_ref[0]) + dot(grad_upward, weight_ref[1])
        )
        sums[0, :, lanes] += dot(normed_across, grad_gate)
        sums[1, :, lanes] += dot(normed_across, grad_upward)
        sums[2, :, lanes] += dot(cotangent_across, hidden)
    out_ref[...] = out.astype(BF16)
    scaled = grad_normed * gain
    gain_grad_ref[...] += jnp.sum(grad_normed * normal, axis=0, keepdims=True)
    back_ref[...] = cotangent.astype(F32) + inverse * (
        scaled - normal * jnp.mean(scaled * normal, axis=-1, keepdims=True)
    )

    @pl.when(step == pl.num_programs(0) - 1)
    def _():
        pieces, kinds, rows, _ = own_grad_ref.shape
        for part, grad_ref in enumerate((own_grad_ref, other_grad_ref)):
            for kind in range(kinds):
                flipped = sums[kind, :, part * units : (part + 1) * units].astype(BF16).T
                for piece in range(pieces):
                    grad_ref[piece, kind] = flipped[piece * rows : (piece + 1) * rows]


def feed_forward(residual, cotangent, own, other, gain, pieces):
    tokens = residual.shape[0]
    tile = 256
    units = own.shape[1]
    spec = pl.BlockSpec((tile, D), lambda s: (s, 0))
    grad_shape = (pieces, 3, units // pieces, D)
    return pl.pallas_call(
        feed_body,
        grid=(tokens // tile,),
        in_specs=[
            spec,
            spec,
            whole(own.shape),
            whole(other.shape),
            whole(gain.shape),
        ],
        out_specs=[spec, spec, whole(grad_shape), whole(grad_shape), whole((1, D))],
        out_shape=[
            jax.ShapeDtypeStruct((tokens, D), BF16),
            jax.ShapeDtypeStruct((tokens, D), F32),
            jax.ShapeDtypeStruct(grad_shape, BF16),
            jax.ShapeDtypeStruct(grad_shape, BF16),
            jax.ShapeDtypeStruct((1, D), F32),
        ],
        scratch_shapes=[pltpu.VMEM((3, D, 2 * units), F32)],
        compiler_params=params(),
        cost_estimate=pl.CostEstimate(
            flops=32_000_000_000, transcendentals=6_000_000, bytes_accessed=30_000_000
        ),
        name="feed_forward",
    )(residual, cotangent, own, other, gain)


def attention_backward_body(
    x_ref,
    start_ref,
    weight_ref,
    gain_ref,
    cosine_ref,
    sine_ref,
    grad_ref,
    query_ref,
    key_ref,
    value_ref,
    mixed_ref,
    total_ref,
    tokens_ref,
    weight_grad_ref,
    gain_grad_ref,
    key_rows,
    value_rows,
    query_rows,
    grad_rows,
    grad_across,
    inner,
    grad_key,
    grad_value,
    grad_projected,
    sums,
):
    step = pl.program_id(0)
    length = x_ref.shape[1]
    cosine = cosine_ref[...]
    sine = sine_ref[...]

    @pl.when(step == 0)
    def _():
        sums[...] = jnp.zeros_like(sums)
        gain_grad_ref[...] = jnp.zeros_like(gain_grad_ref)

    branch = grad_ref[0].astype(BF16)
    sums[QKV:] += dot(mixed_ref[0], branch)
    grad_mixed = dot(weight_ref[QKV:], branch, 1, 1)
    for head in range(HEADS):
        rows = slice(head * 64, head * 64 + 64)
        part = grad_mixed[rows]
        grad_across[rows] = part.astype(BF16)
        grad_rows[head] = part.T.astype(BF16)
        query_rows[head] = query_ref[0, rows].T
        inner[head // RATIO, head % RATIO : head % RATIO + 1] = jnp.sum(
            part.astype(BF16).astype(F32) * mixed_ref[0, rows].astype(F32), axis=0, keepdims=True
        )
    for head in range(KV_HEADS):
        rows = slice(head * 64, head * 64 + 64)
        key_rows[head] = key_ref[0, rows].T
        value_rows[head] = value_ref[0, rows].T

    def group(member, carry):
        grad_key[...] = jnp.zeros_like(grad_key)
        grad_value[...] = jnp.zeros_like(grad_value)
        for block in range(length // BLOCK):
            low, high = block * BLOCK, (block + 1) * BLOCK
            heads = [member * 192 + r * 64 for r in range(RATIO)]
            queries = jnp.concatenate(
                [query_ref[0, pl.ds(h, 64), low:high] for h in heads], axis=1
            )
            grads = jnp.concatenate([grad_across[pl.ds(h, 64), low:high] for h in heads], axis=1)
            total = jnp.concatenate(
                [total_ref[0, member, r : r + 1, low:high] for r in range(RATIO)], axis=1
            )
            inner_row = jnp.concatenate(
                [inner[member, r : r + 1, low:high] for r in range(RATIO)], axis=1
            )
            start_row = triple(start_ref[0, 0:1, low:high])
            place_row = triple(lax.broadcasted_iota(jnp.int32, (1, BLOCK), 1) + low)
            scores = dot(key_rows[member, 0:high], queries)
            scores = visible_scores(scores, start_row, place_row, block)
            weights = jnp.exp(scores - total)
            grad_weights = dot(value_rows[member, 0:high], grads)
            grad_scores = (weights * (grad_weights - inner_row)).astype(BF16)
            grad_natural = jnp.concatenate(
                [grad_rows[member * RATIO + r, low:high] for r in range(RATIO)], axis=0
            )
            query_natural = jnp.concatenate(
                [query_rows[member * RATIO + r, low:high] for r in range(RATIO)], axis=0
            )
            grad_value[0:high] += dot(weights.astype(BF16), grad_natural)
            grad_key[0:high] += dot(grad_scores, query_natural)
            grad_query = dot(key_ref[0, pl.ds(member * 64, 64), 0:high], grad_scores)
            grad_query = grad_query * HEAD_DIM ** (-0.5)
            cos_part = triple(cosine[:, low:high])
            sin_part = triple(sine[:, low:high])
            front, behind = grad_query[:HALF], grad_query[HALF:]
            turned = jnp.concatenate(
                [front * cos_part + behind * sin_part, behind * cos_part - front * sin_part],
                axis=0,
            ).astype(BF16)
            for r in range(RATIO):
                grad_projected[pl.ds(heads[r], 64), low:high] = turned[
                    :, r * BLOCK : (r + 1) * BLOCK
                ]
        key_across = grad_key[...].T
        front, behind = key_across[:HALF], key_across[HALF:]
        grad_projected[pl.ds(D + member * 64, 64)] = jnp.concatenate(
            [front * cosine + behind * sine, behind * cosine - front * sine], axis=0
        ).astype(BF16)
        grad_projected[pl.ds(D + KV_WIDTH + member * 64, 64)] = grad_value[...].T.astype(BF16)
        return carry

    lax.fori_loop(0, KV_HEADS, group, 0)
    x = x_ref[0].astype(F32)
    gain = gain_ref[0:1]
    inverse = inverse_root(x)
    normal = x * inverse
    normed = (normal * gain).astype(BF16)
    projected = grad_projected[...]
    sums[:QKV] += dot(projected, normed)
    grad_normed = dot(projected.T, weight_ref[0:QKV])
    scaled = grad_normed * gain
    gain_grad_ref[...] += jnp.sum(grad_normed * normal, axis=0, keepdims=True)
    tokens_ref[0] = grad_ref[0] + inverse * (
        scaled - normal * jnp.mean(scaled * normal, axis=-1, keepdims=True)
    )

    @pl.when(step == pl.num_programs(0) - 1)
    def _():
        weight_grad_ref[...] = sums[...].astype(BF16)


def attention_backward(x, start, weights, gain, tables, grad, saved):
    count, length, _ = x.shape
    return pl.pallas_call(
        attention_backward_body,
        grid=(count,),
        in_specs=[
            row_block((length, D)),
            row_block((1, length)),
            whole(weights.shape),
            whole(gain.shape),
            whole((HALF, length)),
            whole((HALF, length)),
            row_block((length, D)),
        ]
        + [row_block(part.shape[1:]) for part in saved],
        out_specs=[row_block((length, D)), whole(weights.shape), whole((1, D))],
        out_shape=[
            jax.ShapeDtypeStruct((count, length, D), F32),
            jax.ShapeDtypeStruct(weights.shape, BF16),
            jax.ShapeDtypeStruct((1, D), F32),
        ],
        scratch_shapes=[
            pltpu.VMEM((KV_HEADS, length, HEAD_DIM), BF16),
            pltpu.VMEM((KV_HEADS, length, HEAD_DIM), BF16),
            pltpu.VMEM((HEADS, length, HEAD_DIM), BF16),
            pltpu.VMEM((HEADS, length, HEAD_DIM), BF16),
            pltpu.VMEM((D, length), BF16),
            pltpu.VMEM((KV_HEADS, 8, length), F32),
            pltpu.VMEM((length, HEAD_DIM), F32),
            pltpu.VMEM((length, HEAD_DIM), F32),
            pltpu.VMEM((QKV, length), BF16),
            pltpu.VMEM(weights.shape, F32),
        ],
        compiler_params=params(),
        cost_estimate=pl.CostEstimate(
            flops=17_000_000_000, transcendentals=12_000_000, bytes_accessed=25_000_000
        ),
        name="attention_backward",
    )(x, start, weights, gain, *tables, grad, *saved)


def factors(count):
    inner = 1 << ((count.bit_length() - 1) // 2)
    return count // inner, inner


def partner(values, mask):
    count = lax.axis_size("wide")
    return lax.ppermute(values, "wide", [(i, i ^ mask) for i in range(count)])


def across(values):
    return lax.ppermute(values, "narrow", [(0, 1), (1, 0)])


def in_order(parts, place):
    bit = 1
    while bit < len(parts):
        swap = (place & bit) != 0
        parts = [jnp.where(swap, parts[i ^ bit], part) for i, part in enumerate(parts)]
        bit *= 2
    return parts


def add_all(parts):
    total = parts[0].astype(F32)
    for part in parts[1:]:
        total = total + part.astype(F32)
    return total


def adamw_update(master, first_state, second_state, gradient, factor, step_rate, decay_rate):
    clipped = gradient * factor
    first_new = beta_first * first_state + (1.0 - beta_first) * clipped
    second_new = beta_second * second_state + (1.0 - beta_second) * clipped * clipped
    first_hat = first_new / (1.0 - beta_first**STEP)
    second_hat = second_new / (1.0 - beta_second**STEP)
    master_new = master * (1.0 - step_rate * decay_rate) - step_rate * first_hat / (
        jnp.sqrt(second_hat) + adam_epsilon
    )
    return (master_new, first_new, second_new)


def sum_everywhere(values):
    outer, inner = factors(lax.axis_size("wide"))
    values = values + across(values)
    values = add_all([values] + [partner(values, k) for k in range(1, inner)])
    return add_all([values] + [partner(values, k * inner) for k in range(1, outer)])


def per_device(
    tokens,
    cotangent,
    documents,
    attention_master,
    attention_first,
    attention_second,
    feedforward_master,
    feedforward_first,
    feedforward_second,
    gain_master,
    gain_first,
    gain_second,
):
    seq_count, half_len, _ = tokens.shape
    full_len = 2 * half_len
    own_count = seq_count // 2
    place = lax.axis_index("narrow")
    first = place == 0
    outer, inner = factors(lax.axis_size("wide"))
    wide_place = lax.axis_index("wide")
    outer_place, inner_place = wide_place // inner, wide_place % inner
    tables = rotary_tables(full_len)

    def keep_send(tensor):
        top, bottom = tensor[:own_count], tensor[own_count:]
        return jnp.where(first, top, bottom), jnp.where(first, bottom, top)

    def to_sequences(tensor):
        keep, send = keep_send(tensor)
        received = across(send)
        return jnp.concatenate(
            [jnp.where(first, keep, received), jnp.where(first, received, keep)], axis=1
        )

    def halves(tensor):
        left, right = tensor[:, :half_len], tensor[:, half_len:]
        return jnp.where(first, left, right), jnp.where(first, right, left)

    def to_positions(keep, received):
        return jnp.concatenate(
            [jnp.where(first, keep, received), jnp.where(first, received, keep)], axis=0
        )

    rows = attention_master.shape[0]
    piece = attention_master.astype(BF16)
    outer_parts = [piece] + [partner(piece, k * inner) for k in range(1, outer)]
    outer_stack = jnp.stack(in_order(outer_parts, outer_place))
    inner_parts = [outer_stack] + [partner(outer_stack, k) for k in range(1, inner)]
    inner_stack = jnp.stack(in_order(inner_parts, inner_place), axis=1)
    both = in_order([inner_stack, across(inner_stack)], place)
    attention_low = jnp.stack(both, axis=2).reshape(2 * inner * outer * rows, D)

    feed_piece = feedforward_master.astype(BF16)
    feed_outer = jnp.stack(
        [feed_piece] + [partner(feed_piece, k * inner) for k in range(1, outer)], axis=1
    )
    feed_own = jnp.stack(
        [feed_outer] + [partner(feed_outer, k) for k in range(1, inner)], axis=1
    ).reshape(3, -1, D)
    feed_other = across(feed_own)

    x = to_sequences(tokens)
    cotangent_rows = to_sequences(cotangent)
    own_docs = lax.dynamic_slice_in_dim(documents, place * own_count, own_count, 0)
    start = jnp.zeros_like(own_docs)
    for number in (1, 2):
        before = jnp.sum((own_docs < number).astype(jnp.int32), axis=1, keepdims=True)
        start = jnp.where(own_docs == number, before, start)
    start = start[:, None, :]

    residual, *saved = attention_forward(x, start, attention_low, gain_master, tables)
    flat = (own_count * full_len, D)
    out, back, own_grad, other_grad, gain_second_part = feed_forward(
        residual.reshape(flat), cotangent_rows.reshape(flat), feed_own, feed_other, gain_master, inner
    )
    keep, send = halves(out.reshape(own_count, full_len, D))
    outputs = to_positions(keep, across(send))

    received = across(other_grad)
    summed = [add_all([own_grad[k], received[k]]).astype(BF16) for k in range(inner)]
    summed = add_all([summed[0]] + [partner(summed[k], k) for k in range(1, inner)])
    summed = summed.reshape(3, outer, -1, D)
    feedforward_grad = add_all(
        [summed[:, 0]] + [partner(summed[:, k].astype(BF16), k * inner) for k in range(1, outer)]
    )

    grad_rows, weight_grad, gain_first_part = attention_backward(
        x, start, attention_low, gain_master, tables, back.reshape(own_count, full_len, D), saved
    )
    keep, send = halves(grad_rows)
    grad_tokens = to_positions(keep, across(send.astype(BF16)).astype(F32))

    weight_grad = weight_grad.reshape(outer, inner, 2, rows, D)
    even, odd = weight_grad[:, :, 0], weight_grad[:, :, 1]
    received = across(jnp.where(first, odd, even))
    summed = add_all([jnp.where(first, even, odd), received]).astype(BF16)
    parts = [
        lax.dynamic_index_in_dim(summed, inner_place ^ k, 1, keepdims=False) for k in range(inner)
    ]
    summed = add_all([parts[0]] + [partner(parts[k], k) for k in range(1, inner)])
    parts = [
        lax.dynamic_index_in_dim(summed, outer_place ^ k, 0, keepdims=False) for k in range(outer)
    ]
    attention_grad = add_all(
        [parts[0]] + [partner(parts[k].astype(BF16), k * inner) for k in range(1, outer)]
    )

    gain_grad = sum_everywhere(jnp.concatenate([gain_first_part, gain_second_part], axis=0))
    local_squares = jnp.sum(attention_grad * attention_grad) + jnp.sum(
        feedforward_grad * feedforward_grad
    )
    squares = sum_everywhere(jnp.full((1, 128), local_squares, F32))[0, 0]
    grad_norm = jnp.sqrt(squares + jnp.sum(gain_grad * gain_grad))
    factor = jnp.minimum(1.0, clip_limit / (grad_norm + 1e-06))
    update = functools.partial(adamw_update, factor=factor)
    attention_new = update(
        attention_master,
        attention_first,
        attention_second,
        attention_grad,
        step_rate=rate_matrix,
        decay_rate=weight_decay,
    )
    feedforward_new = update(
        feedforward_master,
        feedforward_first,
        feedforward_second,
        feedforward_grad,
        step_rate=rate_matrix,
        decay_rate=weight_decay,
    )
    gain_new = update(
        gain_master, gain_first, gain_second, gain_grad, step_rate=rate_gain, decay_rate=0.0
    )
    return (outputs, grad_tokens, grad_norm, *attention_new, *feedforward_new, *gain_new)


def solution(mesh):
    sequences = P("wide", "narrow", None)
    attention = P(("wide", "narrow"), None)
    feedforward = P(None, ("narrow", "wide"), None)
    state = (attention,) * 3 + (feedforward,) * 3 + (P(),) * 3
    return jax.shard_map(
        per_device,
        mesh=mesh,
        in_specs=(sequences, sequences, P("wide", None)) + state,
        out_specs=(sequences, sequences, P()) + state,
        check_vma=False,
    )
```

```python
import functools

import jax
import jax.numpy as jnp
import numpy as np
from jax import lax
from jax.experimental import pallas as pl
from jax.experimental.pallas import tpu as pltpu
from jax.sharding import PartitionSpec as P

D = 576
HEADS = 9
KV_HEADS = 3
RATIO = 3
HEAD_DIM = 64
HALF = 32
STEP = 10
KV_WIDTH = 192
QKV = 960
BLOCK = 256

norm_epsilon = 1e-05
adam_epsilon = 1e-08
beta_first = 0.9
beta_second = 0.999
weight_decay = 0.1
rate_matrix = 0.05
rate_gain = 0.5
clip_limit = 1.0
rotary_base = 10000.0
masked_value = -1e30

F32 = jnp.float32
BF16 = jnp.bfloat16
VMEM_LIMIT = 60 * 2**20


def rotary_tables(length):
    frequency = np.float32(rotary_base) ** (
        np.float32(-2.0) * np.arange(HALF, dtype=np.float32) / np.float32(HEAD_DIM)
    )
    angles = np.arange(length, dtype=np.float32)[None, :] * frequency.astype(np.float32)[:, None]
    return jnp.asarray(np.cos(angles), F32), jnp.asarray(np.sin(angles), F32)


def dot(left, right, left_dim=1, right_dim=0):
    return lax.dot_general(
        left, right, (((left_dim,), (right_dim,)), ((), ())), preferred_element_type=F32
    )


def inverse_root(values):
    return lax.rsqrt(jnp.mean(values * values, axis=0, keepdims=True) + norm_epsilon)


def joined(own, other, place):
    first = place == 0
    return jnp.concatenate(
        [jnp.where(first, own, other), jnp.where(first, other, own)], axis=1
    )


def lane_sums(values):
    lanes = 128
    total = values[:, :lanes]
    for low in range(lanes, values.shape[1], lanes):
        total = total + values[:, low : low + lanes]
    return total


def norm_backward(grad_normed, normal, inverse, gain):
    scaled = grad_normed * gain
    return inverse * (scaled - normal * jnp.mean(scaled * normal, axis=0, keepdims=True))


def visible_scores(scores, start_row, place_row, query_block):
    parts = []
    for key_block in range(query_block + 1):
        part = scores[key_block * BLOCK : (key_block + 1) * BLOCK]
        place = lax.broadcasted_iota(jnp.int32, part.shape, 0) + key_block * BLOCK
        seen = place >= start_row
        if key_block == query_block:
            seen = seen & (place <= place_row)
        parts.append(jnp.where(seen, part, masked_value))
    return jnp.concatenate(parts, axis=0) if len(parts) > 1 else parts[0]


def triple(row):
    return jnp.concatenate([row] * RATIO, axis=1)


def turn(rows, cosine, sine):
    front, behind = rows[:HALF], rows[HALF:]
    return jnp.concatenate([front * cosine - behind * sine, behind * cosine + front * sine], axis=0)


def turn_back(rows, cosine, sine):
    front, behind = rows[:HALF], rows[HALF:]
    return jnp.concatenate([front * cosine + behind * sine, behind * cosine - front * sine], axis=0)


def attention_forward_body(
    info_ref,
    own_ref,
    other_ref,
    start_ref,
    pieces_own_ref,
    pieces_other_ref,
    gain_ref,
    cosine_ref,
    sine_ref,
    residual_ref,
    query_ref,
    key_ref,
    value_ref,
    mixed_ref,
    total_ref,
    weight_ref,
    out_rows,
    key_rows,
    x_across,
):
    @pl.when(pl.program_id(0) == 0)
    def _():
        chunks, rows, _ = pieces_own_ref.shape
        for chunk in range(2 * chunks):
            index = info_ref[1 + chunk]
            is_own = index < chunks
            index = jnp.where(is_own, index, index - chunks)
            weight_ref[chunk * rows : (chunk + 1) * rows] = jnp.where(
                is_own, pieces_own_ref[index], pieces_other_ref[index]
            )
        out_rows[...] = weight_ref[QKV:].T

    x = joined(own_ref[0], other_ref[0], info_ref[0])
    length = x.shape[1]
    x_across[...] = x
    x = x.astype(F32)
    normed = (x * inverse_root(x) * gain_ref[:, 0:1]).astype(BF16)
    cosine = cosine_ref[...]
    sine = sine_ref[...]
    projected = dot(weight_ref[0:QKV], normed)
    for head in range(HEADS):
        rows = slice(head * 64, head * 64 + 64)
        query_ref[0, rows] = (turn(projected[rows], cosine, sine) * HEAD_DIM ** (-0.5)).astype(
            BF16
        )
    for head in range(KV_HEADS):
        rows = slice(head * 64, head * 64 + 64)
        rotated = turn(projected[D + head * 64 : D + head * 64 + 64], cosine, sine)
        key_ref[0, rows] = rotated.astype(BF16)
        key_rows[head] = rotated.T.astype(BF16)
    value_ref[0] = projected[D + KV_WIDTH :].astype(BF16)

    def group(member, carry):
        for block in range(length // BLOCK):
            low, high = block * BLOCK, (block + 1) * BLOCK
            heads = [member * 192 + r * 64 for r in range(RATIO)]
            queries = jnp.concatenate(
                [query_ref[0, pl.ds(h, 64), low:high] for h in heads], axis=1
            )
            scores = dot(key_rows[member, 0:high], queries)
            start_row = triple(start_ref[0, 0:1, low:high])
            place_row = triple(lax.broadcasted_iota(jnp.int32, (1, BLOCK), 1) + low)
            scores = visible_scores(scores, start_row, place_row, block)
            top = jnp.max(scores, axis=0, keepdims=True)
            exponent = jnp.exp(scores - top)
            total = jnp.sum(exponent, axis=0, keepdims=True)
            values = value_ref[0, pl.ds(member * 64, 64), 0:high]
            mixed = dot(values, exponent.astype(BF16)) * (1.0 / total)
            log_total = top + jnp.log(total)
            for r in range(RATIO):
                lanes = slice(r * BLOCK, (r + 1) * BLOCK)
                mixed_ref[0, pl.ds(heads[r], 64), low:high] = mixed[:, lanes].astype(BF16)
                total_ref[0, member, r : r + 1, low:high] = log_total[:, lanes]
        return carry

    lax.fori_loop(0, KV_HEADS, group, 0)
    residual_ref[0] = x_across[...].astype(F32) + dot(out_rows[...], mixed_ref[0])


def whole(shape):
    return pl.BlockSpec(
        tuple(shape), lambda *_: (0,) * len(shape), pipeline_mode=pl.Buffered(1)
    )


def step_spec(shape, mode=None):
    return pl.BlockSpec((1,) + tuple(shape[1:]), lambda i, info: (i,) + (0,) * (len(shape) - 1))


def member_spec(shape, index):
    return pl.BlockSpec(
        (1,) + tuple(shape[1:]),
        lambda i, info: (index,) + (0,) * (len(shape) - 1),
        pipeline_mode=pl.Buffered(1),
    )


def own_spec(shape, count, index):
    return pl.BlockSpec(
        (1,) + tuple(shape[1:]),
        lambda i, info: (info[0] * count + index,) + (0,) * (len(shape) - 1),
        pipeline_mode=pl.Buffered(1),
    )


def params():
    return pltpu.CompilerParams(dimension_semantics=("arbitrary",), vmem_limit_bytes=VMEM_LIMIT)


def attention_forward(info, own, other, start, pieces_own, pieces_other, gain, tables):
    count = other.shape[0]
    length = 2 * other.shape[2]
    outs = [
        ((count, D, length), F32),
        ((count, D, length), BF16),
        ((count, KV_WIDTH, length), BF16),
        ((count, KV_WIDTH, length), BF16),
        ((count, D, length), BF16),
        ((count, KV_HEADS, 8, length), F32),
    ]
    weight = (QKV + D, D)
    return pl.pallas_call(
        attention_forward_body,
        grid_spec=pltpu.PrefetchScalarGridSpec(
            num_scalar_prefetch=1,
            grid=(count,),
            in_specs=[
                pl.BlockSpec(
                    (1,) + own.shape[1:], lambda i, info: (info[0] * count + i, 0, 0)
                ),
                step_spec(other.shape),
                step_spec(start.shape),
                whole(pieces_own.shape),
                whole(pieces_other.shape),
                whole(gain.shape),
                whole((HALF, length)),
                whole((HALF, length)),
            ],
            out_specs=[step_spec(shape) for shape, _ in outs] + [whole(weight)],
            scratch_shapes=[
                pltpu.VMEM((D, D), BF16),
                pltpu.VMEM((KV_HEADS, length, HEAD_DIM), BF16),
                pltpu.VMEM((D, length), BF16),
            ],
        ),
        out_shape=[jax.ShapeDtypeStruct(shape, kind) for shape, kind in outs]
        + [jax.ShapeDtypeStruct(weight, BF16)],
        compiler_params=params(),
        cost_estimate=pl.CostEstimate(
            flops=8_000_000_000, transcendentals=12_000_000, bytes_accessed=20_000_000
        ),
        name="attention_forward",
    )(info, own, other, start, pieces_own, pieces_other, gain, *tables)


def stacked(refs, kinds):
    parts = [ref[:, kind].reshape(-1, D) for kind in kinds for ref in refs]
    return jnp.concatenate(parts, axis=0) if len(parts) > 1 else parts[0]


def feed_body(part_count, info_ref, residual_ref, cotangent_own_ref, cotangent_other_ref, *refs):
    weight_refs = refs[:part_count], refs[part_count : 2 * part_count]
    (
        gain_ref,
        out_own_ref,
        out_other_ref,
        back_ref,
        gain_grad_ref,
        grad_own_ref,
        grad_other_ref,
        sums,
        gain_sums,
    ) = refs[2 * part_count :]
    step = pl.program_id(0)
    units = sums.shape[2] // 3
    residual = residual_ref[0]
    cotangent = jnp.where(step % 2 == 0, cotangent_own_ref[0], cotangent_other_ref[0])
    gain = gain_ref[:, 1:2]
    inverse = inverse_root(residual)
    normal = residual * inverse
    normed = (normal * gain).astype(BF16)

    @pl.when(step == 0)
    def _():
        sums[...] = jnp.zeros_like(sums)
        gain_sums[...] = jnp.zeros_like(gain_sums)

    out = residual
    grad_normed = jnp.zeros_like(residual)
    for part, parts in enumerate(weight_refs):
        pair = stacked(parts, (0, 1))
        down = stacked(parts, (2,))
        both = dot(pair, normed)
        gate, upward = both[:units], both[units:]
        grad_hidden = dot(down, cotangent)
        sigmoid_gate = jax.nn.sigmoid(gate)
        swish = gate * sigmoid_gate
        hidden = (swish * upward).astype(BF16)
        grad_gate = (
            grad_hidden * upward * (sigmoid_gate + swish * (1.0 - sigmoid_gate))
        ).astype(BF16)
        grad_upward = (grad_hidden * swish).astype(BF16)
        grads = jnp.concatenate([grad_gate, grad_upward], axis=0)
        out = out + dot(down, hidden, 0, 0)
        grad_normed = grad_normed + dot(pair, grads, 0, 0)
        sums[part, :, : 2 * units] += dot(normed, grads, 1, 1)
        sums[part, :, 2 * units :] += dot(cotangent, hidden, 1, 1)

    out = out.astype(BF16)

    @pl.when(step % 2 == 0)
    def _():
        out_own_ref[0] = out

    @pl.when(step % 2 == 1)
    def _():
        out_other_ref[0] = out

    gain_sums[...] += lane_sums(grad_normed * normal)
    back_ref[0] = cotangent.astype(F32) + norm_backward(grad_normed, normal, inverse, gain)

    @pl.when(step == pl.num_programs(0) - 1)
    def _():
        pieces, kinds, rows, _ = grad_own_ref.shape
        for part, grad_ref in enumerate((grad_own_ref, grad_other_ref)):
            for kind in range(kinds):
                flipped = sums[part, :, kind * units : (kind + 1) * units].astype(BF16).T
                for piece in range(pieces):
                    grad_ref[piece, kind] = flipped[piece * rows : (piece + 1) * rows]
        gain_grad_ref[...] = jnp.sum(gain_sums[...].T, axis=0, keepdims=True)


def feed_forward(info, residual, cotangent_own, cotangent_other, weights, gain, pieces):
    count, _, length = residual.shape
    half = length // 2
    part_count = len(weights) // 2
    units = sum(part.size // (3 * D) for part in weights[:part_count])
    block = (1, D, half)
    full = pl.BlockSpec(block, lambda i, info: (i // 2, 0, (i + info[0]) % 2))
    own = pl.BlockSpec(block, lambda i, info: (info[0] * count + i // 2, 0, 0))
    other = pl.BlockSpec(block, lambda i, info: (i // 2, 0, 0))
    grad_shape = (pieces, 3, units // pieces, D)
    return pl.pallas_call(
        functools.partial(feed_body, part_count),
        grid_spec=pltpu.PrefetchScalarGridSpec(
            num_scalar_prefetch=1,
            grid=(2 * count,),
            in_specs=[full, own, other]
            + [whole(weight.shape) for weight in weights]
            + [whole(gain.shape)],
            out_specs=[own, other, full, whole((1, D))] + [whole(grad_shape)] * 2,
            scratch_shapes=[
                pltpu.VMEM((2, D, 3 * units), F32),
                pltpu.VMEM((D, 128), F32),
            ],
        ),
        out_shape=[
            jax.ShapeDtypeStruct(cotangent_own.shape, BF16),
            jax.ShapeDtypeStruct(cotangent_other.shape, BF16),
            jax.ShapeDtypeStruct(residual.shape, F32),
            jax.ShapeDtypeStruct((1, D), F32),
        ]
        + [jax.ShapeDtypeStruct(grad_shape, BF16)] * 2,
        compiler_params=params(),
        cost_estimate=pl.CostEstimate(
            flops=32_000_000_000, transcendentals=6_000_000, bytes_accessed=30_000_000
        ),
        name="feed_forward",
    )(info, residual, cotangent_own, cotangent_other, *weights, gain)


def attention_backward_body(
    last,
    info_ref,
    own_ref,
    other_ref,
    start_ref,
    weight_ref,
    gain_ref,
    cosine_ref,
    sine_ref,
    grad_ref,
    query_ref,
    key_ref,
    value_ref,
    mixed_ref,
    total_ref,
    *refs,
):
    refs = list(refs)
    if last:
        earlier_ref, earlier_gain_ref = refs[:2]
        refs = refs[3:]
    tokens_own_ref, tokens_other_ref, weight_grad_ref, gain_grad_ref = refs[:4]
    (
        across_rows,
        key_rows,
        value_rows,
        query_rows,
        grad_rows,
        grad_across,
        inner,
        grad_key,
        grad_value,
        grad_projected,
        sums,
    ) = refs[4:15]
    place = info_ref[0]
    half = own_ref.shape[2]
    length = 2 * half
    cosine = cosine_ref[...]
    sine = sine_ref[...]
    across_rows[...] = weight_ref[0:QKV].T
    branch = grad_ref[0].astype(BF16)
    sums[QKV:] = dot(mixed_ref[0], branch, 1, 1)
    grad_mixed = dot(weight_ref[QKV:], branch)
    for head in range(HEADS):
        rows = slice(head * 64, head * 64 + 64)
        part = grad_mixed[rows]
        grad_across[rows] = part.astype(BF16)
        grad_rows[head] = part.T.astype(BF16)
        query_rows[head] = query_ref[0, rows].T
        inner[head // RATIO, head % RATIO : head % RATIO + 1] = jnp.sum(
            part.astype(BF16).astype(F32) * mixed_ref[0, rows].astype(F32), axis=0, keepdims=True
        )
    for head in range(KV_HEADS):
        rows = slice(head * 64, head * 64 + 64)
        key_rows[head] = key_ref[0, rows].T
        value_rows[head] = value_ref[0, rows].T

    def group(member, carry):
        grad_key[...] = jnp.zeros_like(grad_key)
        grad_value[...] = jnp.zeros_like(grad_value)
        for block in range(length // BLOCK):
            low, high = block * BLOCK, (block + 1) * BLOCK
            heads = [member * 192 + r * 64 for r in range(RATIO)]
            queries = jnp.concatenate([query_ref[0, pl.ds(h, 64), low:high] for h in heads], axis=1)
            grads = jnp.concatenate([grad_across[pl.ds(h, 64), low:high] for h in heads], axis=1)
            total = jnp.concatenate(
                [total_ref[0, member, r : r + 1, low:high] for r in range(RATIO)], axis=1
            )
            inner_row = jnp.concatenate(
                [inner[member, r : r + 1, low:high] for r in range(RATIO)], axis=1
            )
            start_row = triple(start_ref[0, 0:1, low:high])
            place_row = triple(lax.broadcasted_iota(jnp.int32, (1, BLOCK), 1) + low)
            scores = dot(key_rows[member, 0:high], queries)
            scores = visible_scores(scores, start_row, place_row, block)
            weights = jnp.exp(scores - total)
            grad_weights = dot(value_rows[member, 0:high], grads)
            grad_scores = (weights * (grad_weights - inner_row)).astype(BF16)
            grad_natural = jnp.concatenate(
                [grad_rows[member * RATIO + r, low:high] for r in range(RATIO)], axis=0
            )
            query_natural = jnp.concatenate(
                [query_rows[member * RATIO + r, low:high] for r in range(RATIO)], axis=0
            )
            grad_value[0:high] += dot(weights.astype(BF16), grad_natural)
            grad_key[0:high] += dot(grad_scores, query_natural)
            grad_query = dot(key_ref[0, pl.ds(member * 64, 64), 0:high], grad_scores)
            turned = turn_back(
                grad_query * HEAD_DIM ** (-0.5),
                triple(cosine[:, low:high]),
                triple(sine[:, low:high]),
            ).astype(BF16)
            for r in range(RATIO):
                grad_projected[pl.ds(heads[r], 64), low:high] = turned[
                    :, r * BLOCK : (r + 1) * BLOCK
                ]
        grad_projected[pl.ds(D + member * 64, 64)] = turn_back(
            grad_key[...].T, cosine, sine
        ).astype(BF16)
        grad_projected[pl.ds(D + KV_WIDTH + member * 64, 64)] = grad_value[...].T.astype(BF16)
        return carry

    lax.fori_loop(0, KV_HEADS, group, 0)
    x = joined(own_ref[0], other_ref[0], place).astype(F32)
    gain = gain_ref[:, 0:1]
    inverse = inverse_root(x)
    normal = x * inverse
    normed = (normal * gain).astype(BF16)
    sums[:QKV] = dot(grad_projected[...], normed, 1, 1)
    if last:
        chunks, rows, _ = weight_grad_ref.shape
        for chunk in range(chunks):
            part = slice(chunk * rows, (chunk + 1) * rows)
            weight_grad_ref[info_ref[1 + chunk]] = (sums[part] + earlier_ref[part]).astype(BF16)
    else:
        weight_grad_ref[...] = sums[...]
    grad_normed = dot(across_rows[...], grad_projected[...])
    gain_sums = lane_sums(grad_normed * normal)
    gain_row = jnp.sum(gain_sums.T, axis=0, keepdims=True)
    gain_grad_ref[...] = gain_row + earlier_gain_ref[...] if last else gain_row
    grad_x = grad_ref[0] + norm_backward(grad_normed, normal, inverse, gain)
    left, right = grad_x[:, :half], grad_x[:, half:]
    first = place == 0
    tokens_own_ref[0] = jnp.where(first, left, right)
    tokens_other_ref[0] = jnp.where(first, right, left).astype(BF16)


def attention_backward(
    index, info, own, other, start, weights, gain, tables, grad, saved, earlier, chunks
):
    count = other.shape[0]
    length = 2 * other.shape[2]
    last = len(earlier) > 0
    rows = QKV + D
    own_out = jax.ShapeDtypeStruct(own.shape, F32)
    if last:
        grad_shape = jax.ShapeDtypeStruct((chunks, rows // chunks, D), BF16)
        extra = [whole((rows, D)), whole((1, D)), pl.BlockSpec(memory_space=pl.ANY)]
        aliases = {14 + 2: 0}
    else:
        grad_shape = jax.ShapeDtypeStruct((rows, D), F32)
        extra = []
        aliases = {}
    return pl.pallas_call(
        functools.partial(attention_backward_body, last),
        grid_spec=pltpu.PrefetchScalarGridSpec(
            num_scalar_prefetch=1,
            grid=(1,),
            in_specs=[
                own_spec(own.shape, count, index),
                member_spec(other.shape, index),
                member_spec(start.shape, index),
                whole(weights.shape),
                whole(gain.shape),
                whole((HALF, length)),
                whole((HALF, length)),
                member_spec(grad.shape, index),
            ]
            + [member_spec(part.shape, index) for part in saved]
            + extra,
            out_specs=[
                own_spec(own.shape, count, index),
                member_spec((1, D, length // 2), 0),
                whole(grad_shape.shape),
                whole((1, D)),
            ],
            scratch_shapes=[
                pltpu.VMEM((D, QKV), BF16),
                pltpu.VMEM((KV_HEADS, length, HEAD_DIM), BF16),
                pltpu.VMEM((KV_HEADS, length, HEAD_DIM), BF16),
                pltpu.VMEM((HEADS, length, HEAD_DIM), BF16),
                pltpu.VMEM((HEADS, length, HEAD_DIM), BF16),
                pltpu.VMEM((D, length), BF16),
                pltpu.VMEM((KV_HEADS, 8, length), F32),
                pltpu.VMEM((length, HEAD_DIM), F32),
                pltpu.VMEM((length, HEAD_DIM), F32),
                pltpu.VMEM((QKV, length), BF16),
                pltpu.VMEM((rows, D), F32),
            ],
        ),
        out_shape=[
            own_out,
            jax.ShapeDtypeStruct((1, D, length // 2), BF16),
            grad_shape,
            jax.ShapeDtypeStruct((1, D), F32),
        ],
        input_output_aliases=aliases,
        compiler_params=params(),
        cost_estimate=pl.CostEstimate(
            flops=9_000_000_000, transcendentals=6_000_000, bytes_accessed=15_000_000
        ),
        name="attention_backward",
    )(info, own, other, start, weights, gain, *tables, grad, *saved, *earlier)


def factors(count):
    inner = 1 << ((count.bit_length() - 1) // 2)
    return count // inner, inner


def partner(values, mask):
    count = lax.axis_size("wide")
    return lax.ppermute(values, "wide", [(i, i ^ mask) for i in range(count)])


def across(values):
    return lax.ppermute(values, "narrow", [(0, 1), (1, 0)])


def in_order(parts, place):
    bit = 1
    while bit < len(parts):
        swap = (place & bit) != 0
        parts = [jnp.where(swap, parts[i ^ bit], part) for i, part in enumerate(parts)]
        bit *= 2
    return parts


def add_all(parts):
    total = parts[0].astype(F32)
    for part in parts[1:]:
        total = total + part.astype(F32)
    return total


def adamw_update(master, first_state, second_state, gradient, factor, step_rate, decay_rate):
    clipped = gradient * factor
    first_new = beta_first * first_state + (1.0 - beta_first) * clipped
    second_new = beta_second * second_state + (1.0 - beta_second) * clipped * clipped
    first_hat = first_new / (1.0 - beta_first**STEP)
    second_hat = second_new / (1.0 - beta_second**STEP)
    master_new = master * (1.0 - step_rate * decay_rate) - step_rate * first_hat / (
        jnp.sqrt(second_hat) + adam_epsilon
    )
    return (master_new, first_new, second_new)


def sum_everywhere(value):
    devices = lax.axis_size("wide") * lax.axis_size("narrow")
    sent = jnp.full((devices, 128), value, F32)
    got = lax.all_to_all(sent, ("wide", "narrow"), 0, 0, tiled=True)
    return jnp.sum(got[:, 0])


def per_device(
    tokens,
    cotangent,
    documents,
    attention_master,
    attention_first,
    attention_second,
    feedforward_master,
    feedforward_first,
    feedforward_second,
    gain_master,
    gain_first,
    gain_second,
):
    seq_count, half_len, _ = tokens.shape
    own_count = seq_count // 2
    place = lax.axis_index("narrow")
    first = place == 0
    outer, inner = factors(lax.axis_size("wide"))
    wide_place = lax.axis_index("wide")
    outer_place, inner_place = wide_place // inner, wide_place % inner
    tables = rotary_tables(2 * half_len)
    gain_columns = gain_master.T
    x_own = jnp.swapaxes(tokens, 1, 2)
    cotangent_own = jnp.swapaxes(cotangent, 1, 2)

    def swap(tensor):
        return across(jnp.where(first, tensor[own_count:], tensor[:own_count]))

    rows = attention_master.shape[0]
    aligned = rows % 16 == 0
    piece = attention_master.astype(BF16)
    parts = [piece] + [partner(piece, k * inner) for k in range(1, outer)]
    stack = jnp.stack(parts if aligned else in_order(parts, outer_place))
    parts = [stack] + [partner(stack, k) for k in range(1, inner)]
    feed_piece = feedforward_master.astype(BF16)
    feed_outer = jnp.stack(
        [feed_piece] + [partner(feed_piece, k * inner) for k in range(1, outer)]
    )
    feed_outer, parts[1:] = lax.optimization_barrier((feed_outer, parts[1:]))
    feed_parts = [feed_outer] + [partner(feed_outer, k) for k in range(1, inner)]
    if aligned:
        stack = jnp.stack(parts)
        pieces_own = stack.reshape(-1, rows, D)
        pieces_other = across(stack).reshape(-1, rows, D)
        chunk = jnp.arange(2 * inner * outer, dtype=jnp.int32)
        order = (
            ((chunk % 2) ^ place) * inner + ((chunk // 2 % inner) ^ inner_place)
        ) * outer + ((chunk // (2 * inner)) ^ outer_place)
    else:
        stack = jnp.stack(in_order(parts, inner_place), axis=1)
        pieces = jnp.stack(in_order([stack, across(stack)], place), axis=2).reshape(-1, 48, D)
        pieces_own, pieces_other = pieces[:16], pieces[16:]
        order = jnp.arange(pieces.shape[0], dtype=jnp.int32)
    chunks = order.shape[0]
    info = jnp.concatenate([jnp.full((1,), place, jnp.int32), order.astype(jnp.int32)])

    x_other = swap(x_own)
    own_docs = lax.dynamic_slice_in_dim(documents, place * own_count, own_count, 0)
    start = jnp.zeros_like(own_docs)
    for number in (1, 2):
        before = jnp.sum((own_docs < number).astype(jnp.int32), axis=1, keepdims=True)
        start = jnp.where(own_docs == number, before, start)
    start = start[:, None, :]

    cotangent_other = swap(cotangent_own)

    residual, *saved, attention_low = attention_forward(
        info, x_own, x_other, start, pieces_own, pieces_other, gain_columns, tables
    )
    feed_parts, residual = lax.optimization_barrier((feed_parts, residual))
    if aligned:
        feed_weights = feed_parts + [across(part) for part in feed_parts]
    else:
        stack = jnp.stack(feed_parts)
        feed_weights = [
            jnp.swapaxes(part.reshape(-1, 3, rows, D), 0, 1).reshape(1, 3, -1, D)
            for part in (stack, across(stack))
        ]
    outputs, out_other, back, gain_second_part, own_grad, other_grad = feed_forward(
        info, residual, cotangent_own, cotangent_other, feed_weights, gain_columns, inner
    )

    def place_other(whole_array, received):
        return lax.dynamic_update_slice_in_dim(
            whole_array, received.astype(whole_array.dtype), (1 - place) * own_count, 0
        )

    outputs = place_other(outputs, across(out_other))

    def narrow_sum(own, other):
        received = across(other)
        return [add_all([own[k], received[k]]).astype(BF16) for k in range(own.shape[0])]

    def backward(index, earlier):
        return attention_backward(
            index,
            info,
            x_own,
            x_other,
            start,
            attention_low,
            gain_columns,
            tables,
            back,
            saved,
            earlier,
            chunks,
        )

    received = across(other_grad)
    grad_own, grad_other, *sums = backward(0, [])
    received, own_grad, sums = lax.optimization_barrier((received, own_grad, sums))
    feed_sums = [add_all([own_grad[k], received[k]]).astype(BF16) for k in range(inner)]
    feed_sums, sums = lax.optimization_barrier((feed_sums, sums))
    feed_got = [feed_sums[0]] + [partner(feed_sums[k], k) for k in range(1, inner)]
    grad_own, grad_last, weight_grad, gain_first_part = backward(1, [*sums, grad_own])
    feed_got, weight_grad, gain_first_part = lax.optimization_barrier(
        (feed_got, weight_grad, gain_first_part)
    )
    grad_other = jnp.concatenate([grad_other, grad_last], axis=0)
    gain_grad = jnp.concatenate([gain_first_part, gain_second_part], axis=0)

    if aligned:
        weight_grad = weight_grad.reshape(2, inner, outer, rows, D)
        kept, sent = weight_grad[0], weight_grad[1]
    else:
        weight_grad = weight_grad.reshape(outer, inner, 2, rows, D)
        even, odd = weight_grad[:, :, 0], weight_grad[:, :, 1]
        kept, sent = jnp.where(first, even, odd), jnp.where(first, odd, even)
    received, gain_received = lax.optimization_barrier((across(sent), across(gain_grad)))
    gain_grad = gain_grad + gain_received
    if aligned:
        parts = [add_all([kept[k], received[k]]).astype(BF16) for k in range(inner)]
    else:
        total = add_all([kept, received]).astype(BF16)
        parts = in_order([total[:, k] for k in range(inner)], inner_place)
    summed = add_all(feed_got).reshape(3, outer, -1, D)
    parts, gain_grad, summed = lax.optimization_barrier((parts, gain_grad, summed))
    got = [parts[0]] + [partner(parts[k], k) for k in range(1, inner)]
    gain_got = [gain_grad] + [partner(gain_grad, k) for k in range(1, inner)]
    feed_last = [summed[:, 0]] + [
        partner(summed[:, k].astype(BF16), k * inner) for k in range(1, outer)
    ]
    grad_tokens = place_other(grad_own, across(grad_other))
    got, gain_got = lax.optimization_barrier((got, gain_got))
    gain_grad = add_all(gain_got)
    total = add_all(got)
    parts = [total[k] for k in range(outer)]
    if not aligned:
        parts = in_order(parts, outer_place)
    attention_grad = add_all(
        [parts[0]] + [partner(parts[k].astype(BF16), k * inner) for k in range(1, outer)]
    )
    gain_grad = add_all([gain_grad] + [partner(gain_grad, k * inner) for k in range(1, outer)])
    feedforward_grad = add_all(feed_last)
    local_squares = jnp.sum(attention_grad * attention_grad) + jnp.sum(
        feedforward_grad * feedforward_grad
    )
    grad_norm = jnp.sqrt(sum_everywhere(local_squares) + jnp.sum(gain_grad * gain_grad))
    factor = jnp.minimum(1.0, clip_limit / (grad_norm + 1e-06))
    update = functools.partial(adamw_update, factor=factor)
    attention_new = update(
        attention_master,
        attention_first,
        attention_second,
        attention_grad,
        step_rate=rate_matrix,
        decay_rate=weight_decay,
    )
    feedforward_new = update(
        feedforward_master,
        feedforward_first,
        feedforward_second,
        feedforward_grad,
        step_rate=rate_matrix,
        decay_rate=weight_decay,
    )
    gain_new = update(
        gain_master, gain_first, gain_second, gain_grad, step_rate=rate_gain, decay_rate=0.0
    )
    outputs = jnp.swapaxes(outputs, 1, 2)
    grad_tokens = jnp.swapaxes(grad_tokens, 1, 2)
    return (outputs, grad_tokens, grad_norm, *attention_new, *feedforward_new, *gain_new)


def solution(mesh):
    sequences = P("wide", "narrow", None)
    attention = P(("wide", "narrow"), None)
    feedforward = P(None, ("narrow", "wide"), None)
    state = (attention,) * 3 + (feedforward,) * 3 + (P(),) * 3
    return jax.shard_map(
        per_device,
        mesh=mesh,
        in_specs=(sequences, sequences, P("wide", None)) + state,
        out_specs=(sequences, sequences, P()) + state,
        check_vma=False,
    )
```

```python
import functools

import jax
import jax.numpy as jnp
import numpy as np
from jax import lax
from jax.experimental import pallas as pl
from jax.experimental.pallas import tpu as pltpu
from jax.sharding import PartitionSpec as P

D = 576
HEADS = 9
KV_HEADS = 3
RATIO = 3
HEAD_DIM = 64
HALF = 32
STEP = 10
KV_WIDTH = 192
QKV = 960
BLOCK = 256

norm_epsilon = 1e-05
adam_epsilon = 1e-08
beta_first = 0.9
beta_second = 0.999
weight_decay = 0.1
rate_matrix = 0.05
rate_gain = 0.5
clip_limit = 1.0
rotary_base = 10000.0
masked_value = -1e30

F32 = jnp.float32
BF16 = jnp.bfloat16
VMEM_LIMIT = 60 * 2**20
SHORT = pl.CostEstimate(flops=1_000_000, transcendentals=0, bytes_accessed=100_000)


def rotary_tables(length):
    frequency = np.float32(rotary_base) ** (
        np.float32(-2.0) * np.arange(HALF, dtype=np.float32) / np.float32(HEAD_DIM)
    )
    angles = np.arange(length, dtype=np.float32)[None, :] * frequency.astype(np.float32)[:, None]
    return jnp.asarray(np.cos(angles), F32), jnp.asarray(np.sin(angles), F32)


def dot(left, right, left_dim=1, right_dim=0):
    return lax.dot_general(
        left, right, (((left_dim,), (right_dim,)), ((), ())), preferred_element_type=F32
    )


def inverse_root(values):
    return lax.rsqrt(jnp.mean(values * values, axis=0, keepdims=True) + norm_epsilon)


def joined(own, other, place):
    first = place == 0
    return jnp.concatenate(
        [jnp.where(first, own, other), jnp.where(first, other, own)], axis=1
    )


def lane_sums(values):
    lanes = 128
    total = values[:, :lanes]
    for low in range(lanes, values.shape[1], lanes):
        total = total + values[:, low : low + lanes]
    return total


def norm_backward(grad_normed, normal, inverse, gain):
    scaled = grad_normed * gain
    return inverse * (scaled - normal * jnp.mean(scaled * normal, axis=0, keepdims=True))


def visible_scores(scores, start_row, place_row, low, key_low):
    inside = low >= 256 and low + BLOCK <= 768 and key_low >= 256
    if inside and key_low < low:
        return scores
    place = lax.broadcasted_iota(jnp.int32, scores.shape, 0) + key_low
    if inside:
        seen = place <= place_row
    else:
        seen = place >= start_row
        if key_low >= low:
            seen = seen & (place <= place_row)
    return jnp.where(seen, scores, masked_value)


def triple(row):
    return jnp.concatenate([row] * RATIO, axis=1)


def turn(rows, cosine, sine):
    front, behind = rows[:HALF], rows[HALF:]
    return jnp.concatenate([front * cosine - behind * sine, behind * cosine + front * sine], axis=0)


def turn_back(rows, cosine, sine):
    front, behind = rows[:HALF], rows[HALF:]
    return jnp.concatenate([front * cosine + behind * sine, behind * cosine - front * sine], axis=0)


def attention_forward_body(
    info_ref,
    own_ref,
    other_ref,
    start_ref,
    pieces_own_ref,
    pieces_other_ref,
    gain_ref,
    cosine_ref,
    sine_ref,
    residual_ref,
    query_ref,
    key_ref,
    value_ref,
    mixed_ref,
    total_ref,
    weight_ref,
    out_weight_ref,
    out_rows,
    key_rows,
    x_across,
):
    @pl.when(pl.program_id(0) == 0)
    def _():
        chunks, rows, _ = pieces_own_ref.shape
        for chunk in range(2 * chunks):
            index = info_ref[1 + chunk]
            is_own = index < chunks
            index = jnp.where(is_own, index, index - chunks)
            part = jnp.where(is_own, pieces_own_ref[index], pieces_other_ref[index])
            low = chunk * rows
            if low < QKV:
                weight_ref[low : low + rows] = part
            else:
                out_weight_ref[low - QKV : low - QKV + rows] = part
        out_rows[...] = out_weight_ref[...].T

    x = joined(own_ref[0], other_ref[0], info_ref[0])
    length = x.shape[1]
    x_across[...] = x
    x = x.astype(F32)
    normed = (x * inverse_root(x) * gain_ref[:, 0:1]).astype(BF16)
    cosine = cosine_ref[...]
    sine = sine_ref[...]
    projected = dot(weight_ref[...], normed)
    for head in range(HEADS):
        rows = slice(head * 64, head * 64 + 64)
        query_ref[0, rows] = (turn(projected[rows], cosine, sine) * HEAD_DIM ** (-0.5)).astype(
            BF16
        )
    for head in range(KV_HEADS):
        rows = slice(head * 64, head * 64 + 64)
        rotated = turn(projected[D + head * 64 : D + head * 64 + 64], cosine, sine)
        key_ref[0, rows] = rotated.astype(BF16)
        key_rows[head] = rotated.T.astype(BF16)
    value_ref[0] = projected[D + KV_WIDTH :].astype(BF16)

    def score(member, block, r):
        low, high = block * BLOCK, (block + 1) * BLOCK
        row = (member * RATIO + r) * 64
        return dot(key_rows[member, 0:high], query_ref[0, row : row + 64, low:high])

    def finish(member, block, r, scores):
        low, high = block * BLOCK, (block + 1) * BLOCK
        start_row = start_ref[0, 0:1, low:high]
        place_row = lax.broadcasted_iota(jnp.int32, (1, BLOCK), 1) + low
        scores = [
            visible_scores(scores[k : k + BLOCK], start_row, place_row, low, k)
            for k in range(0, high, BLOCK)
        ]
        top = functools.reduce(
            jnp.maximum, [jnp.max(part, axis=0, keepdims=True) for part in scores]
        )
        exponents = [jnp.exp(part - top) for part in scores]
        total = sum(jnp.sum(part, axis=0, keepdims=True) for part in exponents)
        exponent = jnp.concatenate([part.astype(BF16) for part in exponents], axis=0)
        mixed = dot(value_ref[0, member * 64 : member * 64 + 64, 0:high], exponent)
        row = (member * RATIO + r) * 64
        mixed_ref[0, row : row + 64, low:high] = (mixed * (1.0 / total)).astype(BF16)
        total_ref[0, member, r : r + 1, low:high] = top + jnp.log(total)

    items = [
        (member, block, r)
        for member in range(KV_HEADS)
        for block in range(length // BLOCK)
        for r in range(RATIO)
    ]
    ahead = [score(*item) for item in items[:2]]
    for i, item in enumerate(items):
        if i + 2 < len(items):
            ahead.append(score(*items[i + 2]))
        finish(*item, ahead.pop(0))
    residual_ref[0] = x_across[...].astype(F32) + dot(out_rows[...], mixed_ref[0])


def whole(shape):
    return pl.BlockSpec(
        tuple(shape), lambda *_: (0,) * len(shape), pipeline_mode=pl.Buffered(1)
    )


def step_spec(shape):
    return pl.BlockSpec((1,) + tuple(shape[1:]), lambda i, info: (i,) + (0,) * (len(shape) - 1))


def params():
    return pltpu.CompilerParams(dimension_semantics=("arbitrary",), vmem_limit_bytes=VMEM_LIMIT)


def attention_forward(info, own, other, start, pieces_own, pieces_other, gain, tables):
    count = other.shape[0]
    length = 2 * other.shape[2]
    outs = [
        ((count, D, length), F32),
        ((count, D, length), BF16),
        ((count, KV_WIDTH, length), BF16),
        ((count, KV_WIDTH, length), BF16),
        ((count, D, length), BF16),
        ((count, KV_HEADS, 8, length), F32),
    ]
    weights = (QKV, D), (D, D)
    return pl.pallas_call(
        attention_forward_body,
        grid_spec=pltpu.PrefetchScalarGridSpec(
            num_scalar_prefetch=1,
            grid=(count,),
            in_specs=[
                pl.BlockSpec(
                    (1,) + own.shape[1:], lambda i, info: (info[0] * count + i, 0, 0)
                ),
                step_spec(other.shape),
                step_spec(start.shape),
                whole(pieces_own.shape),
                whole(pieces_other.shape),
                whole(gain.shape),
                whole((HALF, length)),
                whole((HALF, length)),
            ],
            out_specs=[step_spec(shape) for shape, _ in outs] + [whole(shape) for shape in weights],
            scratch_shapes=[
                pltpu.VMEM((D, D), BF16),
                pltpu.VMEM((KV_HEADS, length, HEAD_DIM), BF16),
                pltpu.VMEM((D, length), BF16),
            ],
        ),
        out_shape=[jax.ShapeDtypeStruct(shape, kind) for shape, kind in outs]
        + [jax.ShapeDtypeStruct(shape, BF16) for shape in weights],
        compiler_params=params(),
        cost_estimate=pl.CostEstimate(
            flops=8_000_000_000, transcendentals=12_000_000, bytes_accessed=20_000_000
        ),
        name="attention_forward",
    )(info, own, other, start, pieces_own, pieces_other, gain, *tables)


def stacked(refs, kinds):
    parts = [ref[:, kind].reshape(-1, D) for kind in kinds for ref in refs]
    return jnp.concatenate(parts, axis=0) if len(parts) > 1 else parts[0]


def feed_body(part_count, info_ref, residual_ref, cotangent_own_ref, cotangent_other_ref, *refs):
    weight_refs = refs[:part_count], refs[part_count : 2 * part_count]
    (
        gain_ref,
        out_own_ref,
        out_other_ref,
        back_ref,
        gain_grad_ref,
        grad_own_ref,
        grad_other_ref,
        sums,
        gain_sums,
    ) = refs[2 * part_count :]
    step = pl.program_id(0)
    units = sums.shape[2] // 3
    residual = residual_ref[0]
    cotangent = jnp.where(step % 2 == 0, cotangent_own_ref[0], cotangent_other_ref[0])
    gain = gain_ref[:, 1:2]
    inverse = inverse_root(residual)
    normal = residual * inverse
    normed = (normal * gain).astype(BF16)

    @pl.when(step == 0)
    def _():
        sums[...] = jnp.zeros_like(sums)
        gain_sums[...] = jnp.zeros_like(gain_sums)

    out = residual
    grad_normed = jnp.zeros_like(residual)
    for part, parts in enumerate(weight_refs):
        pair = stacked(parts, (0, 1))
        down = stacked(parts, (2,))
        both = dot(pair, normed)
        gate, upward = both[:units], both[units:]
        grad_hidden = dot(down, cotangent)
        sigmoid_gate = jax.nn.sigmoid(gate)
        swish = gate * sigmoid_gate
        hidden = (swish * upward).astype(BF16)
        grad_gate = (
            grad_hidden * upward * (sigmoid_gate + swish * (1.0 - sigmoid_gate))
        ).astype(BF16)
        grad_upward = (grad_hidden * swish).astype(BF16)
        grads = jnp.concatenate([grad_gate, grad_upward], axis=0)
        out = out + dot(down, hidden, 0, 0)
        grad_normed = grad_normed + dot(pair, grads, 0, 0)
        sums[part, :, : 2 * units] += dot(normed, grads, 1, 1)
        sums[part, :, 2 * units :] += dot(cotangent, hidden, 1, 1)

    out = out.astype(BF16)

    @pl.when(step % 2 == 0)
    def _():
        out_own_ref[0] = out

    @pl.when(step % 2 == 1)
    def _():
        out_other_ref[0] = out

    gain_sums[...] += lane_sums(grad_normed * normal)
    back_ref[0] = (
        cotangent.astype(F32) + norm_backward(grad_normed, normal, inverse, gain)
    ).astype(BF16)

    @pl.when(step == pl.num_programs(0) - 1)
    def _():
        pieces, kinds, rows, _ = grad_own_ref.shape
        for part, grad_ref in enumerate((grad_own_ref, grad_other_ref)):
            for kind in range(kinds):
                flipped = sums[part, :, kind * units : (kind + 1) * units].astype(BF16).T
                for piece in range(pieces):
                    grad_ref[piece, kind] = flipped[piece * rows : (piece + 1) * rows]
        gain_grad_ref[...] = jnp.sum(gain_sums[...].T, axis=0, keepdims=True)


def feed_forward(info, residual, cotangent_own, cotangent_other, weights, gain, pieces):
    count, _, length = residual.shape
    half = length // 2
    part_count = len(weights) // 2
    units = sum(part.size // (3 * D) for part in weights[:part_count])
    block = (1, D, half)
    full = pl.BlockSpec(block, lambda i, info: (i // 2, 0, (i + info[0]) % 2))
    own = pl.BlockSpec(block, lambda i, info: (info[0] * count + i // 2, 0, 0))
    other = pl.BlockSpec(block, lambda i, info: (i // 2, 0, 0))
    grad_shape = (pieces, 3, units // pieces, D)
    return pl.pallas_call(
        functools.partial(feed_body, part_count),
        grid_spec=pltpu.PrefetchScalarGridSpec(
            num_scalar_prefetch=1,
            grid=(2 * count,),
            in_specs=[full, own, other]
            + [whole(weight.shape) for weight in weights]
            + [whole(gain.shape)],
            out_specs=[own, other, full, whole((1, D))] + [whole(grad_shape)] * 2,
            scratch_shapes=[
                pltpu.VMEM((2, D, 3 * units), F32),
                pltpu.VMEM((D, 128), F32),
            ],
        ),
        out_shape=[
            jax.ShapeDtypeStruct(cotangent_own.shape, BF16),
            jax.ShapeDtypeStruct(cotangent_other.shape, BF16),
            jax.ShapeDtypeStruct(residual.shape, BF16),
            jax.ShapeDtypeStruct((1, D), F32),
        ]
        + [jax.ShapeDtypeStruct(grad_shape, BF16)] * 2,
        compiler_params=params(),
        cost_estimate=pl.CostEstimate(
            flops=32_000_000_000, transcendentals=6_000_000, bytes_accessed=30_000_000
        ),
        name="feed_forward",
    )(info, residual, cotangent_own, cotangent_other, *weights, gain)


def branch_backward_body(
    grad_ref, mixed_ref, weight_ref, grad_mixed_ref, inner_ref, weight_grad_ref
):
    @pl.when(pl.program_id(0) == 0)
    def _():
        weight_grad_ref[...] = jnp.zeros_like(weight_grad_ref)

    branch = grad_ref[0]
    grad_mixed = dot(weight_ref[...], branch).astype(BF16)
    grad_mixed_ref[0] = grad_mixed
    for head in range(HEADS):
        rows = slice(head * 64, head * 64 + 64)
        inner_ref[0, head // RATIO, head % RATIO : head % RATIO + 1] = jnp.sum(
            grad_mixed[rows].astype(F32) * mixed_ref[0, rows].astype(F32), axis=0, keepdims=True
        )
    weight_grad_ref[...] += dot(mixed_ref[0], branch, 1, 1)


def branch_backward(grad, mixed, weight):
    count, _, length = grad.shape

    half = length // 2
    step = pl.BlockSpec((1, D, half), lambda i: (i // 2, 0, i % 2))
    inner = (count, KV_HEADS, 8, length)
    return pl.pallas_call(
        branch_backward_body,
        grid=(2 * count,),
        in_specs=[step, step, whole(weight.shape)],
        out_specs=[
            step,
            pl.BlockSpec((1, KV_HEADS, 8, half), lambda i: (i // 2, 0, 0, i % 2)),
            whole((D, D)),
        ],
        out_shape=[
            jax.ShapeDtypeStruct(mixed.shape, BF16),
            jax.ShapeDtypeStruct(inner, F32),
            jax.ShapeDtypeStruct((D, D), F32),
        ],
        compiler_params=params(),
        cost_estimate=SHORT,
        name="branch_backward",
    )(grad, mixed, weight)


def attention_backward_body(
    info_ref,
    own_ref,
    other_ref,
    start_ref,
    gain_ref,
    gain_row_ref,
    weight_ref,
    out_grad_ref,
    gain_second_ref,
    cosine_ref,
    sine_ref,
    query_ref,
    key_ref,
    value_ref,
    total_ref,
    grad_ref,
    inner_ref,
    projected_ref,
    kept_ref,
    sent_ref,
    key_rows,
    value_rows,
    grad_key,
    grad_value,
    weight_sums,
):
    step = pl.program_id(0)
    length = query_ref.shape[2]
    cosine = cosine_ref[...]
    sine = sine_ref[...]
    for head in range(KV_HEADS):
        rows = slice(head * 64, head * 64 + 64)
        key_rows[head] = key_ref[0, rows].T
        value_rows[head] = value_ref[0, rows].T

    def head_rows(member, r):
        return slice((member * RATIO + r) * 64, (member * RATIO + r) * 64 + 64)

    def products(member, low, key_low, r):
        keys = slice(key_low, key_low + 256)
        rows = head_rows(member, r)
        return (
            dot(key_rows[member, keys], query_ref[0, rows, low : low + BLOCK]),
            dot(value_rows[member, keys], grad_ref[0, rows, low : low + BLOCK]),
        )

    def weighted(member, low, key_low, r, scores, grad_weights):
        lanes = slice(low, low + BLOCK)
        start_row = start_ref[0, 0:1, lanes]
        place_row = lax.broadcasted_iota(jnp.int32, (1, BLOCK), 1) + low
        scores = visible_scores(scores, start_row, place_row, low, key_low)
        weights = jnp.exp(scores - total_ref[0, member, r : r + 1, lanes])
        grad_scores = weights * (grad_weights - inner_ref[0, member, r : r + 1, lanes])
        return weights.astype(BF16), grad_scores.astype(BF16)

    items = [
        (member, low, key_low, r)
        for member in range(KV_HEADS)
        for low in range(0, length, BLOCK)
        for key_low in range(0, low + BLOCK, 256)
        for r in range(RATIO)
    ]
    ahead = [products(*item) for item in items[:2]]
    sums = {}

    def add(key, value):
        sums[key] = sums[key] + value if key in sums else value

    for i, item in enumerate(items):
        member, low, key_low, r = item
        if i + 2 < len(items):
            ahead.append(products(*items[i + 2]))
        weights, grad_scores = weighted(*item, *ahead.pop(0))
        rows = head_rows(member, r)
        keys = slice(key_low, key_low + 256)
        add("value", dot(grad_ref[0, rows, low : low + BLOCK], weights, 1, 1))
        add("key", dot(query_ref[0, rows, low : low + BLOCK], grad_scores, 1, 1))
        add(r, dot(key_ref[0, member * 64 : member * 64 + 64, keys], grad_scores))
        if r == RATIO - 1:
            for name, ref in (("value", grad_value), ("key", grad_key)):
                part = sums.pop(name)
                if key_low - key_low % BLOCK == low:
                    ref[member, :, keys] = part
                else:
                    ref[member, :, keys] += part
        if key_low + 256 == low + BLOCK:
            projected_ref[0, rows, low : low + BLOCK] = turn_back(
                sums.pop(r) * HEAD_DIM ** (-0.5),
                cosine[:, low : low + BLOCK],
                sine[:, low : low + BLOCK],
            ).astype(BF16)
    for member in range(KV_HEADS):
        row = D + member * 64
        projected_ref[0, row : row + 64] = turn_back(grad_key[member], cosine, sine).astype(BF16)
        row += KV_WIDTH
        projected_ref[0, row : row + 64] = grad_value[member].astype(BF16)

    x = joined(own_ref[0], other_ref[0], info_ref[0]).astype(F32)
    normed = (x * inverse_root(x) * gain_ref[:, 0:1]).astype(BF16)
    product = dot(projected_ref[0], normed, 1, 1)

    @pl.when(step == 0)
    def _():
        weight_sums[...] = product

    @pl.when(step > 0)
    def _():
        weight_sums[...] += product

    @pl.when(step == pl.num_programs(0) - 1)
    def _():
        rows = 48
        pairs = (QKV + D) // (2 * rows)
        first = info_ref[0] == 0
        gain_sums = jnp.zeros((rows, D), F32)
        for pair in range(pairs):
            low = pair * 2 * rows
            if low < QKV:
                even, odd = weight_sums[low : low + rows], weight_sums[low + rows : low + 2 * rows]
                gain_sums = gain_sums + even * weight_ref[low : low + rows].astype(F32)
                gain_sums = gain_sums + odd * weight_ref[low + rows : low + 2 * rows].astype(F32)
            else:
                low -= QKV
                even = out_grad_ref[low : low + rows]
                odd = out_grad_ref[low + rows : low + 2 * rows]
            even, odd = even.astype(BF16), odd.astype(BF16)
            piece = info_ref[1 + 2 * pairs + pair]
            target = pl.ds(pl.multiple_of(info_ref[1 + 3 * pairs + pair], 16), rows)
            kept_ref[piece, target] = jnp.where(first, even, odd)
            sent_ref[piece, target] = jnp.where(first, odd, even)
        gain_first = jnp.sum(gain_sums, axis=0, keepdims=True) / gain_row_ref[0:1]
        tail = jnp.concatenate(
            [gain_first, gain_second_ref[...], jnp.zeros((14, D), F32)], axis=0
        ).astype(BF16)
        pieces, held, _ = kept_ref.shape
        for piece in range(pieces):
            kept_ref[piece, held - 16 :] = tail
            sent_ref[piece, held - 16 :] = tail


def attention_backward(
    info, own, other, start, gain, gain_rows, weight, out_grad, gain_second, tables, parts, pieces
):
    count = other.shape[0]
    length = 2 * other.shape[2]
    held = (pieces, (QKV + D) // (2 * pieces) + 16, D)
    projected = (count, QKV, length)
    fixed = [gain, gain_rows, weight, out_grad, gain_second, *tables]
    return pl.pallas_call(
        attention_backward_body,
        grid_spec=pltpu.PrefetchScalarGridSpec(
            num_scalar_prefetch=1,
            grid=(count,),
            in_specs=[
                pl.BlockSpec(
                    (1,) + own.shape[1:], lambda i, info: (info[0] * count + i, 0, 0)
                ),
                step_spec(other.shape),
                step_spec(start.shape),
            ]
            + [whole(part.shape) for part in fixed]
            + [step_spec(part.shape) for part in parts],
            out_specs=[step_spec(projected)] + [whole(held)] * 2,
            scratch_shapes=[
                pltpu.VMEM((KV_HEADS, length, HEAD_DIM), BF16),
                pltpu.VMEM((KV_HEADS, length, HEAD_DIM), BF16),
                pltpu.VMEM((KV_HEADS, HEAD_DIM, length), F32),
                pltpu.VMEM((KV_HEADS, HEAD_DIM, length), F32),
                pltpu.VMEM((QKV, D), F32),
            ],
        ),
        out_shape=[jax.ShapeDtypeStruct(projected, BF16)]
        + [jax.ShapeDtypeStruct(held, BF16)] * 2,
        compiler_params=params(),
        cost_estimate=pl.CostEstimate(
            flops=9_000_000_000, transcendentals=6_000_000, bytes_accessed=15_000_000
        ),
        name="attention_backward",
    )(info, own, other, start, *fixed, *parts)


def input_grads_body(
    info_ref,
    own_ref,
    other_ref,
    gain_ref,
    projected_ref,
    weight_ref,
    grad_ref,
    tokens_own_ref,
    tokens_other_ref,
):
    step = pl.program_id(0)
    x = jnp.where(step % 2 == 0, own_ref[0], other_ref[0]).astype(F32)
    gain = gain_ref[:, 0:1]
    inverse = inverse_root(x)
    normal = x * inverse
    grad_normed = dot(weight_ref[...], projected_ref[0], 0, 0)
    grad_x = grad_ref[0].astype(F32) + norm_backward(grad_normed, normal, inverse, gain)

    @pl.when(step % 2 == 0)
    def _():
        tokens_own_ref[0] = grad_x

    @pl.when(step % 2 == 1)
    def _():
        tokens_other_ref[0] = grad_x.astype(BF16)


def input_grads(info, own, other, gain, projected, weight, grad):
    count = other.shape[0]
    half = other.shape[2]
    own_spec = pl.BlockSpec((1, D, half), lambda i, info: (info[0] * count + i // 2, 0, 0))
    other_spec = pl.BlockSpec((1, D, half), lambda i, info: (i // 2, 0, 0))

    def full(height):
        return pl.BlockSpec((1, height, half), lambda i, info: (i // 2, 0, (i + info[0]) % 2))

    return pl.pallas_call(
        input_grads_body,
        grid_spec=pltpu.PrefetchScalarGridSpec(
            num_scalar_prefetch=1,
            grid=(2 * count,),
            in_specs=[
                own_spec,
                other_spec,
                whole(gain.shape),
                full(QKV),
                whole(weight.shape),
                full(D),
            ],
            out_specs=[own_spec, other_spec],
        ),
        out_shape=[
            jax.ShapeDtypeStruct(own.shape, F32),
            jax.ShapeDtypeStruct(other.shape, BF16),
        ],
        compiler_params=params(),
        cost_estimate=SHORT,
        name="input_grads",
    )(info, own, other, gain, projected, weight, grad)


def factors(count):
    inner = 1 << ((count.bit_length() - 1) // 2)
    return count // inner, inner


def partner(values, mask):
    count = lax.axis_size("wide")
    return lax.ppermute(values, "wide", [(i, i ^ mask) for i in range(count)])


def across(values):
    return lax.ppermute(values, "narrow", [(0, 1), (1, 0)])


def in_order(parts, place):
    bit = 1
    while bit < len(parts):
        swap = (place & bit) != 0
        parts = [jnp.where(swap, parts[i ^ bit], part) for i, part in enumerate(parts)]
        bit *= 2
    return parts


def add_all(parts):
    parts = [part.astype(F32) for part in parts]
    while len(parts) > 1:
        parts = [parts[i] + parts[i + 1] for i in range(0, len(parts), 2)]
    return parts[0]


def adamw_update(master, first_state, second_state, gradient, factor, step_rate, decay_rate):
    clipped = gradient * factor
    first_new = beta_first * first_state + (1.0 - beta_first) * clipped
    second_new = beta_second * second_state + (1.0 - beta_second) * clipped * clipped
    first_hat = first_new / (1.0 - beta_first**STEP)
    second_hat = second_new / (1.0 - beta_second**STEP)
    master_new = master * (1.0 - step_rate * decay_rate) - step_rate * first_hat / (
        jnp.sqrt(second_hat) + adam_epsilon
    )
    return (master_new, first_new, second_new)


def to_all(row):
    devices = lax.axis_size("wide") * lax.axis_size("narrow")
    sent = jnp.broadcast_to(row, (devices, row.shape[1]))
    return lax.all_to_all(sent, ("wide", "narrow"), 0, 0, tiled=True)


def sum_everywhere(value):
    return jnp.sum(to_all(jnp.full((1, 128), value, F32))[:, 0])


def per_device(
    tokens,
    cotangent,
    documents,
    attention_master,
    attention_first,
    attention_second,
    feedforward_master,
    feedforward_first,
    feedforward_second,
    gain_master,
    gain_first,
    gain_second,
):
    seq_count, half_len, _ = tokens.shape
    own_count = seq_count // 2
    place = lax.axis_index("narrow")
    first = place == 0
    outer, inner = factors(lax.axis_size("wide"))
    wide_place = lax.axis_index("wide")
    outer_place, inner_place = wide_place // inner, wide_place % inner
    tables = rotary_tables(2 * half_len)
    gain_columns = gain_master.T
    x_own = jnp.swapaxes(tokens, 1, 2)
    cotangent_own = jnp.swapaxes(cotangent, 1, 2)

    def swap(tensor):
        return across(jnp.where(first, tensor[own_count:], tensor[:own_count]))

    rows = attention_master.shape[0]
    aligned = rows % 16 == 0
    piece = attention_master.astype(BF16)
    parts = [piece] + [partner(piece, k * inner) for k in range(1, outer)]
    stack = jnp.stack(parts if aligned else in_order(parts, outer_place))
    parts = [stack] + [partner(stack, k) for k in range(1, inner)]
    feed_piece = feedforward_master.astype(BF16)
    feed_outer = jnp.stack(
        [feed_piece] + [partner(feed_piece, k * inner) for k in range(1, outer)]
    )
    feed_outer, parts[1:] = lax.optimization_barrier((feed_outer, parts[1:]))
    feed_parts = [feed_outer] + [partner(feed_outer, k) for k in range(1, inner)]
    if aligned:
        stack = jnp.stack(parts)
        pieces_own = stack.reshape(-1, rows, D)
        pieces_other = across(stack).reshape(-1, rows, D)
        chunk = jnp.arange(2 * inner * outer, dtype=jnp.int32)
        order = (
            ((chunk % 2) ^ place) * inner + ((chunk // 2 % inner) ^ inner_place)
        ) * outer + ((chunk // (2 * inner)) ^ outer_place)
        pair = chunk[: inner * outer]
        piece_of = (pair % inner) ^ inner_place
        row_of = ((pair // inner) ^ outer_place) * rows
        grad_pieces = inner
    else:
        stack = jnp.stack(in_order(parts, inner_place), axis=1)
        pieces = jnp.stack(in_order([stack, across(stack)], place), axis=2).reshape(-1, 48, D)
        pieces_own, pieces_other = pieces[:16], pieces[16:]
        order = jnp.arange(32, dtype=jnp.int32)
        piece_of = jnp.zeros((16,), jnp.int32)
        row_of = jnp.arange(16, dtype=jnp.int32) * 48
        grad_pieces = 1
    info = jnp.concatenate(
        [jnp.full((1,), place), order, piece_of, row_of]
    ).astype(jnp.int32)

    x_other = swap(x_own)
    own_docs = lax.dynamic_slice_in_dim(documents, place * own_count, own_count, 0)
    start = jnp.zeros_like(own_docs)
    for number in (1, 2):
        before = jnp.sum((own_docs < number).astype(jnp.int32), axis=1, keepdims=True)
        start = jnp.where(own_docs == number, before, start)
    start = start[:, None, :]

    cotangent_other = swap(cotangent_own)

    residual, query, key, value, mixed, total, weight_qkv, weight_out = attention_forward(
        info, x_own, x_other, start, pieces_own, pieces_other, gain_columns, tables
    )
    feed_parts, residual = lax.optimization_barrier((feed_parts, residual))
    if aligned:
        feed_weights = feed_parts + [across(part) for part in feed_parts]
    else:
        stack = jnp.stack(feed_parts)
        feed_weights = [
            jnp.swapaxes(part.reshape(-1, 3, rows, D), 0, 1).reshape(1, 3, -1, D)
            for part in (stack, across(stack))
        ]
    outputs, out_other, back, gain_second_part, own_grad, other_grad = feed_forward(
        info, residual, cotangent_own, cotangent_other, feed_weights, gain_columns, inner
    )

    def place_other(whole_array, received):
        return lax.dynamic_update_slice_in_dim(
            whole_array, received.astype(whole_array.dtype), (1 - place) * own_count, 0
        )

    out_received = across(out_other)

    received = across(other_grad)
    grad_mixed, inner_sums, out_grad = branch_backward(back, mixed, weight_out)
    received, own_grad, grad_mixed = lax.optimization_barrier((received, own_grad, grad_mixed))
    feed_sums = [add_all([own_grad[k], received[k]]).astype(BF16) for k in range(inner)]
    feed_sums, grad_mixed = lax.optimization_barrier((feed_sums, grad_mixed))
    feed_got = [feed_sums[0]] + [partner(feed_sums[k], k) for k in range(1, inner)]
    projected, kept, sent = attention_backward(
        info,
        x_own,
        x_other,
        start,
        gain_columns,
        gain_master,
        weight_qkv,
        out_grad,
        gain_second_part,
        tables,
        [query, key, value, total, grad_mixed, inner_sums],
        grad_pieces,
    )
    feed_got, kept, sent = lax.optimization_barrier((feed_got, kept, sent))
    summed = add_all(feed_got).astype(BF16).reshape(3, outer, -1, D)
    feed_last = [summed[:, k] for k in range(outer)]
    feed_last, sent = lax.optimization_barrier((feed_last, sent))
    feed_last = [feed_last[0]] + [partner(feed_last[k], k * inner) for k in range(1, outer)]

    received = across(sent)
    if aligned:
        parts = [add_all([kept[k], received[k]]).astype(BF16) for k in range(inner)]
    else:
        gain_grad = lax.psum(kept[0, -16:-14].astype(F32), ("wide", "narrow"))
        total = add_all([kept, received]).astype(BF16)[0, :-16].reshape(outer, inner, rows, D)
        parts = in_order([total[:, k] for k in range(inner)], inner_place)
    parts, projected = lax.optimization_barrier((parts, projected))
    got = [parts[0]] + [partner(parts[k], k) for k in range(1, inner)]
    grad_own, grad_other = input_grads(
        info, x_own, x_other, gain_columns, projected, weight_qkv, back
    )
    got, feed_last, grad_other = lax.optimization_barrier((got, feed_last, grad_other))
    total = add_all(got).astype(BF16)
    if aligned:
        tail = total[outer * rows :]
        parts = [
            jnp.concatenate([total[k * rows : (k + 1) * rows], tail], axis=0)
            for k in range(outer)
        ]
    else:
        parts = in_order([total[k] for k in range(outer)], outer_place)
    attention_grad = add_all(
        [parts[0]] + [partner(parts[k], k * inner) for k in range(1, outer)]
    )
    if aligned:
        attention_grad, gain_grad = attention_grad[:rows], attention_grad[rows : rows + 2]
    feedforward_grad = add_all(feed_last)
    grad_received = across(grad_other)
    attention_grad, gain_grad, grad_received, out_received = lax.optimization_barrier(
        (attention_grad, gain_grad, grad_received, out_received)
    )
    grad_tokens = place_other(grad_own, grad_received)
    outputs = place_other(outputs, out_received)
    local_squares = jnp.sum(attention_grad * attention_grad) + jnp.sum(
        feedforward_grad * feedforward_grad
    )
    grad_norm = jnp.sqrt(sum_everywhere(local_squares) + jnp.sum(gain_grad * gain_grad))
    factor = jnp.minimum(1.0, clip_limit / (grad_norm + 1e-06))
    update = functools.partial(adamw_update, factor=factor)
    attention_new = update(
        attention_master,
        attention_first,
        attention_second,
        attention_grad,
        step_rate=rate_matrix,
        decay_rate=weight_decay,
    )
    feedforward_new = update(
        feedforward_master,
        feedforward_first,
        feedforward_second,
        feedforward_grad,
        step_rate=rate_matrix,
        decay_rate=weight_decay,
    )
    gain_new = update(
        gain_master, gain_first, gain_second, gain_grad, step_rate=rate_gain, decay_rate=0.0
    )
    outputs = jnp.swapaxes(outputs, 1, 2)
    grad_tokens = jnp.swapaxes(grad_tokens, 1, 2)
    return (outputs, grad_tokens, grad_norm, *attention_new, *feedforward_new, *gain_new)


def solution(mesh):
    sequences = P("wide", "narrow", None)
    attention = P(("wide", "narrow"), None)
    feedforward = P(None, ("narrow", "wide"), None)
    state = (attention,) * 3 + (feedforward,) * 3 + (P(),) * 3
    return jax.shard_map(
        per_device,
        mesh=mesh,
        in_specs=(sequences, sequences, P("wide", None)) + state,
        out_specs=(sequences, sequences, P()) + state,
        check_vma=False,
    )
```

```python
import functools

import jax
import jax.numpy as jnp
import numpy as np
from jax import lax
from jax.experimental import pallas as pl
from jax.experimental.pallas import tpu as pltpu
from jax.sharding import PartitionSpec as P

D = 576
HEADS = 9
KV_HEADS = 3
RATIO = 3
HEAD_DIM = 64
HALF = 32
STEP = 10
KV_WIDTH = 192
QKV = 960
BLOCK = 256

norm_epsilon = 1e-05
adam_epsilon = 1e-08
beta_first = 0.9
beta_second = 0.999
weight_decay = 0.1
rate_matrix = 0.05
rate_gain = 0.5
clip_limit = 1.0
rotary_base = 10000.0
masked_value = -1e30

F32 = jnp.float32
BF16 = jnp.bfloat16
VMEM_LIMIT = 60 * 2**20
SHORT = pl.CostEstimate(flops=1_000_000, transcendentals=0, bytes_accessed=100_000)


def rotary_tables(length):
    frequency = np.float32(rotary_base) ** (
        np.float32(-2.0) * np.arange(HALF, dtype=np.float32) / np.float32(HEAD_DIM)
    )
    angles = np.arange(length, dtype=np.float32)[None, :] * frequency.astype(np.float32)[:, None]
    return jnp.asarray(np.cos(angles), F32), jnp.asarray(np.sin(angles), F32)


def dot(left, right, left_dim=1, right_dim=0):
    return lax.dot_general(
        left, right, (((left_dim,), (right_dim,)), ((), ())), preferred_element_type=F32
    )


def inverse_root(values):
    return lax.rsqrt(jnp.mean(values * values, axis=0, keepdims=True) + norm_epsilon)


def joined(own, other, place):
    first = place == 0
    return jnp.concatenate(
        [jnp.where(first, own, other), jnp.where(first, other, own)], axis=1
    )


def lane_sums(values):
    lanes = 128
    total = values[:, :lanes]
    for low in range(lanes, values.shape[1], lanes):
        total = total + values[:, low : low + lanes]
    return total


def norm_backward(grad_normed, normal, inverse, gain):
    scaled = grad_normed * gain
    return inverse * (scaled - normal * jnp.mean(scaled * normal, axis=0, keepdims=True))


def visible_scores(scores, start_row, place_row, low, key_low):
    inside = low >= 256 and low + BLOCK <= 768 and key_low >= 256
    if inside and key_low < low:
        return scores
    place = lax.broadcasted_iota(jnp.int32, scores.shape, 0) + key_low
    if inside:
        seen = place <= place_row
    else:
        seen = place >= start_row
        if key_low >= low:
            seen = seen & (place <= place_row)
    return jnp.where(seen, scores, masked_value)


def triple(row):
    return jnp.concatenate([row] * RATIO, axis=1)


def turn(rows, cosine, sine):
    front, behind = rows[:HALF], rows[HALF:]
    return jnp.concatenate([front * cosine - behind * sine, behind * cosine + front * sine], axis=0)


def turn_back(rows, cosine, sine):
    front, behind = rows[:HALF], rows[HALF:]
    return jnp.concatenate([front * cosine + behind * sine, behind * cosine - front * sine], axis=0)


def attention_forward_body(
    info_ref,
    own_ref,
    other_ref,
    start_ref,
    pieces_own_ref,
    pieces_other_ref,
    gain_ref,
    cosine_ref,
    sine_ref,
    residual_ref,
    query_ref,
    key_ref,
    value_ref,
    mixed_ref,
    total_ref,
    normed_ref,
    weight_ref,
    out_weight_ref,
    out_rows,
    key_rows,
    x_across,
):
    @pl.when(pl.program_id(0) == 0)
    def _():
        chunks, rows, _ = pieces_own_ref.shape
        for chunk in range(2 * chunks):
            index = info_ref[1 + chunk]
            is_own = index < chunks
            index = jnp.where(is_own, index, index - chunks)
            part = jnp.where(is_own, pieces_own_ref[index], pieces_other_ref[index])
            low = chunk * rows
            if low < QKV:
                weight_ref[low : low + rows] = part
            else:
                out_weight_ref[low - QKV : low - QKV + rows] = part
        out_rows[...] = out_weight_ref[...].T

    x = joined(own_ref[0], other_ref[0], info_ref[0])
    length = x.shape[1]
    x_across[...] = x
    x = x.astype(F32)
    normed = (x * inverse_root(x) * gain_ref[:, 0:1]).astype(BF16)
    cosine = cosine_ref[...]
    sine = sine_ref[...]
    normed_ref[0] = normed
    projected = dot(weight_ref[...], normed)
    for head in range(HEADS):
        rows = slice(head * 64, head * 64 + 64)
        query_ref[0, rows] = (turn(projected[rows], cosine, sine) * HEAD_DIM ** (-0.5)).astype(
            BF16
        )
    for head in range(KV_HEADS):
        rows = slice(head * 64, head * 64 + 64)
        rotated = turn(projected[D + head * 64 : D + head * 64 + 64], cosine, sine)
        key_ref[0, rows] = rotated.astype(BF16)
        key_rows[head] = rotated.T.astype(BF16)
    value_ref[0] = projected[D + KV_WIDTH :].astype(BF16)

    def score(member, block, r):
        low, high = block * BLOCK, (block + 1) * BLOCK
        row = (member * RATIO + r) * 64
        return dot(key_rows[member, 0:high], query_ref[0, row : row + 64, low:high])

    def finish(member, block, r, scores):
        low, high = block * BLOCK, (block + 1) * BLOCK
        start_row = start_ref[0, 0:1, low:high]
        place_row = lax.broadcasted_iota(jnp.int32, (1, BLOCK), 1) + low
        scores = [
            visible_scores(scores[k : k + BLOCK], start_row, place_row, low, k)
            for k in range(0, high, BLOCK)
        ]
        top = functools.reduce(
            jnp.maximum, [jnp.max(part, axis=0, keepdims=True) for part in scores]
        )
        exponents = [jnp.exp(part - top) for part in scores]
        total = sum(jnp.sum(part, axis=0, keepdims=True) for part in exponents)
        exponent = jnp.concatenate([part.astype(BF16) for part in exponents], axis=0)
        mixed = dot(value_ref[0, member * 64 : member * 64 + 64, 0:high], exponent)
        row = (member * RATIO + r) * 64
        mixed_ref[0, row : row + 64, low:high] = (mixed * (1.0 / total)).astype(BF16)
        total_ref[0, member, r : r + 1, low:high] = top + jnp.log(total)

    items = [
        (member, block, r)
        for member in range(KV_HEADS)
        for block in range(length // BLOCK)
        for r in range(RATIO)
    ]
    ahead = [score(*item) for item in items[:2]]
    for i, item in enumerate(items):
        if i + 2 < len(items):
            ahead.append(score(*items[i + 2]))
        finish(*item, ahead.pop(0))
    residual_ref[0] = x_across[...].astype(F32) + dot(out_rows[...], mixed_ref[0])


def whole(shape):
    return pl.BlockSpec(
        tuple(shape), lambda *_: (0,) * len(shape), pipeline_mode=pl.Buffered(1)
    )


def step_spec(shape):
    return pl.BlockSpec((1,) + tuple(shape[1:]), lambda i, info: (i,) + (0,) * (len(shape) - 1))


def params():
    return pltpu.CompilerParams(dimension_semantics=("arbitrary",), vmem_limit_bytes=VMEM_LIMIT)


def attention_forward(info, own, other, start, pieces_own, pieces_other, gain, tables):
    count = other.shape[0]
    length = 2 * other.shape[2]
    outs = [
        ((count, D, length), F32),
        ((count, D, length), BF16),
        ((count, KV_WIDTH, length), BF16),
        ((count, KV_WIDTH, length), BF16),
        ((count, D, length), BF16),
        ((count, KV_HEADS, 8, length), F32),
        ((count, D, length), BF16),
    ]
    weights = (QKV, D), (D, D)
    return pl.pallas_call(
        attention_forward_body,
        grid_spec=pltpu.PrefetchScalarGridSpec(
            num_scalar_prefetch=1,
            grid=(count,),
            in_specs=[
                pl.BlockSpec(
                    (1,) + own.shape[1:], lambda i, info: (info[0] * count + i, 0, 0)
                ),
                step_spec(other.shape),
                step_spec(start.shape),
                whole(pieces_own.shape),
                whole(pieces_other.shape),
                whole(gain.shape),
                whole((HALF, length)),
                whole((HALF, length)),
            ],
            out_specs=[step_spec(shape) for shape, _ in outs] + [whole(shape) for shape in weights],
            scratch_shapes=[
                pltpu.VMEM((D, D), BF16),
                pltpu.VMEM((KV_HEADS, length, HEAD_DIM), BF16),
                pltpu.VMEM((D, length), BF16),
            ],
        ),
        out_shape=[jax.ShapeDtypeStruct(shape, kind) for shape, kind in outs]
        + [jax.ShapeDtypeStruct(shape, BF16) for shape in weights],
        compiler_params=params(),
        cost_estimate=pl.CostEstimate(
            flops=8_000_000_000, transcendentals=12_000_000, bytes_accessed=20_000_000
        ),
        name="attention_forward",
    )(info, own, other, start, pieces_own, pieces_other, gain, *tables)


def stacked(refs, kinds):
    parts = [ref[:, kind].reshape(-1, D) for kind in kinds for ref in refs]
    return jnp.concatenate(parts, axis=0) if len(parts) > 1 else parts[0]


def feed_body(part_count, info_ref, residual_ref, cotangent_own_ref, cotangent_other_ref, *refs):
    weight_refs = refs[:part_count], refs[part_count : 2 * part_count]
    (
        gain_ref,
        out_own_ref,
        out_other_ref,
        back_ref,
        gain_grad_ref,
        grad_own_ref,
        grad_other_ref,
        sums,
        gain_sums,
    ) = refs[2 * part_count :]
    step = pl.program_id(0)
    units = sums.shape[2] // 3
    residual = residual_ref[0]
    cotangent = jnp.where(step % 2 == 0, cotangent_own_ref[0], cotangent_other_ref[0])
    gain = gain_ref[:, 1:2]
    inverse = inverse_root(residual)
    normal = residual * inverse
    normed = (normal * gain).astype(BF16)

    @pl.when(step == 0)
    def _():
        sums[...] = jnp.zeros_like(sums)
        gain_sums[...] = jnp.zeros_like(gain_sums)

    out = residual
    grad_normed = jnp.zeros_like(residual)
    for part, parts in enumerate(weight_refs):
        pair = stacked(parts, (0, 1))
        down = stacked(parts, (2,))
        both = dot(pair, normed)
        gate, upward = both[:units], both[units:]
        grad_hidden = dot(down, cotangent)
        sigmoid_gate = jax.nn.sigmoid(gate)
        swish = gate * sigmoid_gate
        hidden = (swish * upward).astype(BF16)
        grad_gate = (
            grad_hidden * upward * (sigmoid_gate + swish * (1.0 - sigmoid_gate))
        ).astype(BF16)
        grad_upward = (grad_hidden * swish).astype(BF16)
        grads = jnp.concatenate([grad_gate, grad_upward], axis=0)
        out = out + dot(down, hidden, 0, 0)
        grad_normed = grad_normed + dot(pair, grads, 0, 0)
        sums[part, :, : 2 * units] += dot(normed, grads, 1, 1)
        sums[part, :, 2 * units :] += dot(cotangent, hidden, 1, 1)

    out = out.astype(BF16)

    @pl.when(step % 2 == 0)
    def _():
        out_own_ref[0] = out

    @pl.when(step % 2 == 1)
    def _():
        out_other_ref[0] = out

    gain_sums[...] += lane_sums(grad_normed * normal)
    back_ref[0] = (
        cotangent.astype(F32) + norm_backward(grad_normed, normal, inverse, gain)
    ).astype(BF16)

    @pl.when(step == pl.num_programs(0) - 1)
    def _():
        pieces, kinds, rows, _ = grad_own_ref.shape
        for part, grad_ref in enumerate((grad_own_ref, grad_other_ref)):
            for kind in range(kinds):
                flipped = sums[part, :, kind * units : (kind + 1) * units].astype(BF16).T
                for piece in range(pieces):
                    grad_ref[piece, kind] = flipped[piece * rows : (piece + 1) * rows]
        gain_grad_ref[...] = jnp.sum(gain_sums[...].T, axis=0, keepdims=True)


def feed_forward(info, residual, cotangent_own, cotangent_other, weights, gain, pieces):
    count, _, length = residual.shape
    half = length // 2
    part_count = len(weights) // 2
    units = sum(part.size // (3 * D) for part in weights[:part_count])
    block = (1, D, half)
    full = pl.BlockSpec(block, lambda i, info: (i // 2, 0, (i + info[0]) % 2))
    own = pl.BlockSpec(block, lambda i, info: (info[0] * count + i // 2, 0, 0))
    other = pl.BlockSpec(block, lambda i, info: (i // 2, 0, 0))
    grad_shape = (pieces, 3, units // pieces, D)
    return pl.pallas_call(
        functools.partial(feed_body, part_count),
        grid_spec=pltpu.PrefetchScalarGridSpec(
            num_scalar_prefetch=1,
            grid=(2 * count,),
            in_specs=[full, own, other]
            + [whole(weight.shape) for weight in weights]
            + [whole(gain.shape)],
            out_specs=[own, other, full, whole((1, D))] + [whole(grad_shape)] * 2,
            scratch_shapes=[
                pltpu.VMEM((2, D, 3 * units), F32),
                pltpu.VMEM((D, 128), F32),
            ],
        ),
        out_shape=[
            jax.ShapeDtypeStruct(cotangent_own.shape, BF16),
            jax.ShapeDtypeStruct(cotangent_other.shape, BF16),
            jax.ShapeDtypeStruct(residual.shape, BF16),
            jax.ShapeDtypeStruct((1, D), F32),
        ]
        + [jax.ShapeDtypeStruct(grad_shape, BF16)] * 2,
        compiler_params=params(),
        cost_estimate=pl.CostEstimate(
            flops=32_000_000_000, transcendentals=6_000_000, bytes_accessed=30_000_000
        ),
        name="feed_forward",
    )(info, residual, cotangent_own, cotangent_other, *weights, gain)


def branch_backward_body(
    grad_ref, mixed_ref, weight_ref, grad_mixed_ref, inner_ref, weight_grad_ref
):
    @pl.when(pl.program_id(0) == 0)
    def _():
        weight_grad_ref[...] = jnp.zeros_like(weight_grad_ref)

    branch = grad_ref[0]
    grad_mixed = dot(weight_ref[...], branch).astype(BF16)
    grad_mixed_ref[0] = grad_mixed
    for head in range(HEADS):
        rows = slice(head * 64, head * 64 + 64)
        inner_ref[0, head // RATIO, head % RATIO : head % RATIO + 1] = jnp.sum(
            grad_mixed[rows].astype(F32) * mixed_ref[0, rows].astype(F32), axis=0, keepdims=True
        )
    weight_grad_ref[...] += dot(mixed_ref[0], branch, 1, 1)


def branch_backward(grad, mixed, weight):
    count, _, length = grad.shape

    half = length // 2
    step = pl.BlockSpec((1, D, half), lambda i: (i // 2, 0, i % 2))
    inner = (count, KV_HEADS, 8, length)
    return pl.pallas_call(
        branch_backward_body,
        grid=(2 * count,),
        in_specs=[step, step, whole(weight.shape)],
        out_specs=[
            step,
            pl.BlockSpec((1, KV_HEADS, 8, half), lambda i: (i // 2, 0, 0, i % 2)),
            whole((D, D)),
        ],
        out_shape=[
            jax.ShapeDtypeStruct(mixed.shape, BF16),
            jax.ShapeDtypeStruct(inner, F32),
            jax.ShapeDtypeStruct((D, D), F32),
        ],
        compiler_params=params(),
        cost_estimate=SHORT,
        name="branch_backward",
    )(grad, mixed, weight)


def attention_backward_body(
    info_ref,
    normed_ref,
    start_ref,
    gain_row_ref,
    weight_hbm,
    out_grad_hbm,
    gain_second_ref,
    cosine_ref,
    sine_ref,
    query_ref,
    key_ref,
    value_ref,
    total_ref,
    grad_ref,
    inner_ref,
    projected_ref,
    kept_ref,
    sent_ref,
    key_rows,
    value_rows,
    grad_key,
    grad_value,
    weight_sums,
    weight_ref,
    out_grad_ref,
    semaphores,
):
    step = pl.program_id(0)
    copies = [
        pltpu.make_async_copy(weight_hbm, weight_ref, semaphores.at[0]),
        pltpu.make_async_copy(out_grad_hbm, out_grad_ref, semaphores.at[1]),
    ]

    @pl.when(step == 0)
    def _():
        for copy in copies:
            copy.start()

    length = query_ref.shape[2]
    cosine = cosine_ref[...]
    sine = sine_ref[...]
    for head in range(KV_HEADS):
        rows = slice(head * 64, head * 64 + 64)
        key_rows[head] = key_ref[0, rows].T
        value_rows[head] = value_ref[0, rows].T

    def head_rows(member, r):
        return slice((member * RATIO + r) * 64, (member * RATIO + r) * 64 + 64)

    def products(member, low, key_low, r):
        keys = slice(key_low, key_low + 256)
        rows = head_rows(member, r)
        return (
            dot(key_rows[member, keys], query_ref[0, rows, low : low + BLOCK]),
            dot(value_rows[member, keys], grad_ref[0, rows, low : low + BLOCK]),
        )

    def weighted(member, low, key_low, r, scores, grad_weights):
        lanes = slice(low, low + BLOCK)
        start_row = start_ref[0, 0:1, lanes]
        place_row = lax.broadcasted_iota(jnp.int32, (1, BLOCK), 1) + low
        scores = visible_scores(scores, start_row, place_row, low, key_low)
        weights = jnp.exp(scores - total_ref[0, member, r : r + 1, lanes])
        grad_scores = weights * (grad_weights - inner_ref[0, member, r : r + 1, lanes])
        return weights.astype(BF16), grad_scores.astype(BF16)

    items = [
        (member, low, key_low, r)
        for member in range(KV_HEADS)
        for low in range(0, length, BLOCK)
        for key_low in range(0, low + BLOCK, 256)
        for r in range(RATIO)
    ]
    ahead = [products(*item) for item in items[:2]]
    sums = {}

    def add(key, value):
        sums[key] = sums[key] + value if key in sums else value

    for i, item in enumerate(items):
        member, low, key_low, r = item
        if i + 2 < len(items):
            ahead.append(products(*items[i + 2]))
        weights, grad_scores = weighted(*item, *ahead.pop(0))
        rows = head_rows(member, r)
        keys = slice(key_low, key_low + 256)
        add("value", dot(grad_ref[0, rows, low : low + BLOCK], weights, 1, 1))
        add("key", dot(query_ref[0, rows, low : low + BLOCK], grad_scores, 1, 1))
        add(r, dot(key_ref[0, member * 64 : member * 64 + 64, keys], grad_scores))
        if r == RATIO - 1:
            for name, ref in (("value", grad_value), ("key", grad_key)):
                part = sums.pop(name)
                if key_low - key_low % BLOCK == low:
                    ref[member, :, keys] = part
                else:
                    ref[member, :, keys] += part
        if key_low + 256 == low + BLOCK:
            projected_ref[0, rows, low : low + BLOCK] = turn_back(
                sums.pop(r) * HEAD_DIM ** (-0.5),
                cosine[:, low : low + BLOCK],
                sine[:, low : low + BLOCK],
            ).astype(BF16)
    for member in range(KV_HEADS):
        row = D + member * 64
        projected_ref[0, row : row + 64] = turn_back(grad_key[member], cosine, sine).astype(BF16)
        row += KV_WIDTH
        projected_ref[0, row : row + 64] = grad_value[member].astype(BF16)

    product = dot(projected_ref[0], normed_ref[0], 1, 1)

    @pl.when(step == 0)
    def _():
        weight_sums[...] = product

    @pl.when(step > 0)
    def _():
        weight_sums[...] += product

    @pl.when(step == pl.num_programs(0) - 1)
    def _():
        for copy in copies:
            copy.wait()
        rows = 48
        pairs = (QKV + D) // (2 * rows)
        first = info_ref[0] == 0
        gain_sums = jnp.zeros((rows, D), F32)
        for pair in range(pairs):
            low = pair * 2 * rows
            if low < QKV:
                even, odd = weight_sums[low : low + rows], weight_sums[low + rows : low + 2 * rows]
                gain_sums = gain_sums + even * weight_ref[low : low + rows].astype(F32)
                gain_sums = gain_sums + odd * weight_ref[low + rows : low + 2 * rows].astype(F32)
            else:
                low -= QKV
                even = out_grad_ref[low : low + rows]
                odd = out_grad_ref[low + rows : low + 2 * rows]
            even, odd = even.astype(BF16), odd.astype(BF16)
            piece = info_ref[1 + 2 * pairs + pair]
            target = pl.ds(pl.multiple_of(info_ref[1 + 3 * pairs + pair], 16), rows)
            kept_ref[piece, target] = jnp.where(first, even, odd)
            sent_ref[piece, target] = jnp.where(first, odd, even)
        gain_first = jnp.sum(gain_sums, axis=0, keepdims=True) / gain_row_ref[0:1]
        tail = jnp.concatenate(
            [gain_first, gain_second_ref[...], jnp.zeros((14, D), F32)], axis=0
        ).astype(BF16)
        pieces, held, _ = kept_ref.shape
        for piece in range(pieces):
            kept_ref[piece, held - 16 :] = tail
            sent_ref[piece, held - 16 :] = tail


def attention_backward(
    info, normed, start, gain_rows, weight, out_grad, gain_second, tables, parts, pieces
):
    count, _, length = normed.shape
    held = (pieces, (QKV + D) // (2 * pieces) + 16, D)
    projected = (count, QKV, length)
    before, after = [gain_rows], [gain_second, *tables]
    return pl.pallas_call(
        attention_backward_body,
        grid_spec=pltpu.PrefetchScalarGridSpec(
            num_scalar_prefetch=1,
            grid=(count,),
            in_specs=[
                step_spec(normed.shape),
                step_spec(start.shape),
            ]
            + [whole(part.shape) for part in before]
            + [pl.BlockSpec(memory_space=pl.ANY)] * 2
            + [whole(part.shape) for part in after]
            + [step_spec(part.shape) for part in parts],
            out_specs=[step_spec(projected)] + [whole(held)] * 2,
            scratch_shapes=[
                pltpu.VMEM((KV_HEADS, length, HEAD_DIM), BF16),
                pltpu.VMEM((KV_HEADS, length, HEAD_DIM), BF16),
                pltpu.VMEM((KV_HEADS, HEAD_DIM, length), F32),
                pltpu.VMEM((KV_HEADS, HEAD_DIM, length), F32),
                pltpu.VMEM((QKV, D), F32),
                pltpu.VMEM(weight.shape, BF16),
                pltpu.VMEM(out_grad.shape, F32),
                pltpu.SemaphoreType.DMA((2,)),
            ],
        ),
        out_shape=[jax.ShapeDtypeStruct(projected, BF16)]
        + [jax.ShapeDtypeStruct(held, BF16)] * 2,
        compiler_params=params(),
        cost_estimate=pl.CostEstimate(
            flops=9_000_000_000, transcendentals=6_000_000, bytes_accessed=15_000_000
        ),
        name="attention_backward",
    )(info, normed, start, *before, weight, out_grad, *after, *parts)


def input_grads_body(
    info_ref,
    own_ref,
    other_ref,
    gain_ref,
    projected_ref,
    weight_ref,
    grad_ref,
    tokens_own_ref,
    tokens_other_ref,
):
    step = pl.program_id(0)
    x = jnp.where(step % 2 == 0, own_ref[0], other_ref[0]).astype(F32)
    gain = gain_ref[:, 0:1]
    inverse = inverse_root(x)
    normal = x * inverse
    grad_normed = dot(weight_ref[...], projected_ref[0], 0, 0)
    grad_x = grad_ref[0].astype(F32) + norm_backward(grad_normed, normal, inverse, gain)

    @pl.when(step % 2 == 0)
    def _():
        tokens_own_ref[0] = grad_x

    @pl.when(step % 2 == 1)
    def _():
        tokens_other_ref[0] = grad_x.astype(BF16)


def input_grads(info, own, other, gain, projected, weight, grad):
    count = other.shape[0]
    half = other.shape[2]
    own_spec = pl.BlockSpec((1, D, half), lambda i, info: (info[0] * count + i // 2, 0, 0))
    other_spec = pl.BlockSpec((1, D, half), lambda i, info: (i // 2, 0, 0))

    def full(height):
        return pl.BlockSpec((1, height, half), lambda i, info: (i // 2, 0, (i + info[0]) % 2))

    return pl.pallas_call(
        input_grads_body,
        grid_spec=pltpu.PrefetchScalarGridSpec(
            num_scalar_prefetch=1,
            grid=(2 * count,),
            in_specs=[
                own_spec,
                other_spec,
                whole(gain.shape),
                full(QKV),
                whole(weight.shape),
                full(D),
            ],
            out_specs=[own_spec, other_spec],
        ),
        out_shape=[
            jax.ShapeDtypeStruct(own.shape, F32),
            jax.ShapeDtypeStruct(other.shape, BF16),
        ],
        compiler_params=params(),
        cost_estimate=SHORT,
        name="input_grads",
    )(info, own, other, gain, projected, weight, grad)


def factors(count):
    inner = 1 << ((count.bit_length() - 1) // 2)
    return count // inner, inner


def partner(values, mask):
    count = lax.axis_size("wide")
    return lax.ppermute(values, "wide", [(i, i ^ mask) for i in range(count)])


def across(values):
    return lax.ppermute(values, "narrow", [(0, 1), (1, 0)])


def in_order(parts, place):
    bit = 1
    while bit < len(parts):
        swap = (place & bit) != 0
        parts = [jnp.where(swap, parts[i ^ bit], part) for i, part in enumerate(parts)]
        bit *= 2
    return parts


def add_all(parts):
    parts = [part.astype(F32) for part in parts]
    while len(parts) > 1:
        parts = [parts[i] + parts[i + 1] for i in range(0, len(parts), 2)]
    return parts[0]


def adamw_update(master, first_state, second_state, gradient, factor, step_rate, decay_rate):
    clipped = gradient * factor
    first_new = beta_first * first_state + (1.0 - beta_first) * clipped
    second_new = beta_second * second_state + (1.0 - beta_second) * clipped * clipped
    first_hat = first_new / (1.0 - beta_first**STEP)
    second_hat = second_new / (1.0 - beta_second**STEP)
    master_new = master * (1.0 - step_rate * decay_rate) - step_rate * first_hat / (
        jnp.sqrt(second_hat) + adam_epsilon
    )
    return (master_new, first_new, second_new)


def squares_body(count, rows, *refs):
    attention_ref, gain_ref, feedforward_ref, sent_ref = refs[2 * count :]
    attention = add_all([ref[...] for ref in refs[:count]])
    feedforward = add_all([ref[...] for ref in refs[count : 2 * count]])
    owned = attention[:rows]
    attention_ref[...] = owned
    if attention.shape[0] > rows:
        gain_ref[...] = attention[rows : rows + 2]
    else:
        gain_ref[...] = jnp.zeros_like(gain_ref)
    feedforward_ref[...] = feedforward
    local = jnp.sum(owned * owned) + jnp.sum(feedforward * feedforward)
    sent_ref[...] = jnp.full(sent_ref.shape, local, F32)


def last_sums(attention, feedforward, rows, devices):
    parts = attention + feedforward
    shapes = [(rows, D), (2, D), feedforward[0].shape, (devices, 1, 128)]
    return pl.pallas_call(
        functools.partial(squares_body, len(attention), rows),
        in_specs=[pl.BlockSpec(memory_space=pltpu.VMEM) for _ in parts],
        out_specs=[pl.BlockSpec(memory_space=pltpu.VMEM) for _ in shapes],
        out_shape=[jax.ShapeDtypeStruct(shape, F32) for shape in shapes],
        cost_estimate=SHORT,
        name="last_sums",
    )(*parts)


def update_body(squares_ref, *refs):
    grads, states, results, norm_ref = refs[:3], refs[3:12], refs[12:21], refs[21]
    gain_grad = grads[2][...]
    squares = jnp.sum(squares_ref[...], axis=0)[:, 0:1] + jnp.sum(gain_grad * gain_grad)
    norm = jnp.sqrt(squares)
    norm_ref[...] = norm
    factor = jnp.minimum(1.0, clip_limit / (norm + 1e-06))
    rates = (rate_matrix, weight_decay), (rate_matrix, weight_decay), (rate_gain, 0.0)
    for kind, (step_rate, decay_rate) in enumerate(rates):
        grad = grads[kind][...]
        scale = factor.reshape((1,) * grad.ndim)
        new = adamw_update(
            *[ref[...] for ref in states[3 * kind : 3 * kind + 3]],
            grad,
            scale,
            step_rate,
            decay_rate,
        )
        for ref, value in zip(results[3 * kind : 3 * kind + 3], new):
            ref[...] = value


def update(squares, grads, states):
    shapes = [state.shape for state in states] + [(1, 1)]
    return pl.pallas_call(
        update_body,
        in_specs=[pl.BlockSpec(memory_space=pltpu.VMEM) for _ in range(13)],
        out_specs=[pl.BlockSpec(memory_space=pltpu.VMEM) for _ in shapes],
        out_shape=[jax.ShapeDtypeStruct(shape, F32) for shape in shapes],
        cost_estimate=SHORT,
        name="update",
    )(squares, *grads, *states)


def per_device(
    tokens,
    cotangent,
    documents,
    attention_master,
    attention_first,
    attention_second,
    feedforward_master,
    feedforward_first,
    feedforward_second,
    gain_master,
    gain_first,
    gain_second,
):
    seq_count, half_len, _ = tokens.shape
    own_count = seq_count // 2
    place = lax.axis_index("narrow")
    first = place == 0
    outer, inner = factors(lax.axis_size("wide"))
    wide_place = lax.axis_index("wide")
    outer_place, inner_place = wide_place // inner, wide_place % inner
    tables = rotary_tables(2 * half_len)
    gain_columns = gain_master.T
    x_own = jnp.swapaxes(tokens, 1, 2)
    cotangent_own = jnp.swapaxes(cotangent, 1, 2)

    def swap(tensor):
        return across(
            lax.dynamic_slice_in_dim(tensor, (1 - place) * own_count, own_count, 0)
        )

    x_other = swap(x_own)
    own_docs = lax.dynamic_slice_in_dim(documents, place * own_count, own_count, 0)
    start = jnp.zeros_like(own_docs)
    for number in (1, 2):
        before = jnp.sum((own_docs < number).astype(jnp.int32), axis=1, keepdims=True)
        start = jnp.where(own_docs == number, before, start)
    start = start[:, None, :]

    rows = attention_master.shape[0]
    aligned = rows % 16 == 0
    if aligned:
        chunk = jnp.arange(2 * inner * outer, dtype=jnp.int32)
        order = (
            ((chunk % 2) ^ place) * inner + ((chunk // 2 % inner) ^ inner_place)
        ) * outer + ((chunk // (2 * inner)) ^ outer_place)
        pair = chunk[: inner * outer]
        piece_of = (pair % inner) ^ inner_place
        row_of = ((pair // inner) ^ outer_place) * rows
        grad_pieces = inner
    else:
        order = jnp.arange(32, dtype=jnp.int32)
        piece_of = jnp.zeros((16,), jnp.int32)
        row_of = jnp.arange(16, dtype=jnp.int32) * 48
        grad_pieces = 1
    info = jnp.concatenate(
        [jnp.full((1,), place), order, piece_of, row_of]
    ).astype(jnp.int32)

    piece = attention_master.astype(BF16)
    parts = [piece] + [partner(piece, k * inner) for k in range(1, outer)]
    stack = jnp.stack(parts if aligned else in_order(parts, outer_place))
    feed_piece = feedforward_master.astype(BF16)
    feed_outer = jnp.stack(
        [feed_piece] + [partner(feed_piece, k * inner) for k in range(1, outer)]
    )
    parts = [stack] + [partner(stack, k) for k in range(1, inner)]
    feed_outer, parts[1:], info, start, gain_columns = lax.optimization_barrier(
        (feed_outer, parts[1:], info, start, gain_columns)
    )
    feed_parts = [feed_outer] + [partner(feed_outer, k) for k in range(1, inner)]
    if aligned:
        stack = jnp.stack(parts)
        pieces_own = stack.reshape(-1, rows, D)
        pieces_other = across(stack).reshape(-1, rows, D)
    else:
        stack = jnp.stack(in_order(parts, inner_place), axis=1)
        pieces = jnp.stack(in_order([stack, across(stack)], place), axis=2).reshape(-1, 48, D)
        pieces_own, pieces_other = pieces[:16], pieces[16:]
    cotangent_other = swap(cotangent_own)

    residual, query, key, value, mixed, total, normed, weight_qkv, weight_out = attention_forward(
        info, x_own, x_other, start, pieces_own, pieces_other, gain_columns, tables
    )
    feed_parts, residual = lax.optimization_barrier((feed_parts, residual))
    if aligned:
        feed_weights = feed_parts + [across(part) for part in feed_parts]
    else:
        stack = jnp.stack(feed_parts)
        feed_weights = [
            jnp.swapaxes(part.reshape(-1, 3, rows, D), 0, 1).reshape(1, 3, -1, D)
            for part in (stack, across(stack))
        ]
    outputs, out_other, back, gain_second_part, own_grad, other_grad = feed_forward(
        info, residual, cotangent_own, cotangent_other, feed_weights, gain_columns, inner
    )

    def place_other(whole_array, received):
        return lax.dynamic_update_slice_in_dim(
            whole_array, received.astype(whole_array.dtype), (1 - place) * own_count, 0
        )

    out_received = across(out_other)

    received = across(other_grad)
    grad_mixed, inner_sums, out_grad = branch_backward(back, mixed, weight_out)
    received, own_grad, grad_mixed = lax.optimization_barrier((received, own_grad, grad_mixed))
    feed_sums = [add_all([own_grad[k], received[k]]).astype(BF16) for k in range(inner)]
    feed_sums, grad_mixed = lax.optimization_barrier((feed_sums, grad_mixed))
    feed_got = [feed_sums[0]] + [partner(feed_sums[k], k) for k in range(1, inner)]
    projected, kept, sent = attention_backward(
        info,
        normed,
        start,
        gain_master,
        weight_qkv,
        out_grad,
        gain_second_part,
        tables,
        [query, key, value, total, grad_mixed, inner_sums],
        grad_pieces,
    )
    feed_got, kept, sent = lax.optimization_barrier((feed_got, kept, sent))
    summed = add_all(feed_got).astype(BF16).reshape(3, outer, -1, D)
    feed_last = [summed[:, k] for k in range(outer)]
    feed_last, sent = lax.optimization_barrier((feed_last, sent))
    feed_last = [feed_last[0]] + [partner(feed_last[k], k * inner) for k in range(1, outer)]

    received = across(sent)
    if aligned:
        parts = [add_all([kept[k], received[k]]).astype(BF16) for k in range(inner)]
    else:
        gain_grad = lax.psum(kept[0, -16:-14].astype(F32), ("wide", "narrow"))
        total = add_all([kept, received]).astype(BF16)[0, :-16].reshape(outer, inner, rows, D)
        parts = in_order([total[:, k] for k in range(inner)], inner_place)
    parts, projected = lax.optimization_barrier((parts, projected))
    got = [parts[0]] + [partner(parts[k], k) for k in range(1, inner)]
    grad_own, grad_other = input_grads(
        info, x_own, x_other, gain_columns, projected, weight_qkv, back
    )
    got, feed_last, grad_other = lax.optimization_barrier((got, feed_last, grad_other))
    total = add_all(got).astype(BF16)
    if aligned:
        tail = total[outer * rows :]
        parts = [
            jnp.concatenate([total[k * rows : (k + 1) * rows], tail], axis=0)
            for k in range(outer)
        ]
    else:
        parts = in_order([total[k] for k in range(outer)], outer_place)
    last = [parts[0]] + [partner(parts[k], k * inner) for k in range(1, outer)]
    devices = lax.axis_size("wide") * lax.axis_size("narrow")
    attention_grad, gain_total, feedforward_grad, squares = last_sums(
        last, feed_last, rows, devices
    )
    if aligned:
        gain_grad = gain_total
    squares = lax.all_to_all(squares, ("wide", "narrow"), 0, 0, tiled=True)
    grad_received = across(grad_other)
    attention_grad, gain_grad, grad_received, out_received = lax.optimization_barrier(
        (attention_grad, gain_grad, grad_received, out_received)
    )
    grad_tokens = place_other(grad_own, grad_received)
    outputs = place_other(outputs, out_received)
    states = (
        attention_master,
        attention_first,
        attention_second,
        feedforward_master,
        feedforward_first,
        feedforward_second,
        gain_master,
        gain_first,
        gain_second,
    )
    *updated, grad_norm = update(squares, (attention_grad, feedforward_grad, gain_grad), states)
    outputs = jnp.swapaxes(outputs, 1, 2)
    grad_tokens = jnp.swapaxes(grad_tokens, 1, 2)
    return (outputs, grad_tokens, grad_norm.reshape(()), *updated)


def solution(mesh):
    sequences = P("wide", "narrow", None)
    attention = P(("wide", "narrow"), None)
    feedforward = P(None, ("narrow", "wide"), None)
    state = (attention,) * 3 + (feedforward,) * 3 + (P(),) * 3
    return jax.shard_map(
        per_device,
        mesh=mesh,
        in_specs=(sequences, sequences, P("wide", None)) + state,
        out_specs=(sequences, sequences, P()) + state,
        check_vma=False,
    )
```

```python
import functools

import jax
import jax.numpy as jnp
import numpy as np
from jax import lax
from jax.experimental import pallas as pl
from jax.experimental.pallas import tpu as pltpu
from jax.sharding import PartitionSpec as P

D = 576
HEADS = 9
KV_HEADS = 3
RATIO = 3
HEAD_DIM = 64
HALF = 32
STEP = 10
KV_WIDTH = 192
QKV = 960
BLOCK = 256

norm_epsilon = 1e-05
adam_epsilon = 1e-08
beta_first = 0.9
beta_second = 0.999
weight_decay = 0.1
rate_matrix = 0.05
rate_gain = 0.5
clip_limit = 1.0
rotary_base = 10000.0
masked_value = -1e30

F32 = jnp.float32
BF16 = jnp.bfloat16
SHORT = pl.CostEstimate(flops=1_000_000, transcendentals=0, bytes_accessed=100_000)


def rotary_tables(length):
    frequency = np.float32(rotary_base) ** (
        np.float32(-2.0) * np.arange(HALF, dtype=np.float32) / np.float32(HEAD_DIM)
    )
    angles = np.arange(length, dtype=np.float32)[None, :] * frequency.astype(np.float32)[:, None]
    return jnp.asarray(np.cos(angles), F32), jnp.asarray(np.sin(angles), F32)


def dot(left, right, left_dim=1, right_dim=0):
    return lax.dot_general(
        left, right, (((left_dim,), (right_dim,)), ((), ())), preferred_element_type=F32
    )


def inverse_root(values):
    return lax.rsqrt(jnp.mean(values * values, axis=0, keepdims=True) + norm_epsilon)


def joined(own, other, place):
    first = place == 0
    return jnp.concatenate(
        [jnp.where(first, own, other), jnp.where(first, other, own)], axis=1
    )


def lane_sums(values):
    lanes = 128
    total = values[:, :lanes]
    for low in range(lanes, values.shape[1], lanes):
        total = total + values[:, low : low + lanes]
    return total


def norm_backward(grad_normed, normal, inverse, gain):
    scaled = grad_normed * gain
    return inverse * (scaled - normal * jnp.mean(scaled * normal, axis=0, keepdims=True))


def visible_scores(scores, start_row, place_row, low, key_low):
    inside = low >= 256 and low + BLOCK <= 768 and key_low >= 256
    if inside and key_low < low:
        return scores
    place = lax.broadcasted_iota(jnp.int32, scores.shape, 0) + key_low
    if inside:
        seen = place <= place_row
    else:
        seen = place >= start_row
        if key_low >= low:
            seen = seen & (place <= place_row)
    return jnp.where(seen, scores, masked_value)


def triple(row):
    return jnp.concatenate([row] * RATIO, axis=1)


def turn(rows, cosine, sine):
    front, behind = rows[:HALF], rows[HALF:]
    return jnp.concatenate([front * cosine - behind * sine, behind * cosine + front * sine], axis=0)


def turn_back(rows, cosine, sine):
    front, behind = rows[:HALF], rows[HALF:]
    return jnp.concatenate([front * cosine + behind * sine, behind * cosine - front * sine], axis=0)


def attention_forward_body(
    info_ref,
    own_ref,
    other_ref,
    start_ref,
    pieces_own_ref,
    pieces_other_ref,
    gain_ref,
    cosine_ref,
    sine_ref,
    residual_ref,
    query_ref,
    key_ref,
    value_ref,
    mixed_ref,
    total_ref,
    normed_ref,
    weight_ref,
    out_weight_ref,
    out_rows,
    key_rows,
    x_across,
):
    @pl.when(pl.program_id(0) == 0)
    def _():
        chunks, rows, _ = pieces_own_ref.shape
        for chunk in range(2 * chunks):
            index = info_ref[1 + chunk]
            is_own = index < chunks
            index = jnp.where(is_own, index, index - chunks)
            part = jnp.where(is_own, pieces_own_ref[index], pieces_other_ref[index])
            low = chunk * rows
            if low < QKV:
                weight_ref[low : low + rows] = part
            else:
                out_weight_ref[low - QKV : low - QKV + rows] = part
        out_rows[...] = out_weight_ref[...].T

    x = joined(own_ref[0], other_ref[0], info_ref[0])
    length = x.shape[1]
    x_across[...] = x
    x = x.astype(F32)
    normed = (x * inverse_root(x) * gain_ref[:, 0:1]).astype(BF16)
    cosine = cosine_ref[...]
    sine = sine_ref[...]
    normed_ref[0] = normed
    projected = dot(weight_ref[...], normed)
    for head in range(HEADS):
        rows = slice(head * 64, head * 64 + 64)
        query_ref[0, rows] = (turn(projected[rows], cosine, sine) * HEAD_DIM ** (-0.5)).astype(
            BF16
        )
    for head in range(KV_HEADS):
        rows = slice(head * 64, head * 64 + 64)
        rotated = turn(projected[D + head * 64 : D + head * 64 + 64], cosine, sine)
        key_ref[0, rows] = rotated.astype(BF16)
        key_rows[head] = rotated.T.astype(BF16)
    value_ref[0] = projected[D + KV_WIDTH :].astype(BF16)

    def score(member, block, r):
        low, high = block * BLOCK, (block + 1) * BLOCK
        row = (member * RATIO + r) * 64
        return dot(key_rows[member, 0:high], query_ref[0, row : row + 64, low:high])

    def finish(member, block, r, scores):
        low, high = block * BLOCK, (block + 1) * BLOCK
        start_row = start_ref[0, 0:1, low:high]
        place_row = lax.broadcasted_iota(jnp.int32, (1, BLOCK), 1) + low
        scores = [
            visible_scores(scores[k : k + BLOCK], start_row, place_row, low, k)
            for k in range(0, high, BLOCK)
        ]
        top = functools.reduce(
            jnp.maximum, [jnp.max(part, axis=0, keepdims=True) for part in scores]
        )
        exponents = [jnp.exp(part - top) for part in scores]
        total = sum(jnp.sum(part, axis=0, keepdims=True) for part in exponents)
        exponent = jnp.concatenate([part.astype(BF16) for part in exponents], axis=0)
        mixed = dot(value_ref[0, member * 64 : member * 64 + 64, 0:high], exponent)
        row = (member * RATIO + r) * 64
        mixed_ref[0, row : row + 64, low:high] = (mixed * (1.0 / total)).astype(BF16)
        total_ref[0, member, r : r + 1, low:high] = top + jnp.log(total)

    items = [
        (member, block, r)
        for member in range(KV_HEADS)
        for block in range(length // BLOCK)
        for r in range(RATIO)
    ]
    ahead = [score(*item) for item in items[:2]]
    for i, item in enumerate(items):
        if i + 2 < len(items):
            ahead.append(score(*items[i + 2]))
        finish(*item, ahead.pop(0))
    residual_ref[0] = x_across[...].astype(F32) + dot(out_rows[...], mixed_ref[0])


def whole(shape):
    return pl.BlockSpec(
        tuple(shape), lambda *_: (0,) * len(shape), pipeline_mode=pl.Buffered(1)
    )


def step_spec(shape):
    return pl.BlockSpec((1,) + tuple(shape[1:]), lambda i, info: (i,) + (0,) * (len(shape) - 1))


def params(mebibytes):
    return pltpu.CompilerParams(
        dimension_semantics=("arbitrary",), vmem_limit_bytes=mebibytes * 2**20
    )


def attention_forward(info, own, other, start, pieces_own, pieces_other, gain, tables):
    count = other.shape[0]
    length = 2 * other.shape[2]
    outs = [
        ((count, D, length), F32),
        ((count, D, length), BF16),
        ((count, KV_WIDTH, length), BF16),
        ((count, KV_WIDTH, length), BF16),
        ((count, D, length), BF16),
        ((count, KV_HEADS, 8, length), F32),
        ((count, D, length), BF16),
    ]
    weights = (QKV, D), (D, D)
    return pl.pallas_call(
        attention_forward_body,
        grid_spec=pltpu.PrefetchScalarGridSpec(
            num_scalar_prefetch=1,
            grid=(count,),
            in_specs=[
                pl.BlockSpec(
                    (1,) + own.shape[1:], lambda i, info: (info[0] * count + i, 0, 0)
                ),
                step_spec(other.shape),
                step_spec(start.shape),
                whole(pieces_own.shape),
                whole(pieces_other.shape),
                whole(gain.shape),
                whole((HALF, length)),
                whole((HALF, length)),
            ],
            out_specs=[step_spec(shape) for shape, _ in outs] + [whole(shape) for shape in weights],
            scratch_shapes=[
                pltpu.VMEM((D, D), BF16),
                pltpu.VMEM((KV_HEADS, length, HEAD_DIM), BF16),
                pltpu.VMEM((D, length), BF16),
            ],
        ),
        out_shape=[jax.ShapeDtypeStruct(shape, kind) for shape, kind in outs]
        + [jax.ShapeDtypeStruct(shape, BF16) for shape in weights],
        compiler_params=params(28),
        cost_estimate=pl.CostEstimate(
            flops=8_000_000_000, transcendentals=12_000_000, bytes_accessed=20_000_000
        ),
        name="attention_forward",
    )(info, own, other, start, pieces_own, pieces_other, gain, *tables)


def stacked(refs, kinds):
    parts = [ref[:, kind].reshape(-1, D) for kind in kinds for ref in refs]
    return jnp.concatenate(parts, axis=0) if len(parts) > 1 else parts[0]


def feed_body(part_count, info_ref, residual_ref, cotangent_own_ref, cotangent_other_ref, *refs):
    weight_refs = refs[:part_count], refs[part_count : 2 * part_count]
    (
        gain_ref,
        out_own_ref,
        out_other_ref,
        back_ref,
        gain_grad_ref,
        grad_own_ref,
        grad_other_ref,
        sums,
        gain_sums,
    ) = refs[2 * part_count :]
    step = pl.program_id(0)
    units = sums.shape[2] // 3
    residual = residual_ref[0]
    cotangent = jnp.where(step % 2 == 0, cotangent_own_ref[0], cotangent_other_ref[0])
    gain = gain_ref[:, 1:2]
    inverse = inverse_root(residual)
    normal = residual * inverse
    normed = (normal * gain).astype(BF16)

    @pl.when(step == 0)
    def _():
        sums[...] = jnp.zeros_like(sums)
        gain_sums[...] = jnp.zeros_like(gain_sums)

    out = residual
    grad_normed = jnp.zeros_like(residual)
    for part, parts in enumerate(weight_refs):
        pair = stacked(parts, (0, 1))
        down = stacked(parts, (2,))
        both = dot(pair, normed)
        gate, upward = both[:units], both[units:]
        grad_hidden = dot(down, cotangent)
        sigmoid_gate = jax.nn.sigmoid(gate)
        swish = gate * sigmoid_gate
        hidden = (swish * upward).astype(BF16)
        grad_gate = (
            grad_hidden * upward * (sigmoid_gate + swish * (1.0 - sigmoid_gate))
        ).astype(BF16)
        grad_upward = (grad_hidden * swish).astype(BF16)
        grads = jnp.concatenate([grad_gate, grad_upward], axis=0)
        out = out + dot(down, hidden, 0, 0)
        grad_normed = grad_normed + dot(pair, grads, 0, 0)
        sums[part, :, : 2 * units] += dot(normed, grads, 1, 1)
        sums[part, :, 2 * units :] += dot(cotangent, hidden, 1, 1)

    out = out.astype(BF16)

    @pl.when(step % 2 == 0)
    def _():
        out_own_ref[0] = out

    @pl.when(step % 2 == 1)
    def _():
        out_other_ref[0] = out

    gain_sums[...] += lane_sums(grad_normed * normal)
    back_ref[0] = (
        cotangent.astype(F32) + norm_backward(grad_normed, normal, inverse, gain)
    ).astype(BF16)

    @pl.when(step == pl.num_programs(0) - 1)
    def _():
        pieces, kinds, rows, _ = grad_own_ref.shape
        for part, grad_ref in enumerate((grad_own_ref, grad_other_ref)):
            for kind in range(kinds):
                flipped = sums[part, :, kind * units : (kind + 1) * units].astype(BF16).T
                for piece in range(pieces):
                    grad_ref[piece, kind] = flipped[piece * rows : (piece + 1) * rows]
        gain_grad_ref[...] = jnp.sum(gain_sums[...].T, axis=0, keepdims=True)


def feed_forward(info, residual, cotangent_own, cotangent_other, weights, gain, pieces):
    count, _, length = residual.shape
    half = length // 2
    part_count = len(weights) // 2
    units = sum(part.size // (3 * D) for part in weights[:part_count])
    block = (1, D, half)
    full = pl.BlockSpec(block, lambda i, info: (i // 2, 0, (i + info[0]) % 2))
    own = pl.BlockSpec(block, lambda i, info: (info[0] * count + i // 2, 0, 0))
    other = pl.BlockSpec(block, lambda i, info: (i // 2, 0, 0))
    grad_shape = (pieces, 3, units // pieces, D)
    return pl.pallas_call(
        functools.partial(feed_body, part_count),
        grid_spec=pltpu.PrefetchScalarGridSpec(
            num_scalar_prefetch=1,
            grid=(2 * count,),
            in_specs=[full, own, other]
            + [whole(weight.shape) for weight in weights]
            + [whole(gain.shape)],
            out_specs=[own, other, full, whole((1, D))] + [whole(grad_shape)] * 2,
            scratch_shapes=[
                pltpu.VMEM((2, D, 3 * units), F32),
                pltpu.VMEM((D, 128), F32),
            ],
        ),
        out_shape=[
            jax.ShapeDtypeStruct(cotangent_own.shape, BF16),
            jax.ShapeDtypeStruct(cotangent_other.shape, BF16),
            jax.ShapeDtypeStruct(residual.shape, BF16),
            jax.ShapeDtypeStruct((1, D), F32),
        ]
        + [jax.ShapeDtypeStruct(grad_shape, BF16)] * 2,
        compiler_params=params(48),
        cost_estimate=pl.CostEstimate(
            flops=32_000_000_000, transcendentals=6_000_000, bytes_accessed=30_000_000
        ),
        name="feed_forward",
    )(info, residual, cotangent_own, cotangent_other, *weights, gain)


def branch_backward_body(
    grad_ref, mixed_ref, weight_ref, grad_mixed_ref, inner_ref, weight_grad_ref
):
    @pl.when(pl.program_id(0) == 0)
    def _():
        weight_grad_ref[...] = jnp.zeros_like(weight_grad_ref)

    branch = grad_ref[0]
    grad_mixed = dot(weight_ref[...], branch).astype(BF16)
    grad_mixed_ref[0] = grad_mixed
    for head in range(HEADS):
        rows = slice(head * 64, head * 64 + 64)
        inner_ref[0, head // RATIO, head % RATIO : head % RATIO + 1] = jnp.sum(
            grad_mixed[rows].astype(F32) * mixed_ref[0, rows].astype(F32), axis=0, keepdims=True
        )
    weight_grad_ref[...] += dot(mixed_ref[0], branch, 1, 1)


def branch_backward(grad, mixed, weight):
    count, _, length = grad.shape

    half = length // 2
    step = pl.BlockSpec((1, D, half), lambda i: (i // 2, 0, i % 2))
    inner = (count, KV_HEADS, 8, length)
    return pl.pallas_call(
        branch_backward_body,
        grid=(2 * count,),
        in_specs=[step, step, whole(weight.shape)],
        out_specs=[
            step,
            pl.BlockSpec((1, KV_HEADS, 8, half), lambda i: (i // 2, 0, 0, i % 2)),
            whole((D, D)),
        ],
        out_shape=[
            jax.ShapeDtypeStruct(mixed.shape, BF16),
            jax.ShapeDtypeStruct(inner, F32),
            jax.ShapeDtypeStruct((D, D), F32),
        ],
        compiler_params=params(8),
        cost_estimate=SHORT,
        name="branch_backward",
    )(grad, mixed, weight)


def attention_backward_body(
    info_ref,
    normed_ref,
    start_ref,
    gain_row_ref,
    weight_hbm,
    out_grad_hbm,
    gain_second_ref,
    cosine_ref,
    sine_ref,
    query_ref,
    key_ref,
    value_ref,
    total_ref,
    grad_ref,
    inner_ref,
    projected_ref,
    kept_ref,
    sent_ref,
    key_rows,
    value_rows,
    grad_key,
    grad_value,
    weight_sums,
    weight_ref,
    out_grad_ref,
    semaphores,
):
    step = pl.program_id(0)
    copies = [
        pltpu.make_async_copy(weight_hbm, weight_ref, semaphores.at[0]),
        pltpu.make_async_copy(out_grad_hbm, out_grad_ref, semaphores.at[1]),
    ]

    @pl.when(step == 0)
    def _():
        for copy in copies:
            copy.start()

    length = query_ref.shape[2]
    cosine = cosine_ref[...]
    sine = sine_ref[...]
    for head in range(KV_HEADS):
        rows = slice(head * 64, head * 64 + 64)
        key_rows[head] = key_ref[0, rows].T
        value_rows[head] = value_ref[0, rows].T

    def head_rows(member, r):
        return slice((member * RATIO + r) * 64, (member * RATIO + r) * 64 + 64)

    def products(member, low, key_low, r):
        keys = slice(key_low, key_low + 256)
        rows = head_rows(member, r)
        return (
            dot(key_rows[member, keys], query_ref[0, rows, low : low + BLOCK]),
            dot(value_rows[member, keys], grad_ref[0, rows, low : low + BLOCK]),
        )

    def weighted(member, low, key_low, r, scores, grad_weights):
        lanes = slice(low, low + BLOCK)
        start_row = start_ref[0, 0:1, lanes]
        place_row = lax.broadcasted_iota(jnp.int32, (1, BLOCK), 1) + low
        scores = visible_scores(scores, start_row, place_row, low, key_low)
        weights = jnp.exp(scores - total_ref[0, member, r : r + 1, lanes])
        grad_scores = weights * (grad_weights - inner_ref[0, member, r : r + 1, lanes])
        return weights.astype(BF16), grad_scores.astype(BF16)

    items = [
        (member, low, key_low, r)
        for member in range(KV_HEADS)
        for low in range(0, length, BLOCK)
        for key_low in range(0, low + BLOCK, 256)
        for r in range(RATIO)
    ]
    ahead = [products(*item) for item in items[:2]]
    sums = {}

    def add(key, value):
        sums[key] = sums[key] + value if key in sums else value

    for i, item in enumerate(items):
        member, low, key_low, r = item
        if i + 2 < len(items):
            ahead.append(products(*items[i + 2]))
        weights, grad_scores = weighted(*item, *ahead.pop(0))
        rows = head_rows(member, r)
        keys = slice(key_low, key_low + 256)
        add("value", dot(grad_ref[0, rows, low : low + BLOCK], weights, 1, 1))
        add("key", dot(query_ref[0, rows, low : low + BLOCK], grad_scores, 1, 1))
        add(r, dot(key_ref[0, member * 64 : member * 64 + 64, keys], grad_scores))
        if r == RATIO - 1:
            for name, ref in (("value", grad_value), ("key", grad_key)):
                part = sums.pop(name)
                if key_low - key_low % BLOCK == low:
                    ref[member, :, keys] = part
                else:
                    ref[member, :, keys] += part
        if key_low + 256 == low + BLOCK:
            projected_ref[0, rows, low : low + BLOCK] = turn_back(
                sums.pop(r) * HEAD_DIM ** (-0.5),
                cosine[:, low : low + BLOCK],
                sine[:, low : low + BLOCK],
            ).astype(BF16)
    for member in range(KV_HEADS):
        row = D + member * 64
        projected_ref[0, row : row + 64] = turn_back(grad_key[member], cosine, sine).astype(BF16)
        row += KV_WIDTH
        projected_ref[0, row : row + 64] = grad_value[member].astype(BF16)

    product = dot(projected_ref[0], normed_ref[0], 1, 1)

    @pl.when(step == 0)
    def _():
        weight_sums[...] = product

    @pl.when(step > 0)
    def _():
        weight_sums[...] += product

    @pl.when(step == pl.num_programs(0) - 1)
    def _():
        for copy in copies:
            copy.wait()
        rows = 48
        pairs = (QKV + D) // (2 * rows)
        first = info_ref[0] == 0
        gain_sums = jnp.zeros((rows, D), F32)
        for pair in range(pairs):
            low = pair * 2 * rows
            if low < QKV:
                even, odd = weight_sums[low : low + rows], weight_sums[low + rows : low + 2 * rows]
                gain_sums = gain_sums + even * weight_ref[low : low + rows].astype(F32)
                gain_sums = gain_sums + odd * weight_ref[low + rows : low + 2 * rows].astype(F32)
            else:
                low -= QKV
                even = out_grad_ref[low : low + rows]
                odd = out_grad_ref[low + rows : low + 2 * rows]
            even, odd = even.astype(BF16), odd.astype(BF16)
            piece = info_ref[1 + 2 * pairs + pair]
            target = pl.ds(pl.multiple_of(info_ref[1 + 3 * pairs + pair], 16), rows)
            kept_ref[piece, target] = jnp.where(first, even, odd)
            sent_ref[piece, target] = jnp.where(first, odd, even)
        gain_first = jnp.sum(gain_sums, axis=0, keepdims=True) / gain_row_ref[0:1]
        tail = jnp.concatenate(
            [gain_first, gain_second_ref[...], jnp.zeros((14, D), F32)], axis=0
        ).astype(BF16)
        pieces, held, _ = kept_ref.shape
        for piece in range(pieces):
            kept_ref[piece, held - 16 :] = tail
            sent_ref[piece, held - 16 :] = tail


def attention_backward(
    info, normed, start, gain_rows, weight, out_grad, gain_second, tables, parts, pieces
):
    count, _, length = normed.shape
    held = (pieces, (QKV + D) // (2 * pieces) + 16, D)
    projected = (count, QKV, length)
    before, after = [gain_rows], [gain_second, *tables]
    return pl.pallas_call(
        attention_backward_body,
        grid_spec=pltpu.PrefetchScalarGridSpec(
            num_scalar_prefetch=1,
            grid=(count,),
            in_specs=[
                step_spec(normed.shape),
                step_spec(start.shape),
            ]
            + [whole(part.shape) for part in before]
            + [pl.BlockSpec(memory_space=pl.ANY)] * 2
            + [whole(part.shape) for part in after]
            + [step_spec(part.shape) for part in parts],
            out_specs=[step_spec(projected)] + [whole(held)] * 2,
            scratch_shapes=[
                pltpu.VMEM((KV_HEADS, length, HEAD_DIM), BF16),
                pltpu.VMEM((KV_HEADS, length, HEAD_DIM), BF16),
                pltpu.VMEM((KV_HEADS, HEAD_DIM, length), F32),
                pltpu.VMEM((KV_HEADS, HEAD_DIM, length), F32),
                pltpu.VMEM((QKV, D), F32),
                pltpu.VMEM(weight.shape, BF16),
                pltpu.VMEM(out_grad.shape, F32),
                pltpu.SemaphoreType.DMA((2,)),
            ],
        ),
        out_shape=[jax.ShapeDtypeStruct(projected, BF16)]
        + [jax.ShapeDtypeStruct(held, BF16)] * 2,
        compiler_params=params(28),
        cost_estimate=pl.CostEstimate(
            flops=9_000_000_000, transcendentals=6_000_000, bytes_accessed=15_000_000
        ),
        name="attention_backward",
    )(info, normed, start, *before, weight, out_grad, *after, *parts)


def input_grads_body(
    info_ref,
    own_ref,
    other_ref,
    gain_ref,
    projected_ref,
    weight_ref,
    grad_ref,
    tokens_own_ref,
    tokens_other_ref,
):
    step = pl.program_id(0)
    x = jnp.where(step % 2 == 0, own_ref[0], other_ref[0]).astype(F32)
    gain = gain_ref[:, 0:1]
    inverse = inverse_root(x)
    normal = x * inverse
    grad_normed = dot(weight_ref[...], projected_ref[0], 0, 0)
    grad_x = grad_ref[0].astype(F32) + norm_backward(grad_normed, normal, inverse, gain)

    @pl.when(step % 2 == 0)
    def _():
        tokens_own_ref[0] = grad_x

    @pl.when(step % 2 == 1)
    def _():
        tokens_other_ref[0] = grad_x.astype(BF16)


def input_grads(info, own, other, gain, projected, weight, grad):
    count = other.shape[0]
    half = other.shape[2]
    own_spec = pl.BlockSpec((1, D, half), lambda i, info: (info[0] * count + i // 2, 0, 0))
    other_spec = pl.BlockSpec((1, D, half), lambda i, info: (i // 2, 0, 0))

    def full(height):
        return pl.BlockSpec((1, height, half), lambda i, info: (i // 2, 0, (i + info[0]) % 2))

    return pl.pallas_call(
        input_grads_body,
        grid_spec=pltpu.PrefetchScalarGridSpec(
            num_scalar_prefetch=1,
            grid=(2 * count,),
            in_specs=[
                own_spec,
                other_spec,
                whole(gain.shape),
                full(QKV),
                whole(weight.shape),
                full(D),
            ],
            out_specs=[own_spec, other_spec],
        ),
        out_shape=[
            jax.ShapeDtypeStruct(own.shape, F32),
            jax.ShapeDtypeStruct(other.shape, BF16),
        ],
        compiler_params=params(16),
        cost_estimate=SHORT,
        name="input_grads",
    )(info, own, other, gain, projected, weight, grad)


def factors(count):
    inner = 1 << ((count.bit_length() - 1) // 2)
    return count // inner, inner


def partner(values, mask):
    count = lax.axis_size("wide")
    return lax.ppermute(values, "wide", [(i, i ^ mask) for i in range(count)])


def across(values):
    return lax.ppermute(values, "narrow", [(0, 1), (1, 0)])


def in_order(parts, place):
    bit = 1
    while bit < len(parts):
        swap = (place & bit) != 0
        parts = [jnp.where(swap, parts[i ^ bit], part) for i, part in enumerate(parts)]
        bit *= 2
    return parts


def add_all(parts):
    parts = [part.astype(F32) for part in parts]
    while len(parts) > 1:
        parts = [parts[i] + parts[i + 1] for i in range(0, len(parts), 2)]
    return parts[0]


def adamw_update(master, first_state, second_state, gradient, factor, step_rate, decay_rate):
    clipped = gradient * factor
    first_new = beta_first * first_state + (1.0 - beta_first) * clipped
    second_new = beta_second * second_state + (1.0 - beta_second) * clipped * clipped
    first_hat = first_new / (1.0 - beta_first**STEP)
    second_hat = second_new / (1.0 - beta_second**STEP)
    master_new = master * (1.0 - step_rate * decay_rate) - step_rate * first_hat / (
        jnp.sqrt(second_hat) + adam_epsilon
    )
    return (master_new, first_new, second_new)


def squares_body(count, rows, *refs):
    attention_ref, gain_ref, feedforward_ref, sent_ref = refs[2 * count :]
    attention = add_all([ref[...] for ref in refs[:count]])
    feedforward = add_all([ref[...] for ref in refs[count : 2 * count]])
    owned = attention[:rows]
    attention_ref[...] = owned
    if attention.shape[0] > rows:
        gain_ref[...] = attention[rows : rows + 2]
    else:
        gain_ref[...] = jnp.zeros_like(gain_ref)
    feedforward_ref[...] = feedforward
    local = jnp.sum(owned * owned) + jnp.sum(feedforward * feedforward)
    sent_ref[...] = jnp.full(sent_ref.shape, local, F32)


def last_sums(attention, feedforward, rows, devices):
    parts = attention + feedforward
    shapes = [(rows, D), (2, D), feedforward[0].shape, (devices, 1, 128)]
    return pl.pallas_call(
        functools.partial(squares_body, len(attention), rows),
        in_specs=[pl.BlockSpec(memory_space=pltpu.VMEM) for _ in parts],
        out_specs=[pl.BlockSpec(memory_space=pltpu.VMEM) for _ in shapes],
        out_shape=[jax.ShapeDtypeStruct(shape, F32) for shape in shapes],
        compiler_params=pltpu.CompilerParams(vmem_limit_bytes=6 * 2**20),
        cost_estimate=SHORT,
        name="last_sums",
    )(*parts)


def update_body(squares_ref, *refs):
    grads, states, results, norm_ref = refs[:3], refs[3:12], refs[12:21], refs[21]
    gain_grad = grads[2][...]
    squares = jnp.sum(squares_ref[...], axis=0)[:, 0:1] + jnp.sum(gain_grad * gain_grad)
    norm = jnp.sqrt(squares)
    norm_ref[...] = norm
    factor = jnp.minimum(1.0, clip_limit / (norm + 1e-06))
    rates = (rate_matrix, weight_decay), (rate_matrix, weight_decay), (rate_gain, 0.0)
    for kind, (step_rate, decay_rate) in enumerate(rates):
        grad = grads[kind][...]
        scale = factor.reshape((1,) * grad.ndim)
        new = adamw_update(
            *[ref[...] for ref in states[3 * kind : 3 * kind + 3]],
            grad,
            scale,
            step_rate,
            decay_rate,
        )
        for ref, value in zip(results[3 * kind : 3 * kind + 3], new):
            ref[...] = value


def update(squares, grads, states):
    shapes = [state.shape for state in states] + [(1, 1)]
    return pl.pallas_call(
        update_body,
        in_specs=[pl.BlockSpec(memory_space=pltpu.VMEM) for _ in range(13)],
        out_specs=[pl.BlockSpec(memory_space=pltpu.VMEM) for _ in shapes],
        out_shape=[jax.ShapeDtypeStruct(shape, F32) for shape in shapes],
        compiler_params=pltpu.CompilerParams(vmem_limit_bytes=12 * 2**20),
        cost_estimate=SHORT,
        name="update",
    )(squares, *grads, *states)


def per_device(
    tokens,
    cotangent,
    documents,
    attention_master,
    attention_first,
    attention_second,
    feedforward_master,
    feedforward_first,
    feedforward_second,
    gain_master,
    gain_first,
    gain_second,
):
    seq_count, half_len, _ = tokens.shape
    own_count = seq_count // 2
    place = lax.axis_index("narrow")
    first = place == 0
    outer, inner = factors(lax.axis_size("wide"))
    wide_place = lax.axis_index("wide")
    outer_place, inner_place = wide_place // inner, wide_place % inner
    tables = rotary_tables(2 * half_len)
    gain_columns = gain_master.T
    x_own = jnp.swapaxes(tokens, 1, 2)
    cotangent_own = jnp.swapaxes(cotangent, 1, 2)

    def swap(tensor):
        return across(
            lax.dynamic_slice_in_dim(tensor, (1 - place) * own_count, own_count, 0)
        )

    x_other = swap(x_own)
    own_docs = lax.dynamic_slice_in_dim(documents, place * own_count, own_count, 0)
    start = jnp.zeros_like(own_docs)
    for number in (1, 2):
        before = jnp.sum((own_docs < number).astype(jnp.int32), axis=1, keepdims=True)
        start = jnp.where(own_docs == number, before, start)
    start = start[:, None, :]

    rows = attention_master.shape[0]
    aligned = rows % 16 == 0
    if aligned:
        chunk = jnp.arange(2 * inner * outer, dtype=jnp.int32)
        order = (
            ((chunk % 2) ^ place) * inner + ((chunk // 2 % inner) ^ inner_place)
        ) * outer + ((chunk // (2 * inner)) ^ outer_place)
        pair = chunk[: inner * outer]
        piece_of = (pair % inner) ^ inner_place
        row_of = ((pair // inner) ^ outer_place) * rows
        grad_pieces = inner
    else:
        order = jnp.arange(32, dtype=jnp.int32)
        piece_of = jnp.zeros((16,), jnp.int32)
        row_of = jnp.arange(16, dtype=jnp.int32) * 48
        grad_pieces = 1
    info = jnp.concatenate(
        [jnp.full((1,), place), order, piece_of, row_of]
    ).astype(jnp.int32)

    piece = attention_master.astype(BF16)
    parts = [piece] + [partner(piece, k * inner) for k in range(1, outer)]
    stack = jnp.stack(parts if aligned else in_order(parts, outer_place))
    feed_piece = feedforward_master.astype(BF16)
    feed_outer = jnp.stack(
        [feed_piece] + [partner(feed_piece, k * inner) for k in range(1, outer)]
    )
    parts = [stack] + [partner(stack, k) for k in range(1, inner)]
    feed_outer, parts[1:], info, start, gain_columns = lax.optimization_barrier(
        (feed_outer, parts[1:], info, start, gain_columns)
    )
    feed_parts = [feed_outer] + [partner(feed_outer, k) for k in range(1, inner)]
    if aligned:
        stack = jnp.stack(parts)
        pieces_own = stack.reshape(-1, rows, D)
        pieces_other = across(stack).reshape(-1, rows, D)
    else:
        stack = jnp.stack(in_order(parts, inner_place), axis=1)
        pieces = jnp.stack(in_order([stack, across(stack)], place), axis=2).reshape(-1, 48, D)
        pieces_own, pieces_other = pieces[:16], pieces[16:]
    cotangent_other = swap(cotangent_own)

    residual, query, key, value, mixed, total, normed, weight_qkv, weight_out = attention_forward(
        info, x_own, x_other, start, pieces_own, pieces_other, gain_columns, tables
    )
    feed_parts, residual = lax.optimization_barrier((feed_parts, residual))
    if aligned:
        feed_weights = feed_parts + [across(part) for part in feed_parts]
    else:
        stack = jnp.stack(feed_parts)
        feed_weights = [
            jnp.swapaxes(part.reshape(-1, 3, rows, D), 0, 1).reshape(1, 3, -1, D)
            for part in (stack, across(stack))
        ]
    outputs, out_other, back, gain_second_part, own_grad, other_grad = feed_forward(
        info, residual, cotangent_own, cotangent_other, feed_weights, gain_columns, inner
    )

    def place_other(whole_array, received):
        return lax.dynamic_update_slice_in_dim(
            whole_array, received.astype(whole_array.dtype), (1 - place) * own_count, 0
        )

    out_received = across(out_other)

    received = across(other_grad)
    grad_mixed, inner_sums, out_grad = branch_backward(back, mixed, weight_out)
    received, own_grad, grad_mixed = lax.optimization_barrier((received, own_grad, grad_mixed))
    feed_sums = [add_all([own_grad[k], received[k]]).astype(BF16) for k in range(inner)]
    feed_sums, grad_mixed = lax.optimization_barrier((feed_sums, grad_mixed))
    feed_got = [feed_sums[0]] + [partner(feed_sums[k], k) for k in range(1, inner)]
    projected, kept, sent = attention_backward(
        info,
        normed,
        start,
        gain_master,
        weight_qkv,
        out_grad,
        gain_second_part,
        tables,
        [query, key, value, total, grad_mixed, inner_sums],
        grad_pieces,
    )
    feed_got, kept, sent = lax.optimization_barrier((feed_got, kept, sent))
    summed = add_all(feed_got).astype(BF16).reshape(3, outer, -1, D)
    feed_last = [summed[:, k] for k in range(outer)]
    feed_last, sent = lax.optimization_barrier((feed_last, sent))
    feed_last = [feed_last[0]] + [partner(feed_last[k], k * inner) for k in range(1, outer)]

    received = across(sent)
    if aligned:
        parts = [add_all([kept[k], received[k]]).astype(BF16) for k in range(inner)]
    else:
        gain_grad = lax.psum(kept[0, -16:-14].astype(F32), ("wide", "narrow"))
        total = add_all([kept, received]).astype(BF16)[0, :-16].reshape(outer, inner, rows, D)
        parts = in_order([total[:, k] for k in range(inner)], inner_place)
    parts, projected = lax.optimization_barrier((parts, projected))
    got = [parts[0]] + [partner(parts[k], k) for k in range(1, inner)]
    grad_own, grad_other = input_grads(
        info, x_own, x_other, gain_columns, projected, weight_qkv, back
    )
    got, feed_last, grad_other = lax.optimization_barrier((got, feed_last, grad_other))
    total = add_all(got).astype(BF16)
    if aligned:
        tail = total[outer * rows :]
        parts = [
            jnp.concatenate([total[k * rows : (k + 1) * rows], tail], axis=0)
            for k in range(outer)
        ]
    else:
        parts = in_order([total[k] for k in range(outer)], outer_place)
    last = [parts[0]] + [partner(parts[k], k * inner) for k in range(1, outer)]
    devices = lax.axis_size("wide") * lax.axis_size("narrow")
    attention_grad, gain_total, feedforward_grad, squares = last_sums(
        last, feed_last, rows, devices
    )
    if aligned:
        gain_grad = gain_total
    squares = lax.all_to_all(squares, ("wide", "narrow"), 0, 0, tiled=True)
    grad_received = across(grad_other)
    attention_grad, gain_grad, grad_received, out_received = lax.optimization_barrier(
        (attention_grad, gain_grad, grad_received, out_received)
    )
    grad_tokens = place_other(grad_own, grad_received)
    outputs = place_other(outputs, out_received)
    states = (
        attention_master,
        attention_first,
        attention_second,
        feedforward_master,
        feedforward_first,
        feedforward_second,
        gain_master,
        gain_first,
        gain_second,
    )
    *updated, grad_norm = update(squares, (attention_grad, feedforward_grad, gain_grad), states)
    outputs = jnp.swapaxes(outputs, 1, 2)
    grad_tokens = jnp.swapaxes(grad_tokens, 1, 2)
    return (outputs, grad_tokens, grad_norm.reshape(()), *updated)


def solution(mesh):
    sequences = P("wide", "narrow", None)
    attention = P(("wide", "narrow"), None)
    feedforward = P(None, ("narrow", "wide"), None)
    state = (attention,) * 3 + (feedforward,) * 3 + (P(),) * 3
    return jax.shard_map(
        per_device,
        mesh=mesh,
        in_specs=(sequences, sequences, P("wide", None)) + state,
        out_specs=(sequences, sequences, P()) + state,
        check_vma=False,
    )
```

```python
import functools

import jax
import jax.numpy as jnp
import numpy as np
from jax import lax
from jax.experimental import pallas as pl
from jax.experimental.pallas import tpu as pltpu
from jax.sharding import PartitionSpec as P

D = 576
HEADS = 9
KV_HEADS = 3
RATIO = 3
HEAD_DIM = 64
HALF = 32
STEP = 10
KV_WIDTH = 192
QKV = 960
BLOCK = 256

norm_epsilon = 1e-05
adam_epsilon = 1e-08
beta_first = 0.9
beta_second = 0.999
weight_decay = 0.1
rate_matrix = 0.05
rate_gain = 0.5
clip_limit = 1.0
rotary_base = 10000.0
masked_value = -1e30

F32 = jnp.float32
BF16 = jnp.bfloat16
SHORT = pl.CostEstimate(flops=1_000_000, transcendentals=0, bytes_accessed=100_000)


def rotary_tables(length):
    frequency = np.float32(rotary_base) ** (
        np.float32(-2.0) * np.arange(HALF, dtype=np.float32) / np.float32(HEAD_DIM)
    )
    angles = np.arange(length, dtype=np.float32)[None, :] * frequency.astype(np.float32)[:, None]
    return jnp.asarray(np.cos(angles), F32), jnp.asarray(np.sin(angles), F32)


def dot(left, right, left_dim=1, right_dim=0):
    return lax.dot_general(
        left, right, (((left_dim,), (right_dim,)), ((), ())), preferred_element_type=F32
    )


def inverse_root(values):
    return lax.rsqrt(jnp.mean(values * values, axis=0, keepdims=True) + norm_epsilon)


def joined(own, other, place):
    first = place == 0
    return jnp.concatenate(
        [jnp.where(first, own, other), jnp.where(first, other, own)], axis=1
    )


def lane_sums(values):
    lanes = 128
    total = values[:, :lanes]
    for low in range(lanes, values.shape[1], lanes):
        total = total + values[:, low : low + lanes]
    return total


def norm_backward(grad_normed, normal, inverse, gain):
    scaled = grad_normed * gain
    return inverse * (scaled - normal * jnp.mean(scaled * normal, axis=0, keepdims=True))


def visible_scores(scores, start_row, place_row, low, key_low):
    inside = low >= 256 and low + BLOCK <= 768 and key_low >= 256
    if inside and key_low < low:
        return scores
    place = lax.broadcasted_iota(jnp.int32, scores.shape, 0) + key_low
    if inside:
        seen = place <= place_row
    else:
        seen = place >= start_row
        if key_low >= low:
            seen = seen & (place <= place_row)
    return jnp.where(seen, scores, masked_value)


def triple(row):
    return jnp.concatenate([row] * RATIO, axis=1)


def turn(rows, cosine, sine):
    front, behind = rows[:HALF], rows[HALF:]
    return jnp.concatenate([front * cosine - behind * sine, behind * cosine + front * sine], axis=0)


def turn_back(rows, cosine, sine):
    front, behind = rows[:HALF], rows[HALF:]
    return jnp.concatenate([front * cosine + behind * sine, behind * cosine - front * sine], axis=0)


def attention_forward_body(
    info_ref,
    own_ref,
    other_ref,
    start_ref,
    pieces_own_ref,
    pieces_other_ref,
    gain_ref,
    cosine_ref,
    sine_ref,
    residual_ref,
    query_ref,
    key_ref,
    value_ref,
    mixed_ref,
    total_ref,
    normed_ref,
    weight_ref,
    out_weight_ref,
    out_rows,
    key_rows,
    x_across,
):
    @pl.when(pl.program_id(0) == 0)
    def _():
        chunks, rows, _ = pieces_own_ref.shape
        for chunk in range(2 * chunks):
            index = info_ref[1 + chunk]
            is_own = index < chunks
            index = jnp.where(is_own, index, index - chunks)
            part = jnp.where(is_own, pieces_own_ref[index], pieces_other_ref[index])
            low = chunk * rows
            if low < QKV:
                weight_ref[low : low + rows] = part
            else:
                out_weight_ref[low - QKV : low - QKV + rows] = part
        out_rows[...] = out_weight_ref[...].T

    x = joined(own_ref[0], other_ref[0], info_ref[0])
    length = x.shape[1]
    x_across[...] = x
    x = x.astype(F32)
    normed = (x * inverse_root(x) * gain_ref[:, 0:1]).astype(BF16)
    cosine = cosine_ref[...]
    sine = sine_ref[...]
    normed_ref[0] = normed
    projected = dot(weight_ref[...], normed)
    for head in range(HEADS):
        rows = slice(head * 64, head * 64 + 64)
        query_ref[0, rows] = (turn(projected[rows], cosine, sine) * HEAD_DIM ** (-0.5)).astype(
            BF16
        )
    for head in range(KV_HEADS):
        rows = slice(head * 64, head * 64 + 64)
        rotated = turn(projected[D + head * 64 : D + head * 64 + 64], cosine, sine)
        key_ref[0, rows] = rotated.astype(BF16)
        key_rows[head] = rotated.T.astype(BF16)
    value_ref[0] = projected[D + KV_WIDTH :].astype(BF16)

    def score(member, block, r):
        low, high = block * BLOCK, (block + 1) * BLOCK
        row = (member * RATIO + r) * 64
        return dot(key_rows[member, 0:high], query_ref[0, row : row + 64, low:high])

    def finish(member, block, r, scores):
        low, high = block * BLOCK, (block + 1) * BLOCK
        start_row = start_ref[0, 0:1, low:high]
        place_row = lax.broadcasted_iota(jnp.int32, (1, BLOCK), 1) + low
        scores = [
            visible_scores(scores[k : k + BLOCK], start_row, place_row, low, k)
            for k in range(0, high, BLOCK)
        ]
        top = functools.reduce(
            jnp.maximum, [jnp.max(part, axis=0, keepdims=True) for part in scores]
        )
        exponents = [jnp.exp(part - top) for part in scores]
        total = sum(jnp.sum(part, axis=0, keepdims=True) for part in exponents)
        exponent = jnp.concatenate([part.astype(BF16) for part in exponents], axis=0)
        mixed = dot(value_ref[0, member * 64 : member * 64 + 64, 0:high], exponent)
        row = (member * RATIO + r) * 64
        mixed_ref[0, row : row + 64, low:high] = (mixed * (1.0 / total)).astype(BF16)
        total_ref[0, member, r : r + 1, low:high] = top + jnp.log(total)

    items = [
        (member, block, r)
        for member in range(KV_HEADS)
        for block in range(length // BLOCK)
        for r in range(RATIO)
    ]
    ahead = [score(*item) for item in items[:2]]
    for i, item in enumerate(items):
        if i + 2 < len(items):
            ahead.append(score(*items[i + 2]))
        finish(*item, ahead.pop(0))
    residual_ref[0] = x_across[...].astype(F32) + dot(out_rows[...], mixed_ref[0])


def whole(shape):
    return pl.BlockSpec(
        tuple(shape), lambda *_: (0,) * len(shape), pipeline_mode=pl.Buffered(1)
    )


def step_spec(shape):
    return pl.BlockSpec((1,) + tuple(shape[1:]), lambda i, info: (i,) + (0,) * (len(shape) - 1))


def params(mebibytes):
    return pltpu.CompilerParams(
        dimension_semantics=("arbitrary",), vmem_limit_bytes=mebibytes * 2**20
    )


def attention_forward(info, own, other, start, pieces_own, pieces_other, gain, tables):
    count = other.shape[0]
    length = 2 * other.shape[2]
    outs = [
        ((count, D, length), F32),
        ((count, D, length), BF16),
        ((count, KV_WIDTH, length), BF16),
        ((count, KV_WIDTH, length), BF16),
        ((count, D, length), BF16),
        ((count, KV_HEADS, 8, length), F32),
        ((count, D, length), BF16),
    ]
    weights = (QKV, D), (D, D)
    return pl.pallas_call(
        attention_forward_body,
        grid_spec=pltpu.PrefetchScalarGridSpec(
            num_scalar_prefetch=1,
            grid=(count,),
            in_specs=[
                pl.BlockSpec(
                    (1,) + own.shape[1:], lambda i, info: (info[0] * count + i, 0, 0)
                ),
                step_spec(other.shape),
                step_spec(start.shape),
                whole(pieces_own.shape),
                whole(pieces_other.shape),
                whole(gain.shape),
                whole((HALF, length)),
                whole((HALF, length)),
            ],
            out_specs=[step_spec(shape) for shape, _ in outs] + [whole(shape) for shape in weights],
            scratch_shapes=[
                pltpu.VMEM((D, D), BF16),
                pltpu.VMEM((KV_HEADS, length, HEAD_DIM), BF16),
                pltpu.VMEM((D, length), BF16),
            ],
        ),
        out_shape=[jax.ShapeDtypeStruct(shape, kind) for shape, kind in outs]
        + [jax.ShapeDtypeStruct(shape, BF16) for shape in weights],
        compiler_params=params(44),
        cost_estimate=pl.CostEstimate(
            flops=8_000_000_000, transcendentals=12_000_000, bytes_accessed=20_000_000
        ),
        name="attention_forward",
    )(info, own, other, start, pieces_own, pieces_other, gain, *tables)


def stacked(refs, kinds):
    parts = [ref[:, kind].reshape(-1, D) for kind in kinds for ref in refs]
    return jnp.concatenate(parts, axis=0) if len(parts) > 1 else parts[0]


def feed_body(part_count, info_ref, residual_ref, cotangent_own_ref, cotangent_other_ref, *refs):
    weight_refs = refs[:part_count], refs[part_count : 2 * part_count]
    (
        gain_ref,
        out_own_ref,
        out_other_ref,
        back_ref,
        gain_grad_ref,
        grad_own_ref,
        grad_other_ref,
        sums,
        gain_sums,
    ) = refs[2 * part_count :]
    step = pl.program_id(0)
    units = sums.shape[2] // 3
    residual = residual_ref[0]
    cotangent = jnp.where(step % 2 == 0, cotangent_own_ref[0], cotangent_other_ref[0])
    gain = gain_ref[:, 1:2]
    inverse = inverse_root(residual)
    normal = residual * inverse
    normed = (normal * gain).astype(BF16)

    @pl.when(step == 0)
    def _():
        sums[...] = jnp.zeros_like(sums)
        gain_sums[...] = jnp.zeros_like(gain_sums)

    out = residual
    grad_normed = jnp.zeros_like(residual)
    for part, parts in enumerate(weight_refs):
        pair = stacked(parts, (0, 1))
        down = stacked(parts, (2,))
        both = dot(pair, normed)
        gate, upward = both[:units], both[units:]
        grad_hidden = dot(down, cotangent)
        sigmoid_gate = jax.nn.sigmoid(gate)
        swish = gate * sigmoid_gate
        hidden = (swish * upward).astype(BF16)
        grad_gate = (
            grad_hidden * upward * (sigmoid_gate + swish * (1.0 - sigmoid_gate))
        ).astype(BF16)
        grad_upward = (grad_hidden * swish).astype(BF16)
        grads = jnp.concatenate([grad_gate, grad_upward], axis=0)
        out = out + dot(down, hidden, 0, 0)
        grad_normed = grad_normed + dot(pair, grads, 0, 0)
        sums[part, :, : 2 * units] += dot(normed, grads, 1, 1)
        sums[part, :, 2 * units :] += dot(cotangent, hidden, 1, 1)

    out = out.astype(BF16)

    @pl.when(step % 2 == 0)
    def _():
        out_own_ref[0] = out

    @pl.when(step % 2 == 1)
    def _():
        out_other_ref[0] = out

    gain_sums[...] += lane_sums(grad_normed * normal)
    back_ref[0] = (
        cotangent.astype(F32) + norm_backward(grad_normed, normal, inverse, gain)
    ).astype(BF16)

    @pl.when(step == pl.num_programs(0) - 1)
    def _():
        pieces, kinds, rows, _ = grad_own_ref.shape
        for part, grad_ref in enumerate((grad_own_ref, grad_other_ref)):
            for kind in range(kinds):
                flipped = sums[part, :, kind * units : (kind + 1) * units].astype(BF16).T
                for piece in range(pieces):
                    grad_ref[piece, kind] = flipped[piece * rows : (piece + 1) * rows]
        gain_grad_ref[...] = jnp.sum(gain_sums[...].T, axis=0, keepdims=True)


def feed_forward(info, residual, cotangent_own, cotangent_other, weights, gain, pieces):
    count, _, length = residual.shape
    half = length // 2
    part_count = len(weights) // 2
    units = sum(part.size // (3 * D) for part in weights[:part_count])
    block = (1, D, half)
    full = pl.BlockSpec(block, lambda i, info: (i // 2, 0, (i + info[0]) % 2))
    own = pl.BlockSpec(block, lambda i, info: (info[0] * count + i // 2, 0, 0))
    other = pl.BlockSpec(block, lambda i, info: (i // 2, 0, 0))
    grad_shape = (pieces, 3, units // pieces, D)
    resident = pl.BlockSpec(memory_space=pltpu.VMEM)
    return pl.pallas_call(
        functools.partial(feed_body, part_count),
        grid_spec=pltpu.PrefetchScalarGridSpec(
            num_scalar_prefetch=1,
            grid=(2 * count,),
            in_specs=[full, own, other]
            + [whole(weight.shape) for weight in weights]
            + [whole(gain.shape)],
            out_specs=[own, other, full, whole((1, D))] + [resident] * 2,
            scratch_shapes=[
                pltpu.VMEM((2, D, 3 * units), F32),
                pltpu.VMEM((D, 128), F32),
            ],
        ),
        out_shape=[
            jax.ShapeDtypeStruct(cotangent_own.shape, BF16),
            jax.ShapeDtypeStruct(cotangent_other.shape, BF16),
            jax.ShapeDtypeStruct(residual.shape, BF16),
            jax.ShapeDtypeStruct((1, D), F32),
        ]
        + [jax.ShapeDtypeStruct(grad_shape, BF16)] * 2,
        compiler_params=params(42),
        cost_estimate=pl.CostEstimate(
            flops=32_000_000_000, transcendentals=6_000_000, bytes_accessed=30_000_000
        ),
        name="feed_forward",
    )(info, residual, cotangent_own, cotangent_other, *weights, gain)


def branch_backward_body(
    grad_ref, mixed_ref, weight_ref, grad_mixed_ref, inner_ref, weight_grad_ref
):
    @pl.when(pl.program_id(0) == 0)
    def _():
        weight_grad_ref[...] = jnp.zeros_like(weight_grad_ref)

    branch = grad_ref[0]
    grad_mixed = dot(weight_ref[...], branch).astype(BF16)
    grad_mixed_ref[0] = grad_mixed
    for head in range(HEADS):
        rows = slice(head * 64, head * 64 + 64)
        inner_ref[0, head // RATIO, head % RATIO : head % RATIO + 1] = jnp.sum(
            grad_mixed[rows].astype(F32) * mixed_ref[0, rows].astype(F32), axis=0, keepdims=True
        )
    weight_grad_ref[...] += dot(mixed_ref[0], branch, 1, 1)


def branch_backward(grad, mixed, weight):
    count, _, length = grad.shape

    half = length // 2
    step = pl.BlockSpec((1, D, half), lambda i: (i // 2, 0, i % 2))
    inner = (count, KV_HEADS, 8, length)
    return pl.pallas_call(
        branch_backward_body,
        grid=(2 * count,),
        in_specs=[step, step, whole(weight.shape)],
        out_specs=[
            step,
            pl.BlockSpec((1, KV_HEADS, 8, half), lambda i: (i // 2, 0, 0, i % 2)),
            whole((D, D)),
        ],
        out_shape=[
            jax.ShapeDtypeStruct(mixed.shape, BF16),
            jax.ShapeDtypeStruct(inner, F32),
            jax.ShapeDtypeStruct((D, D), F32),
        ],
        compiler_params=params(8),
        cost_estimate=SHORT,
        name="branch_backward",
    )(grad, mixed, weight)


def attention_backward_body(
    info_ref,
    normed_ref,
    start_ref,
    gain_row_ref,
    weight_hbm,
    out_grad_hbm,
    gain_second_ref,
    cosine_ref,
    sine_ref,
    query_ref,
    key_ref,
    value_ref,
    total_ref,
    grad_ref,
    inner_ref,
    projected_ref,
    kept_ref,
    sent_ref,
    key_rows,
    value_rows,
    grad_key,
    grad_value,
    weight_sums,
    weight_ref,
    out_grad_ref,
    semaphores,
):
    step = pl.program_id(0)
    copies = [
        pltpu.make_async_copy(weight_hbm, weight_ref, semaphores.at[0]),
        pltpu.make_async_copy(out_grad_hbm, out_grad_ref, semaphores.at[1]),
    ]

    @pl.when(step == 0)
    def _():
        for copy in copies:
            copy.start()

    length = query_ref.shape[2]
    cosine = cosine_ref[...]
    sine = sine_ref[...]
    for head in range(KV_HEADS):
        rows = slice(head * 64, head * 64 + 64)
        key_rows[head] = key_ref[0, rows].T
        value_rows[head] = value_ref[0, rows].T

    def head_rows(member, r):
        return slice((member * RATIO + r) * 64, (member * RATIO + r) * 64 + 64)

    def products(member, low, key_low, r):
        keys = slice(key_low, key_low + 256)
        rows = head_rows(member, r)
        return (
            dot(key_rows[member, keys], query_ref[0, rows, low : low + BLOCK]),
            dot(value_rows[member, keys], grad_ref[0, rows, low : low + BLOCK]),
        )

    def weighted(member, low, key_low, r, scores, grad_weights):
        lanes = slice(low, low + BLOCK)
        start_row = start_ref[0, 0:1, lanes]
        place_row = lax.broadcasted_iota(jnp.int32, (1, BLOCK), 1) + low
        scores = visible_scores(scores, start_row, place_row, low, key_low)
        weights = jnp.exp(scores - total_ref[0, member, r : r + 1, lanes])
        grad_scores = weights * (grad_weights - inner_ref[0, member, r : r + 1, lanes])
        return weights.astype(BF16), grad_scores.astype(BF16)

    items = [
        (member, low, key_low, r)
        for member in range(KV_HEADS)
        for low in range(0, length, BLOCK)
        for key_low in range(0, low + BLOCK, 256)
        for r in range(RATIO)
    ]
    ahead = [products(*item) for item in items[:2]]
    sums = {}

    def add(key, value):
        sums[key] = sums[key] + value if key in sums else value

    for i, item in enumerate(items):
        member, low, key_low, r = item
        if i + 2 < len(items):
            ahead.append(products(*items[i + 2]))
        weights, grad_scores = weighted(*item, *ahead.pop(0))
        rows = head_rows(member, r)
        keys = slice(key_low, key_low + 256)
        add("value", dot(grad_ref[0, rows, low : low + BLOCK], weights, 1, 1))
        add("key", dot(query_ref[0, rows, low : low + BLOCK], grad_scores, 1, 1))
        add(r, dot(key_ref[0, member * 64 : member * 64 + 64, keys], grad_scores))
        if r == RATIO - 1:
            for name, ref in (("value", grad_value), ("key", grad_key)):
                part = sums.pop(name)
                if key_low - key_low % BLOCK == low:
                    ref[member, :, keys] = part
                else:
                    ref[member, :, keys] += part
        if key_low + 256 == low + BLOCK:
            projected_ref[0, rows, low : low + BLOCK] = turn_back(
                sums.pop(r) * HEAD_DIM ** (-0.5),
                cosine[:, low : low + BLOCK],
                sine[:, low : low + BLOCK],
            ).astype(BF16)
    for member in range(KV_HEADS):
        row = D + member * 64
        projected_ref[0, row : row + 64] = turn_back(grad_key[member], cosine, sine).astype(BF16)
        row += KV_WIDTH
        projected_ref[0, row : row + 64] = grad_value[member].astype(BF16)

    product = dot(projected_ref[0], normed_ref[0], 1, 1)

    @pl.when(step == 0)
    def _():
        weight_sums[...] = product

    @pl.when(step > 0)
    def _():
        weight_sums[...] += product

    @pl.when(step == pl.num_programs(0) - 1)
    def _():
        for copy in copies:
            copy.wait()
        rows = 48
        pairs = (QKV + D) // (2 * rows)
        first = info_ref[0] == 0
        gain_sums = jnp.zeros((rows, D), F32)
        for pair in range(pairs):
            low = pair * 2 * rows
            if low < QKV:
                even, odd = weight_sums[low : low + rows], weight_sums[low + rows : low + 2 * rows]
                gain_sums = gain_sums + even * weight_ref[low : low + rows].astype(F32)
                gain_sums = gain_sums + odd * weight_ref[low + rows : low + 2 * rows].astype(F32)
            else:
                low -= QKV
                even = out_grad_ref[low : low + rows]
                odd = out_grad_ref[low + rows : low + 2 * rows]
            even, odd = even.astype(BF16), odd.astype(BF16)
            piece = info_ref[1 + 2 * pairs + pair]
            target = pl.ds(pl.multiple_of(info_ref[1 + 3 * pairs + pair], 16), rows)
            kept_ref[piece, target] = jnp.where(first, even, odd)
            sent_ref[piece, target] = jnp.where(first, odd, even)
        gain_first = jnp.sum(gain_sums, axis=0, keepdims=True) / gain_row_ref[0:1]
        tail = jnp.concatenate(
            [gain_first, gain_second_ref[...], jnp.zeros((14, D), F32)], axis=0
        ).astype(BF16)
        pieces, held, _ = kept_ref.shape
        for piece in range(pieces):
            kept_ref[piece, held - 16 :] = tail
            sent_ref[piece, held - 16 :] = tail


def attention_backward(
    info, normed, start, gain_rows, weight, out_grad, gain_second, tables, parts, pieces
):
    count, _, length = normed.shape
    held = (pieces, (QKV + D) // (2 * pieces) + 16, D)
    projected = (count, QKV, length)
    before, after = [gain_rows], [gain_second, *tables]
    return pl.pallas_call(
        attention_backward_body,
        grid_spec=pltpu.PrefetchScalarGridSpec(
            num_scalar_prefetch=1,
            grid=(count,),
            in_specs=[
                step_spec(normed.shape),
                step_spec(start.shape),
            ]
            + [whole(part.shape) for part in before]
            + [pl.BlockSpec(memory_space=pl.ANY)] * 2
            + [whole(part.shape) for part in after]
            + [step_spec(part.shape) for part in parts],
            out_specs=[step_spec(projected)] + [whole(held)] * 2,
            scratch_shapes=[
                pltpu.VMEM((KV_HEADS, length, HEAD_DIM), BF16),
                pltpu.VMEM((KV_HEADS, length, HEAD_DIM), BF16),
                pltpu.VMEM((KV_HEADS, HEAD_DIM, length), F32),
                pltpu.VMEM((KV_HEADS, HEAD_DIM, length), F32),
                pltpu.VMEM((QKV, D), F32),
                pltpu.VMEM(weight.shape, BF16),
                pltpu.VMEM(out_grad.shape, F32),
                pltpu.SemaphoreType.DMA((2,)),
            ],
        ),
        out_shape=[jax.ShapeDtypeStruct(projected, BF16)]
        + [jax.ShapeDtypeStruct(held, BF16)] * 2,
        compiler_params=params(28),
        cost_estimate=pl.CostEstimate(
            flops=9_000_000_000, transcendentals=6_000_000, bytes_accessed=15_000_000
        ),
        name="attention_backward",
    )(info, normed, start, *before, weight, out_grad, *after, *parts)


def input_grads_body(
    info_ref,
    own_ref,
    other_ref,
    gain_ref,
    projected_ref,
    weight_ref,
    grad_ref,
    tokens_own_ref,
    tokens_other_ref,
):
    step = pl.program_id(0)
    x = jnp.where(step % 2 == 0, own_ref[0], other_ref[0]).astype(F32)
    gain = gain_ref[:, 0:1]
    inverse = inverse_root(x)
    normal = x * inverse
    grad_normed = dot(weight_ref[...], projected_ref[0], 0, 0)
    grad_x = grad_ref[0].astype(F32) + norm_backward(grad_normed, normal, inverse, gain)

    @pl.when(step % 2 == 0)
    def _():
        tokens_own_ref[0] = grad_x

    @pl.when(step % 2 == 1)
    def _():
        tokens_other_ref[0] = grad_x.astype(BF16)


def input_grads(info, own, other, gain, projected, weight, grad):
    count = other.shape[0]
    half = other.shape[2]
    own_spec = pl.BlockSpec((1, D, half), lambda i, info: (info[0] * count + i // 2, 0, 0))
    other_spec = pl.BlockSpec((1, D, half), lambda i, info: (i // 2, 0, 0))

    def full(height):
        return pl.BlockSpec((1, height, half), lambda i, info: (i // 2, 0, (i + info[0]) % 2))

    return pl.pallas_call(
        input_grads_body,
        grid_spec=pltpu.PrefetchScalarGridSpec(
            num_scalar_prefetch=1,
            grid=(2 * count,),
            in_specs=[
                own_spec,
                other_spec,
                whole(gain.shape),
                full(QKV),
                whole(weight.shape),
                full(D),
            ],
            out_specs=[own_spec, other_spec],
        ),
        out_shape=[
            jax.ShapeDtypeStruct(own.shape, F32),
            jax.ShapeDtypeStruct(other.shape, BF16),
        ],
        compiler_params=params(16),
        cost_estimate=SHORT,
        name="input_grads",
    )(info, own, other, gain, projected, weight, grad)


def factors(count):
    inner = 1 << ((count.bit_length() - 1) // 2)
    return count // inner, inner


def partner(values, mask):
    count = lax.axis_size("wide")
    return lax.ppermute(values, "wide", [(i, i ^ mask) for i in range(count)])


def across(values):
    return lax.ppermute(values, "narrow", [(0, 1), (1, 0)])


def in_order(parts, place):
    bit = 1
    while bit < len(parts):
        swap = (place & bit) != 0
        parts = [jnp.where(swap, parts[i ^ bit], part) for i, part in enumerate(parts)]
        bit *= 2
    return parts


def add_all(parts):
    parts = [part.astype(F32) for part in parts]
    while len(parts) > 1:
        parts = [parts[i] + parts[i + 1] for i in range(0, len(parts), 2)]
    return parts[0]


def adamw_update(master, first_state, second_state, gradient, factor, step_rate, decay_rate):
    clipped = gradient * factor
    first_new = beta_first * first_state + (1.0 - beta_first) * clipped
    second_new = beta_second * second_state + (1.0 - beta_second) * clipped * clipped
    first_hat = first_new / (1.0 - beta_first**STEP)
    second_hat = second_new / (1.0 - beta_second**STEP)
    master_new = master * (1.0 - step_rate * decay_rate) - step_rate * first_hat / (
        jnp.sqrt(second_hat) + adam_epsilon
    )
    return (master_new, first_new, second_new)


def squares_body(count, rows, *refs):
    attention_ref, gain_ref, feedforward_ref, sent_ref = refs[2 * count :]
    attention = add_all([ref[...] for ref in refs[:count]])
    feedforward = add_all([ref[...] for ref in refs[count : 2 * count]])
    owned = attention[:rows]
    attention_ref[...] = owned
    if attention.shape[0] > rows:
        gain_ref[...] = attention[rows : rows + 2]
    else:
        gain_ref[...] = jnp.zeros_like(gain_ref)
    feedforward_ref[...] = feedforward
    local = jnp.sum(owned * owned) + jnp.sum(feedforward * feedforward)
    sent_ref[...] = jnp.full(sent_ref.shape, local, F32)


def last_sums(attention, feedforward, rows, devices):
    parts = attention + feedforward
    shapes = [(rows, D), (2, D), feedforward[0].shape, (devices, 1, 128)]
    return pl.pallas_call(
        functools.partial(squares_body, len(attention), rows),
        in_specs=[pl.BlockSpec(memory_space=pltpu.VMEM) for _ in parts],
        out_specs=[pl.BlockSpec(memory_space=pltpu.VMEM) for _ in shapes],
        out_shape=[jax.ShapeDtypeStruct(shape, F32) for shape in shapes],
        compiler_params=pltpu.CompilerParams(vmem_limit_bytes=6 * 2**20),
        cost_estimate=SHORT,
        name="last_sums",
    )(*parts)


def update_body(squares_ref, *refs):
    grads, states, results, norm_ref = refs[:3], refs[3:12], refs[12:21], refs[21]
    gain_grad = grads[2][...]
    squares = jnp.sum(squares_ref[...], axis=0)[:, 0:1] + jnp.sum(gain_grad * gain_grad)
    norm = jnp.sqrt(squares)
    norm_ref[...] = norm
    factor = jnp.minimum(1.0, clip_limit / (norm + 1e-06))
    rates = (rate_matrix, weight_decay), (rate_matrix, weight_decay), (rate_gain, 0.0)
    for kind, (step_rate, decay_rate) in enumerate(rates):
        grad = grads[kind][...]
        scale = factor.reshape((1,) * grad.ndim)
        new = adamw_update(
            *[ref[...] for ref in states[3 * kind : 3 * kind + 3]],
            grad,
            scale,
            step_rate,
            decay_rate,
        )
        for ref, value in zip(results[3 * kind : 3 * kind + 3], new):
            ref[...] = value


def update(squares, grads, states):
    shapes = [state.shape for state in states] + [(1, 1)]
    return pl.pallas_call(
        update_body,
        in_specs=[pl.BlockSpec(memory_space=pltpu.VMEM) for _ in range(13)],
        out_specs=[pl.BlockSpec(memory_space=pltpu.VMEM) for _ in shapes],
        out_shape=[jax.ShapeDtypeStruct(shape, F32) for shape in shapes],
        compiler_params=pltpu.CompilerParams(vmem_limit_bytes=12 * 2**20),
        cost_estimate=SHORT,
        name="update",
    )(squares, *grads, *states)


def per_device(
    tokens,
    cotangent,
    documents,
    attention_master,
    attention_first,
    attention_second,
    feedforward_master,
    feedforward_first,
    feedforward_second,
    gain_master,
    gain_first,
    gain_second,
):
    seq_count, half_len, _ = tokens.shape
    own_count = seq_count // 2
    place = lax.axis_index("narrow")
    first = place == 0
    outer, inner = factors(lax.axis_size("wide"))
    wide_place = lax.axis_index("wide")
    outer_place, inner_place = wide_place // inner, wide_place % inner
    tables = rotary_tables(2 * half_len)
    gain_columns = gain_master.T
    x_own = jnp.swapaxes(tokens, 1, 2)
    cotangent_own = jnp.swapaxes(cotangent, 1, 2)

    def swap(tensor):
        return across(
            lax.dynamic_slice_in_dim(tensor, (1 - place) * own_count, own_count, 0)
        )

    x_other = swap(x_own)
    own_docs = lax.dynamic_slice_in_dim(documents, place * own_count, own_count, 0)
    start = jnp.zeros_like(own_docs)
    for number in (1, 2):
        before = jnp.sum((own_docs < number).astype(jnp.int32), axis=1, keepdims=True)
        start = jnp.where(own_docs == number, before, start)
    start = start[:, None, :]

    rows = attention_master.shape[0]
    aligned = rows % 16 == 0
    if aligned:
        chunk = jnp.arange(2 * inner * outer, dtype=jnp.int32)
        order = (
            ((chunk % 2) ^ place) * inner + ((chunk // 2 % inner) ^ inner_place)
        ) * outer + ((chunk // (2 * inner)) ^ outer_place)
        pair = chunk[: inner * outer]
        piece_of = (pair % inner) ^ inner_place
        row_of = ((pair // inner) ^ outer_place) * rows
        grad_pieces = inner
    else:
        order = jnp.arange(32, dtype=jnp.int32)
        piece_of = jnp.zeros((16,), jnp.int32)
        row_of = jnp.arange(16, dtype=jnp.int32) * 48
        grad_pieces = 1
    info = jnp.concatenate(
        [jnp.full((1,), place), order, piece_of, row_of]
    ).astype(jnp.int32)

    piece = attention_master.astype(BF16)
    parts = [piece] + [partner(piece, k * inner) for k in range(1, outer)]
    stack = jnp.stack(parts if aligned else in_order(parts, outer_place))
    feed_piece = feedforward_master.astype(BF16)
    feed_outer = jnp.stack(
        [feed_piece] + [partner(feed_piece, k * inner) for k in range(1, outer)]
    )
    parts = [stack] + [partner(stack, k) for k in range(1, inner)]
    feed_outer, parts[1:], info, start, gain_columns = lax.optimization_barrier(
        (feed_outer, parts[1:], info, start, gain_columns)
    )
    feed_parts = [feed_outer] + [partner(feed_outer, k) for k in range(1, inner)]
    if aligned:
        stack = jnp.stack(parts)
        pieces_own = stack.reshape(-1, rows, D)
        pieces_other = across(stack).reshape(-1, rows, D)
    else:
        stack = jnp.stack(in_order(parts, inner_place), axis=1)
        pieces = jnp.stack(in_order([stack, across(stack)], place), axis=2).reshape(-1, 48, D)
        pieces_own, pieces_other = pieces[:16], pieces[16:]
    cotangent_other = swap(cotangent_own)

    residual, query, key, value, mixed, total, normed, weight_qkv, weight_out = attention_forward(
        info, x_own, x_other, start, pieces_own, pieces_other, gain_columns, tables
    )
    feed_parts, residual = lax.optimization_barrier((feed_parts, residual))
    if aligned:
        feed_weights = feed_parts + [across(part) for part in feed_parts]
    else:
        stack = jnp.stack(feed_parts)
        feed_weights = [
            jnp.swapaxes(part.reshape(-1, 3, rows, D), 0, 1).reshape(1, 3, -1, D)
            for part in (stack, across(stack))
        ]
    outputs, out_other, back, gain_second_part, own_grad, other_grad = feed_forward(
        info, residual, cotangent_own, cotangent_other, feed_weights, gain_columns, inner
    )

    def place_other(whole_array, received):
        return lax.dynamic_update_slice_in_dim(
            whole_array, received.astype(whole_array.dtype), (1 - place) * own_count, 0
        )

    out_received = across(out_other)

    received = across(other_grad)
    grad_mixed, inner_sums, out_grad = branch_backward(back, mixed, weight_out)
    received, own_grad, grad_mixed = lax.optimization_barrier((received, own_grad, grad_mixed))
    feed_sums = [add_all([own_grad[k], received[k]]).astype(BF16) for k in range(inner)]
    feed_sums, grad_mixed = lax.optimization_barrier((feed_sums, grad_mixed))
    feed_got = [feed_sums[0]] + [partner(feed_sums[k], k) for k in range(1, inner)]
    projected, kept, sent = attention_backward(
        info,
        normed,
        start,
        gain_master,
        weight_qkv,
        out_grad,
        gain_second_part,
        tables,
        [query, key, value, total, grad_mixed, inner_sums],
        grad_pieces,
    )
    feed_got, kept, sent = lax.optimization_barrier((feed_got, kept, sent))
    summed = add_all(feed_got).astype(BF16).reshape(3, outer, -1, D)
    feed_last = [summed[:, k] for k in range(outer)]
    feed_last, sent = lax.optimization_barrier((feed_last, sent))
    feed_last = [feed_last[0]] + [partner(feed_last[k], k * inner) for k in range(1, outer)]

    received = across(sent)
    if aligned:
        parts = [add_all([kept[k], received[k]]).astype(BF16) for k in range(inner)]
    else:
        gain_grad = lax.psum(kept[0, -16:-14].astype(F32), ("wide", "narrow"))
        total = add_all([kept, received]).astype(BF16)[0, :-16].reshape(outer, inner, rows, D)
        parts = in_order([total[:, k] for k in range(inner)], inner_place)
    parts, projected = lax.optimization_barrier((parts, projected))
    got = [parts[0]] + [partner(parts[k], k) for k in range(1, inner)]
    grad_own, grad_other = input_grads(
        info, x_own, x_other, gain_columns, projected, weight_qkv, back
    )
    got, feed_last, grad_other = lax.optimization_barrier((got, feed_last, grad_other))
    total = add_all(got).astype(BF16)
    if aligned:
        tail = total[outer * rows :]
        parts = [
            jnp.concatenate([total[k * rows : (k + 1) * rows], tail], axis=0)
            for k in range(outer)
        ]
    else:
        parts = in_order([total[k] for k in range(outer)], outer_place)
    last = [parts[0]] + [partner(parts[k], k * inner) for k in range(1, outer)]
    devices = lax.axis_size("wide") * lax.axis_size("narrow")
    attention_grad, gain_total, feedforward_grad, squares = last_sums(
        last, feed_last, rows, devices
    )
    if aligned:
        gain_grad = gain_total
    squares = lax.all_to_all(squares, ("wide", "narrow"), 0, 0, tiled=True)
    grad_received = across(grad_other)
    attention_grad, gain_grad, grad_received, out_received = lax.optimization_barrier(
        (attention_grad, gain_grad, grad_received, out_received)
    )
    grad_tokens = place_other(grad_own, grad_received)
    outputs = place_other(outputs, out_received)
    states = (
        attention_master,
        attention_first,
        attention_second,
        feedforward_master,
        feedforward_first,
        feedforward_second,
        gain_master,
        gain_first,
        gain_second,
    )
    *updated, grad_norm = update(squares, (attention_grad, feedforward_grad, gain_grad), states)
    outputs = jnp.swapaxes(outputs, 1, 2)
    grad_tokens = jnp.swapaxes(grad_tokens, 1, 2)
    return (outputs, grad_tokens, grad_norm.reshape(()), *updated)


def solution(mesh):
    sequences = P("wide", "narrow", None)
    attention = P(("wide", "narrow"), None)
    feedforward = P(None, ("narrow", "wide"), None)
    state = (attention,) * 3 + (feedforward,) * 3 + (P(),) * 3
    return jax.shard_map(
        per_device,
        mesh=mesh,
        in_specs=(sequences, sequences, P("wide", None)) + state,
        out_specs=(sequences, sequences, P()) + state,
        check_vma=False,
    )
```

```python
import functools

import jax
import jax.numpy as jnp
import numpy as np
from jax import lax
from jax.experimental import pallas as pl
from jax.experimental.pallas import tpu as pltpu
from jax.sharding import PartitionSpec as P

D = 576
HEADS = 9
KV_HEADS = 3
RATIO = 3
HEAD_DIM = 64
HALF = 32
STEP = 10
KV_WIDTH = 192
QKV = 960
BLOCK = 256

norm_epsilon = 1e-05
adam_epsilon = 1e-08
beta_first = 0.9
beta_second = 0.999
weight_decay = 0.1
rate_matrix = 0.05
rate_gain = 0.5
clip_limit = 1.0
rotary_base = 10000.0
masked_value = -1e30

F32 = jnp.float32
BF16 = jnp.bfloat16
SHORT = pl.CostEstimate(flops=1_000_000, transcendentals=0, bytes_accessed=100_000)


def rotary_tables(length):
    frequency = np.float32(rotary_base) ** (
        np.float32(-2.0) * np.arange(HALF, dtype=np.float32) / np.float32(HEAD_DIM)
    )
    angles = np.arange(length, dtype=np.float32)[None, :] * frequency.astype(np.float32)[:, None]
    return jnp.asarray(np.cos(angles), F32), jnp.asarray(np.sin(angles), F32)


def dot(left, right, left_dim=1, right_dim=0):
    return lax.dot_general(
        left, right, (((left_dim,), (right_dim,)), ((), ())), preferred_element_type=F32
    )


def inverse_root(values):
    return lax.rsqrt(jnp.mean(values * values, axis=0, keepdims=True) + norm_epsilon)


def joined(own, other, place):
    first = place == 0
    return jnp.concatenate(
        [jnp.where(first, own, other), jnp.where(first, other, own)], axis=1
    )


def lane_sums(values):
    lanes = 128
    total = values[:, :lanes]
    for low in range(lanes, values.shape[1], lanes):
        total = total + values[:, low : low + lanes]
    return total


def norm_backward(grad_normed, normal, inverse, gain):
    scaled = grad_normed * gain
    return inverse * (scaled - normal * jnp.mean(scaled * normal, axis=0, keepdims=True))


def visible_scores(scores, start_row, place_row, low, key_low):
    inside = low >= 256 and low + BLOCK <= 768 and key_low >= 256
    if inside and key_low < low:
        return scores
    place = lax.broadcasted_iota(jnp.int32, scores.shape, 0) + key_low
    if inside:
        seen = place <= place_row
    else:
        seen = place >= start_row
        if key_low >= low:
            seen = seen & (place <= place_row)
    return jnp.where(seen, scores, masked_value)


def triple(row):
    return jnp.concatenate([row] * RATIO, axis=1)


def turn(rows, cosine, sine):
    front, behind = rows[:HALF], rows[HALF:]
    return jnp.concatenate([front * cosine - behind * sine, behind * cosine + front * sine], axis=0)


def turn_back(rows, cosine, sine):
    front, behind = rows[:HALF], rows[HALF:]
    return jnp.concatenate([front * cosine + behind * sine, behind * cosine - front * sine], axis=0)


def attention_forward_body(
    info_ref,
    own_ref,
    other_ref,
    start_ref,
    pieces_own_ref,
    pieces_other_ref,
    gain_ref,
    cosine_ref,
    sine_ref,
    residual_ref,
    query_ref,
    key_ref,
    value_ref,
    mixed_ref,
    total_ref,
    normed_ref,
    weight_ref,
    out_weight_ref,
    out_rows,
    key_rows,
    x_across,
):
    @pl.when(pl.program_id(0) == 0)
    def _():
        chunks, rows, _ = pieces_own_ref.shape
        for chunk in range(2 * chunks):
            index = info_ref[1 + chunk]
            is_own = index < chunks
            index = jnp.where(is_own, index, index - chunks)
            part = jnp.where(is_own, pieces_own_ref[index], pieces_other_ref[index])
            low = chunk * rows
            if low < QKV:
                weight_ref[low : low + rows] = part
            else:
                out_weight_ref[low - QKV : low - QKV + rows] = part
        out_rows[...] = out_weight_ref[...].T

    x = joined(own_ref[0], other_ref[0], info_ref[0])
    length = x.shape[1]
    x_across[...] = x
    x = x.astype(F32)
    normed = (x * inverse_root(x) * gain_ref[:, 0:1]).astype(BF16)
    cosine = cosine_ref[...]
    sine = sine_ref[...]
    normed_ref[0] = normed
    projected = dot(weight_ref[...], normed)
    for head in range(HEADS):
        rows = slice(head * 64, head * 64 + 64)
        query_ref[0, rows] = (turn(projected[rows], cosine, sine) * HEAD_DIM ** (-0.5)).astype(
            BF16
        )
    for head in range(KV_HEADS):
        rows = slice(head * 64, head * 64 + 64)
        rotated = turn(projected[D + head * 64 : D + head * 64 + 64], cosine, sine)
        key_ref[0, rows] = rotated.astype(BF16)
        key_rows[head] = rotated.T.astype(BF16)
    value_ref[0] = projected[D + KV_WIDTH :].astype(BF16)

    def score(member, block, r):
        low, high = block * BLOCK, (block + 1) * BLOCK
        row = (member * RATIO + r) * 64
        return dot(key_rows[member, 0:high], query_ref[0, row : row + 64, low:high])

    def finish(member, block, r, scores):
        low, high = block * BLOCK, (block + 1) * BLOCK
        start_row = start_ref[0, 0:1, low:high]
        place_row = lax.broadcasted_iota(jnp.int32, (1, BLOCK), 1) + low
        scores = [
            visible_scores(scores[k : k + BLOCK], start_row, place_row, low, k)
            for k in range(0, high, BLOCK)
        ]
        top = functools.reduce(
            jnp.maximum, [jnp.max(part, axis=0, keepdims=True) for part in scores]
        )
        exponents = [jnp.exp(part - top) for part in scores]
        total = sum(jnp.sum(part, axis=0, keepdims=True) for part in exponents)
        exponent = jnp.concatenate([part.astype(BF16) for part in exponents], axis=0)
        mixed = dot(value_ref[0, member * 64 : member * 64 + 64, 0:high], exponent)
        row = (member * RATIO + r) * 64
        mixed_ref[0, row : row + 64, low:high] = (mixed * (1.0 / total)).astype(BF16)
        total_ref[0, member, r : r + 1, low:high] = top + jnp.log(total)

    items = [
        (member, block, r)
        for member in range(KV_HEADS)
        for block in range(length // BLOCK)
        for r in range(RATIO)
    ]
    ahead = [score(*item) for item in items[:2]]
    for i, item in enumerate(items):
        if i + 2 < len(items):
            ahead.append(score(*items[i + 2]))
        finish(*item, ahead.pop(0))
    residual_ref[0] = x_across[...].astype(F32) + dot(out_rows[...], mixed_ref[0])


def whole(shape):
    return pl.BlockSpec(
        tuple(shape), lambda *_: (0,) * len(shape), pipeline_mode=pl.Buffered(1)
    )


def step_spec(shape):
    return pl.BlockSpec((1,) + tuple(shape[1:]), lambda i, info: (i,) + (0,) * (len(shape) - 1))


def params(mebibytes):
    return pltpu.CompilerParams(
        dimension_semantics=("arbitrary",), vmem_limit_bytes=mebibytes * 2**20
    )


def attention_forward(info, own, other, start, pieces_own, pieces_other, gain, tables):
    count = other.shape[0]
    length = 2 * other.shape[2]
    outs = [
        ((count, D, length), F32),
        ((count, D, length), BF16),
        ((count, KV_WIDTH, length), BF16),
        ((count, KV_WIDTH, length), BF16),
        ((count, D, length), BF16),
        ((count, KV_HEADS, 8, length), F32),
        ((count, D, length), BF16),
    ]
    weights = (QKV, D), (D, D)
    return pl.pallas_call(
        attention_forward_body,
        grid_spec=pltpu.PrefetchScalarGridSpec(
            num_scalar_prefetch=1,
            grid=(count,),
            in_specs=[
                pl.BlockSpec(
                    (1,) + own.shape[1:], lambda i, info: (info[0] * count + i, 0, 0)
                ),
                step_spec(other.shape),
                step_spec(start.shape),
                whole(pieces_own.shape),
                whole(pieces_other.shape),
                whole(gain.shape),
                whole((HALF, length)),
                whole((HALF, length)),
            ],
            out_specs=[step_spec(shape) for shape, _ in outs] + [whole(shape) for shape in weights],
            scratch_shapes=[
                pltpu.VMEM((D, D), BF16),
                pltpu.VMEM((KV_HEADS, length, HEAD_DIM), BF16),
                pltpu.VMEM((D, length), BF16),
            ],
        ),
        out_shape=[jax.ShapeDtypeStruct(shape, kind) for shape, kind in outs]
        + [jax.ShapeDtypeStruct(shape, BF16) for shape in weights],
        compiler_params=params(44),
        cost_estimate=pl.CostEstimate(
            flops=8_000_000_000, transcendentals=12_000_000, bytes_accessed=20_000_000
        ),
        name="attention_forward",
    )(info, own, other, start, pieces_own, pieces_other, gain, *tables)


def stacked(refs, kinds):
    parts = [ref[:, kind].reshape(-1, D) for kind in kinds for ref in refs]
    return jnp.concatenate(parts, axis=0) if len(parts) > 1 else parts[0]


def feed_body(part_count, info_ref, residual_ref, cotangent_own_ref, cotangent_other_ref, *refs):
    weight_refs = refs[:part_count], refs[part_count : 2 * part_count]
    (
        gain_ref,
        out_own_ref,
        out_other_ref,
        back_ref,
        gain_grad_ref,
        grad_own_ref,
        grad_other_ref,
        sums,
        gain_sums,
    ) = refs[2 * part_count :]
    step = pl.program_id(0)
    units = sums.shape[2] // 3
    residual = residual_ref[0]
    cotangent = jnp.where(step % 2 == 0, cotangent_own_ref[0], cotangent_other_ref[0])
    gain = gain_ref[:, 1:2]
    inverse = inverse_root(residual)
    normal = residual * inverse
    normed = (normal * gain).astype(BF16)

    @pl.when(step == 0)
    def _():
        sums[...] = jnp.zeros_like(sums)
        gain_sums[...] = jnp.zeros_like(gain_sums)

    out = residual
    grad_normed = jnp.zeros_like(residual)
    for part, parts in enumerate(weight_refs):
        pair = stacked(parts, (0, 1))
        down = stacked(parts, (2,))
        both = dot(pair, normed)
        gate, upward = both[:units], both[units:]
        grad_hidden = dot(down, cotangent)
        sigmoid_gate = jax.nn.sigmoid(gate)
        swish = gate * sigmoid_gate
        hidden = (swish * upward).astype(BF16)
        grad_gate = (
            grad_hidden * upward * (sigmoid_gate + swish * (1.0 - sigmoid_gate))
        ).astype(BF16)
        grad_upward = (grad_hidden * swish).astype(BF16)
        grads = jnp.concatenate([grad_gate, grad_upward], axis=0)
        out = out + dot(down, hidden, 0, 0)
        grad_normed = grad_normed + dot(pair, grads, 0, 0)
        sums[part, :, : 2 * units] += dot(normed, grads, 1, 1)
        sums[part, :, 2 * units :] += dot(cotangent, hidden, 1, 1)

    out = out.astype(BF16)

    @pl.when(step % 2 == 0)
    def _():
        out_own_ref[0] = out

    @pl.when(step % 2 == 1)
    def _():
        out_other_ref[0] = out

    gain_sums[...] += lane_sums(grad_normed * normal)
    back_ref[0] = (
        cotangent.astype(F32) + norm_backward(grad_normed, normal, inverse, gain)
    ).astype(BF16)

    @pl.when(step == pl.num_programs(0) - 1)
    def _():
        pieces, kinds, rows, _ = grad_own_ref.shape
        for part, grad_ref in enumerate((grad_own_ref, grad_other_ref)):
            for kind in range(kinds):
                flipped = sums[part, :, kind * units : (kind + 1) * units].astype(BF16).T
                for piece in range(pieces):
                    grad_ref[piece, kind] = flipped[piece * rows : (piece + 1) * rows]
        gain_grad_ref[...] = jnp.sum(gain_sums[...].T, axis=0, keepdims=True)


def feed_forward(info, residual, cotangent_own, cotangent_other, weights, gain, pieces):
    count, _, length = residual.shape
    half = length // 2
    part_count = len(weights) // 2
    units = sum(part.size // (3 * D) for part in weights[:part_count])
    block = (1, D, half)
    full = pl.BlockSpec(block, lambda i, info: (i // 2, 0, (i + info[0]) % 2))
    own = pl.BlockSpec(block, lambda i, info: (info[0] * count + i // 2, 0, 0))
    other = pl.BlockSpec(block, lambda i, info: (i // 2, 0, 0))
    grad_shape = (pieces, 3, units // pieces, D)
    resident = pl.BlockSpec(memory_space=pltpu.VMEM)
    return pl.pallas_call(
        functools.partial(feed_body, part_count),
        grid_spec=pltpu.PrefetchScalarGridSpec(
            num_scalar_prefetch=1,
            grid=(2 * count,),
            in_specs=[full, own, other]
            + [whole(weight.shape) for weight in weights]
            + [whole(gain.shape)],
            out_specs=[own, other, full, whole((1, D))] + [resident] * 2,
            scratch_shapes=[
                pltpu.VMEM((2, D, 3 * units), F32),
                pltpu.VMEM((D, 128), F32),
            ],
        ),
        out_shape=[
            jax.ShapeDtypeStruct(cotangent_own.shape, BF16),
            jax.ShapeDtypeStruct(cotangent_other.shape, BF16),
            jax.ShapeDtypeStruct(residual.shape, BF16),
            jax.ShapeDtypeStruct((1, D), F32),
        ]
        + [jax.ShapeDtypeStruct(grad_shape, BF16)] * 2,
        compiler_params=params(42),
        cost_estimate=pl.CostEstimate(
            flops=32_000_000_000, transcendentals=6_000_000, bytes_accessed=30_000_000
        ),
        name="feed_forward",
    )(info, residual, cotangent_own, cotangent_other, *weights, gain)


def branch_backward_body(
    grad_ref, mixed_ref, weight_ref, grad_mixed_ref, inner_ref, weight_grad_ref
):
    @pl.when(pl.program_id(0) == 0)
    def _():
        weight_grad_ref[...] = jnp.zeros_like(weight_grad_ref)

    branch = grad_ref[0]
    grad_mixed = dot(weight_ref[...], branch).astype(BF16)
    grad_mixed_ref[0] = grad_mixed
    for head in range(HEADS):
        rows = slice(head * 64, head * 64 + 64)
        inner_ref[0, head // RATIO, head % RATIO : head % RATIO + 1] = jnp.sum(
            grad_mixed[rows].astype(F32) * mixed_ref[0, rows].astype(F32), axis=0, keepdims=True
        )
    weight_grad_ref[...] += dot(mixed_ref[0], branch, 1, 1)


def branch_backward(grad, mixed, weight):
    count, _, length = grad.shape

    half = length // 2
    step = pl.BlockSpec((1, D, half), lambda i: (i // 2, 0, i % 2))
    inner = (count, KV_HEADS, 8, length)
    return pl.pallas_call(
        branch_backward_body,
        grid=(2 * count,),
        in_specs=[step, step, whole(weight.shape)],
        out_specs=[
            step,
            pl.BlockSpec((1, KV_HEADS, 8, half), lambda i: (i // 2, 0, 0, i % 2)),
            whole((D, D)),
        ],
        out_shape=[
            jax.ShapeDtypeStruct(mixed.shape, BF16),
            jax.ShapeDtypeStruct(inner, F32),
            jax.ShapeDtypeStruct((D, D), F32),
        ],
        compiler_params=params(8),
        cost_estimate=SHORT,
        name="branch_backward",
    )(grad, mixed, weight)


def attention_backward_body(
    info_ref,
    normed_ref,
    start_ref,
    gain_row_ref,
    weight_hbm,
    out_grad_hbm,
    gain_second_ref,
    cosine_ref,
    sine_ref,
    query_ref,
    key_ref,
    value_ref,
    total_ref,
    grad_ref,
    inner_ref,
    projected_ref,
    kept_ref,
    sent_ref,
    key_rows,
    value_rows,
    grad_key,
    grad_value,
    weight_sums,
    weight_ref,
    out_grad_ref,
    semaphores,
):
    step = pl.program_id(0)
    copies = [
        pltpu.make_async_copy(weight_hbm, weight_ref, semaphores.at[0]),
        pltpu.make_async_copy(out_grad_hbm, out_grad_ref, semaphores.at[1]),
    ]

    @pl.when(step == 0)
    def _():
        for copy in copies:
            copy.start()

    length = query_ref.shape[2]
    cosine = cosine_ref[...]
    sine = sine_ref[...]
    for head in range(KV_HEADS):
        rows = slice(head * 64, head * 64 + 64)
        key_rows[head] = key_ref[0, rows].T
        value_rows[head] = value_ref[0, rows].T

    def head_rows(member, r):
        return slice((member * RATIO + r) * 64, (member * RATIO + r) * 64 + 64)

    def products(member, low, key_low, r):
        keys = slice(key_low, key_low + 256)
        rows = head_rows(member, r)
        return (
            dot(key_rows[member, keys], query_ref[0, rows, low : low + BLOCK]),
            dot(value_rows[member, keys], grad_ref[0, rows, low : low + BLOCK]),
        )

    def weighted(member, low, key_low, r, scores, grad_weights):
        lanes = slice(low, low + BLOCK)
        start_row = start_ref[0, 0:1, lanes]
        place_row = lax.broadcasted_iota(jnp.int32, (1, BLOCK), 1) + low
        scores = visible_scores(scores, start_row, place_row, low, key_low)
        weights = jnp.exp(scores - total_ref[0, member, r : r + 1, lanes])
        grad_scores = weights * (grad_weights - inner_ref[0, member, r : r + 1, lanes])
        return weights.astype(BF16), grad_scores.astype(BF16)

    items = [
        (member, low, key_low, r)
        for member in range(KV_HEADS)
        for low in range(0, length, BLOCK)
        for key_low in range(0, low + BLOCK, 256)
        for r in range(RATIO)
    ]
    ahead = [products(*item) for item in items[:2]]
    sums = {}

    def add(key, value):
        sums[key] = sums[key] + value if key in sums else value

    for i, item in enumerate(items):
        member, low, key_low, r = item
        if i + 2 < len(items):
            ahead.append(products(*items[i + 2]))
        weights, grad_scores = weighted(*item, *ahead.pop(0))
        rows = head_rows(member, r)
        keys = slice(key_low, key_low + 256)
        add("value", dot(grad_ref[0, rows, low : low + BLOCK], weights, 1, 1))
        add("key", dot(query_ref[0, rows, low : low + BLOCK], grad_scores, 1, 1))
        add(r, dot(key_ref[0, member * 64 : member * 64 + 64, keys], grad_scores))
        if r == RATIO - 1:
            for name, ref in (("value", grad_value), ("key", grad_key)):
                part = sums.pop(name)
                if key_low - key_low % BLOCK == low:
                    ref[member, :, keys] = part
                else:
                    ref[member, :, keys] += part
        if key_low + 256 == low + BLOCK:
            projected_ref[0, rows, low : low + BLOCK] = turn_back(
                sums.pop(r) * HEAD_DIM ** (-0.5),
                cosine[:, low : low + BLOCK],
                sine[:, low : low + BLOCK],
            ).astype(BF16)
    for member in range(KV_HEADS):
        row = D + member * 64
        projected_ref[0, row : row + 64] = turn_back(grad_key[member], cosine, sine).astype(BF16)
        row += KV_WIDTH
        projected_ref[0, row : row + 64] = grad_value[member].astype(BF16)

    product = dot(projected_ref[0], normed_ref[0], 1, 1)

    @pl.when(step == 0)
    def _():
        weight_sums[...] = product

    @pl.when(step > 0)
    def _():
        weight_sums[...] += product

    @pl.when(step == pl.num_programs(0) - 1)
    def _():
        for copy in copies:
            copy.wait()
        rows = 48
        pairs = (QKV + D) // (2 * rows)
        first = info_ref[0] == 0
        gain_sums = jnp.zeros((rows, D), F32)
        for pair in range(pairs):
            low = pair * 2 * rows
            if low < QKV:
                even, odd = weight_sums[low : low + rows], weight_sums[low + rows : low + 2 * rows]
                gain_sums = gain_sums + even * weight_ref[low : low + rows].astype(F32)
                gain_sums = gain_sums + odd * weight_ref[low + rows : low + 2 * rows].astype(F32)
            else:
                low -= QKV
                even = out_grad_ref[low : low + rows]
                odd = out_grad_ref[low + rows : low + 2 * rows]
            even, odd = even.astype(BF16), odd.astype(BF16)
            piece = info_ref[1 + 2 * pairs + pair]
            target = pl.ds(pl.multiple_of(info_ref[1 + 3 * pairs + pair], 16), rows)
            kept_ref[piece, target] = jnp.where(first, even, odd)
            sent_ref[piece, target] = jnp.where(first, odd, even)
        gain_first = jnp.sum(gain_sums, axis=0, keepdims=True) / gain_row_ref[0:1]
        tail = jnp.concatenate(
            [gain_first, gain_second_ref[...], jnp.zeros((14, D), F32)], axis=0
        ).astype(BF16)
        pieces, held, _ = kept_ref.shape
        for piece in range(pieces):
            kept_ref[piece, held - 16 :] = tail
            sent_ref[piece, held - 16 :] = tail


def attention_backward(
    info, normed, start, gain_rows, weight, out_grad, gain_second, tables, parts, pieces
):
    count, _, length = normed.shape
    held = (pieces, (QKV + D) // (2 * pieces) + 16, D)
    projected = (count, QKV, length)
    before, after = [gain_rows], [gain_second, *tables]
    return pl.pallas_call(
        attention_backward_body,
        grid_spec=pltpu.PrefetchScalarGridSpec(
            num_scalar_prefetch=1,
            grid=(count,),
            in_specs=[
                step_spec(normed.shape),
                step_spec(start.shape),
            ]
            + [whole(part.shape) for part in before]
            + [pl.BlockSpec(memory_space=pl.ANY)] * 2
            + [whole(part.shape) for part in after]
            + [step_spec(part.shape) for part in parts],
            out_specs=[step_spec(projected)] + [pl.BlockSpec(memory_space=pltpu.VMEM)] * 2,
            scratch_shapes=[
                pltpu.VMEM((KV_HEADS, length, HEAD_DIM), BF16),
                pltpu.VMEM((KV_HEADS, length, HEAD_DIM), BF16),
                pltpu.VMEM((KV_HEADS, HEAD_DIM, length), F32),
                pltpu.VMEM((KV_HEADS, HEAD_DIM, length), F32),
                pltpu.VMEM((QKV, D), F32),
                pltpu.VMEM(weight.shape, BF16),
                pltpu.VMEM(out_grad.shape, F32),
                pltpu.SemaphoreType.DMA((2,)),
            ],
        ),
        out_shape=[jax.ShapeDtypeStruct(projected, BF16)]
        + [jax.ShapeDtypeStruct(held, BF16)] * 2,
        compiler_params=params(28),
        cost_estimate=pl.CostEstimate(
            flops=9_000_000_000, transcendentals=6_000_000, bytes_accessed=15_000_000
        ),
        name="attention_backward",
    )(info, normed, start, *before, weight, out_grad, *after, *parts)


def input_grads_body(
    info_ref,
    own_ref,
    other_ref,
    gain_ref,
    projected_ref,
    weight_ref,
    grad_ref,
    tokens_own_ref,
    tokens_other_ref,
):
    step = pl.program_id(0)
    x = jnp.where(step % 2 == 0, own_ref[0], other_ref[0]).astype(F32)
    gain = gain_ref[:, 0:1]
    inverse = inverse_root(x)
    normal = x * inverse
    grad_normed = dot(weight_ref[...], projected_ref[0], 0, 0)
    grad_x = grad_ref[0].astype(F32) + norm_backward(grad_normed, normal, inverse, gain)

    @pl.when(step % 2 == 0)
    def _():
        tokens_own_ref[0] = grad_x

    @pl.when(step % 2 == 1)
    def _():
        tokens_other_ref[0] = grad_x.astype(BF16)


def input_grads(info, own, other, gain, projected, weight, grad):
    count = other.shape[0]
    half = other.shape[2]
    own_spec = pl.BlockSpec((1, D, half), lambda i, info: (info[0] * count + i // 2, 0, 0))
    other_spec = pl.BlockSpec((1, D, half), lambda i, info: (i // 2, 0, 0))

    def full(height):
        return pl.BlockSpec((1, height, half), lambda i, info: (i // 2, 0, (i + info[0]) % 2))

    return pl.pallas_call(
        input_grads_body,
        grid_spec=pltpu.PrefetchScalarGridSpec(
            num_scalar_prefetch=1,
            grid=(2 * count,),
            in_specs=[
                own_spec,
                other_spec,
                whole(gain.shape),
                full(QKV),
                whole(weight.shape),
                full(D),
            ],
            out_specs=[own_spec, other_spec],
        ),
        out_shape=[
            jax.ShapeDtypeStruct(own.shape, F32),
            jax.ShapeDtypeStruct(other.shape, BF16),
        ],
        compiler_params=params(16),
        cost_estimate=SHORT,
        name="input_grads",
    )(info, own, other, gain, projected, weight, grad)


def factors(count):
    inner = 1 << ((count.bit_length() - 1) // 2)
    return count // inner, inner


def partner(values, mask):
    count = lax.axis_size("wide")
    return lax.ppermute(values, "wide", [(i, i ^ mask) for i in range(count)])


def across(values):
    return lax.ppermute(values, "narrow", [(0, 1), (1, 0)])


def in_order(parts, place):
    bit = 1
    while bit < len(parts):
        swap = (place & bit) != 0
        parts = [jnp.where(swap, parts[i ^ bit], part) for i, part in enumerate(parts)]
        bit *= 2
    return parts


def add_all(parts):
    parts = [part.astype(F32) for part in parts]
    while len(parts) > 1:
        parts = [parts[i] + parts[i + 1] for i in range(0, len(parts), 2)]
    return parts[0]


def adamw_update(master, first_state, second_state, gradient, factor, step_rate, decay_rate):
    clipped = gradient * factor
    first_new = beta_first * first_state + (1.0 - beta_first) * clipped
    second_new = beta_second * second_state + (1.0 - beta_second) * clipped * clipped
    first_hat = first_new / (1.0 - beta_first**STEP)
    second_hat = second_new / (1.0 - beta_second**STEP)
    master_new = master * (1.0 - step_rate * decay_rate) - step_rate * first_hat / (
        jnp.sqrt(second_hat) + adam_epsilon
    )
    return (master_new, first_new, second_new)


def squares_body(count, rows, *refs):
    attention_ref, gain_ref, feedforward_ref, sent_ref = refs[2 * count :]
    attention = add_all([ref[...] for ref in refs[:count]])
    feedforward = add_all([ref[...] for ref in refs[count : 2 * count]])
    owned = attention[:rows]
    attention_ref[...] = owned
    if attention.shape[0] > rows:
        gain_ref[...] = attention[rows : rows + 2]
    else:
        gain_ref[...] = jnp.zeros_like(gain_ref)
    feedforward_ref[...] = feedforward
    local = jnp.sum(owned * owned) + jnp.sum(feedforward * feedforward)
    sent_ref[...] = jnp.full(sent_ref.shape, local, F32)


def last_sums(attention, feedforward, rows, devices):
    parts = attention + feedforward
    shapes = [(rows, D), (2, D), feedforward[0].shape, (devices, 1, 128)]
    return pl.pallas_call(
        functools.partial(squares_body, len(attention), rows),
        in_specs=[pl.BlockSpec(memory_space=pltpu.VMEM) for _ in parts],
        out_specs=[pl.BlockSpec(memory_space=pltpu.VMEM) for _ in shapes],
        out_shape=[jax.ShapeDtypeStruct(shape, F32) for shape in shapes],
        compiler_params=pltpu.CompilerParams(vmem_limit_bytes=6 * 2**20),
        cost_estimate=SHORT,
        name="last_sums",
    )(*parts)


def update_body(squares_ref, *refs):
    grads, states, results, norm_ref = refs[:3], refs[3:12], refs[12:21], refs[21]
    gain_grad = grads[2][...]
    squares = jnp.sum(squares_ref[...], axis=0)[:, 0:1] + jnp.sum(gain_grad * gain_grad)
    norm = jnp.sqrt(squares)
    norm_ref[...] = norm
    factor = jnp.minimum(1.0, clip_limit / (norm + 1e-06))
    rates = (rate_matrix, weight_decay), (rate_matrix, weight_decay), (rate_gain, 0.0)
    for kind, (step_rate, decay_rate) in enumerate(rates):
        grad = grads[kind][...]
        scale = factor.reshape((1,) * grad.ndim)
        new = adamw_update(
            *[ref[...] for ref in states[3 * kind : 3 * kind + 3]],
            grad,
            scale,
            step_rate,
            decay_rate,
        )
        for ref, value in zip(results[3 * kind : 3 * kind + 3], new):
            ref[...] = value


def update(squares, grads, states):
    shapes = [state.shape for state in states] + [(1, 1)]
    return pl.pallas_call(
        update_body,
        in_specs=[pl.BlockSpec(memory_space=pltpu.VMEM) for _ in range(13)],
        out_specs=[pl.BlockSpec(memory_space=pltpu.VMEM) for _ in shapes],
        out_shape=[jax.ShapeDtypeStruct(shape, F32) for shape in shapes],
        compiler_params=pltpu.CompilerParams(vmem_limit_bytes=12 * 2**20),
        cost_estimate=SHORT,
        name="update",
    )(squares, *grads, *states)


def per_device(
    tokens,
    cotangent,
    documents,
    attention_master,
    attention_first,
    attention_second,
    feedforward_master,
    feedforward_first,
    feedforward_second,
    gain_master,
    gain_first,
    gain_second,
):
    seq_count, half_len, _ = tokens.shape
    own_count = seq_count // 2
    place = lax.axis_index("narrow")
    first = place == 0
    outer, inner = factors(lax.axis_size("wide"))
    wide_place = lax.axis_index("wide")
    outer_place, inner_place = wide_place // inner, wide_place % inner
    tables = rotary_tables(2 * half_len)
    gain_columns = gain_master.T
    x_own = jnp.swapaxes(tokens, 1, 2)
    cotangent_own = jnp.swapaxes(cotangent, 1, 2)

    def swap(tensor):
        return across(
            lax.dynamic_slice_in_dim(tensor, (1 - place) * own_count, own_count, 0)
        )

    x_other = swap(x_own)
    own_docs = lax.dynamic_slice_in_dim(documents, place * own_count, own_count, 0)
    start = jnp.zeros_like(own_docs)
    for number in (1, 2):
        before = jnp.sum((own_docs < number).astype(jnp.int32), axis=1, keepdims=True)
        start = jnp.where(own_docs == number, before, start)
    start = start[:, None, :]

    rows = attention_master.shape[0]
    aligned = rows % 16 == 0
    if aligned:
        chunk = jnp.arange(2 * inner * outer, dtype=jnp.int32)
        order = (
            ((chunk % 2) ^ place) * inner + ((chunk // 2 % inner) ^ inner_place)
        ) * outer + ((chunk // (2 * inner)) ^ outer_place)
        pair = chunk[: inner * outer]
        piece_of = (pair % inner) ^ inner_place
        row_of = ((pair // inner) ^ outer_place) * rows
        grad_pieces = inner
    else:
        order = jnp.arange(32, dtype=jnp.int32)
        piece_of = jnp.zeros((16,), jnp.int32)
        row_of = jnp.arange(16, dtype=jnp.int32) * 48
        grad_pieces = 1
    info = jnp.concatenate(
        [jnp.full((1,), place), order, piece_of, row_of]
    ).astype(jnp.int32)

    piece = attention_master.astype(BF16)
    parts = [piece] + [partner(piece, k * inner) for k in range(1, outer)]
    stack = jnp.stack(parts if aligned else in_order(parts, outer_place))
    feed_piece = feedforward_master.astype(BF16)
    feed_outer = jnp.stack(
        [feed_piece] + [partner(feed_piece, k * inner) for k in range(1, outer)]
    )
    parts = [stack] + [partner(stack, k) for k in range(1, inner)]
    feed_outer, parts[1:], info, start, gain_columns = lax.optimization_barrier(
        (feed_outer, parts[1:], info, start, gain_columns)
    )
    feed_parts = [feed_outer] + [partner(feed_outer, k) for k in range(1, inner)]
    if aligned:
        stack = jnp.stack(parts)
        pieces_own = stack.reshape(-1, rows, D)
        pieces_other = across(stack).reshape(-1, rows, D)
    else:
        stack = jnp.stack(in_order(parts, inner_place), axis=1)
        pieces = jnp.stack(in_order([stack, across(stack)], place), axis=2).reshape(-1, 48, D)
        pieces_own, pieces_other = pieces[:16], pieces[16:]
    cotangent_other = swap(cotangent_own)

    residual, query, key, value, mixed, total, normed, weight_qkv, weight_out = attention_forward(
        info, x_own, x_other, start, pieces_own, pieces_other, gain_columns, tables
    )
    feed_parts, residual = lax.optimization_barrier((feed_parts, residual))
    if aligned:
        feed_weights = feed_parts + [across(part) for part in feed_parts]
    else:
        stack = jnp.stack(feed_parts)
        feed_weights = [
            jnp.swapaxes(part.reshape(-1, 3, rows, D), 0, 1).reshape(1, 3, -1, D)
            for part in (stack, across(stack))
        ]
    outputs, out_other, back, gain_second_part, own_grad, other_grad = feed_forward(
        info, residual, cotangent_own, cotangent_other, feed_weights, gain_columns, inner
    )

    def place_other(whole_array, received):
        return lax.dynamic_update_slice_in_dim(
            whole_array, received.astype(whole_array.dtype), (1 - place) * own_count, 0
        )

    out_received = across(out_other)

    received = across(other_grad)
    grad_mixed, inner_sums, out_grad = branch_backward(back, mixed, weight_out)
    received, own_grad, grad_mixed = lax.optimization_barrier((received, own_grad, grad_mixed))
    feed_sums = [add_all([own_grad[k], received[k]]).astype(BF16) for k in range(inner)]
    feed_sums, grad_mixed = lax.optimization_barrier((feed_sums, grad_mixed))
    feed_got = [feed_sums[0]] + [partner(feed_sums[k], k) for k in range(1, inner)]
    projected, kept, sent = attention_backward(
        info,
        normed,
        start,
        gain_master,
        weight_qkv,
        out_grad,
        gain_second_part,
        tables,
        [query, key, value, total, grad_mixed, inner_sums],
        grad_pieces,
    )
    feed_got, kept, sent = lax.optimization_barrier((feed_got, kept, sent))
    summed = add_all(feed_got).astype(BF16).reshape(3, outer, -1, D)
    feed_last = [summed[:, k] for k in range(outer)]
    feed_last, sent = lax.optimization_barrier((feed_last, sent))
    feed_last = [feed_last[0]] + [partner(feed_last[k], k * inner) for k in range(1, outer)]

    received = across(sent)
    if aligned:
        parts = [add_all([kept[k], received[k]]).astype(BF16) for k in range(inner)]
    else:
        gain_grad = lax.psum(kept[0, -16:-14].astype(F32), ("wide", "narrow"))
        total = add_all([kept, received]).astype(BF16)[0, :-16].reshape(outer, inner, rows, D)
        parts = in_order([total[:, k] for k in range(inner)], inner_place)
    parts, projected = lax.optimization_barrier((parts, projected))
    got = [parts[0]] + [partner(parts[k], k) for k in range(1, inner)]
    grad_own, grad_other = input_grads(
        info, x_own, x_other, gain_columns, projected, weight_qkv, back
    )
    got, feed_last, grad_other = lax.optimization_barrier((got, feed_last, grad_other))
    total = add_all(got).astype(BF16)
    if aligned:
        tail = total[outer * rows :]
        parts = [
            jnp.concatenate([total[k * rows : (k + 1) * rows], tail], axis=0)
            for k in range(outer)
        ]
    else:
        parts = in_order([total[k] for k in range(outer)], outer_place)
    last = [parts[0]] + [partner(parts[k], k * inner) for k in range(1, outer)]
    devices = lax.axis_size("wide") * lax.axis_size("narrow")
    attention_grad, gain_total, feedforward_grad, squares = last_sums(
        last, feed_last, rows, devices
    )
    if aligned:
        gain_grad = gain_total
    squares = lax.all_to_all(squares, ("wide", "narrow"), 0, 0, tiled=True)
    grad_received = across(grad_other)
    attention_grad, gain_grad, grad_received, out_received = lax.optimization_barrier(
        (attention_grad, gain_grad, grad_received, out_received)
    )
    grad_tokens = place_other(grad_own, grad_received)
    outputs = place_other(outputs, out_received)
    states = (
        attention_master,
        attention_first,
        attention_second,
        feedforward_master,
        feedforward_first,
        feedforward_second,
        gain_master,
        gain_first,
        gain_second,
    )
    *updated, grad_norm = update(squares, (attention_grad, feedforward_grad, gain_grad), states)
    outputs = jnp.swapaxes(outputs, 1, 2)
    grad_tokens = jnp.swapaxes(grad_tokens, 1, 2)
    return (outputs, grad_tokens, grad_norm.reshape(()), *updated)


def solution(mesh):
    sequences = P("wide", "narrow", None)
    attention = P(("wide", "narrow"), None)
    feedforward = P(None, ("narrow", "wide"), None)
    state = (attention,) * 3 + (feedforward,) * 3 + (P(),) * 3
    return jax.shard_map(
        per_device,
        mesh=mesh,
        in_specs=(sequences, sequences, P("wide", None)) + state,
        out_specs=(sequences, sequences, P()) + state,
        check_vma=False,
    )
```
